512 devices in a mesh: tok: 64 (over y, z), kv: 8 (over x, core).
Axes of the slice: x: 4, y: 8, z: 8, core: 2. Of those that a mesh axis runs over, the one named last changes fastest.
Arguments:
- hidden_in: bfloat16 [256, 2048], P('tok'), may hold values from -6 to 6
- w_query: bfloat16 [2048, 2048], P(None, 'kv'), may hold values from -0.125 to 0.125
- w_keyval: bfloat16 [2048, 8, 128], P(None, 'kv')
- w_out: bfloat16 [2048, 2048], P('kv'), may hold values from -0.125 to 0.125
- own_cache: bfloat16 [8, 256, 1024, 128], P('kv', 'tok')
- prefix_cache: bfloat16 [8, 21, 15872, 128], P('kv', None, 'tok')
- own_len: int32 [256], P('tok'), may hold values from 1 to 1024, as said below
- req_group: int32 [256], replicated, may hold values from 0 to 20, never falling along the last dimension, each value on 1 to 16 neighbouring positions
- pre_len: int32 [21], replicated, may hold values from 1 to 15872, as said below
Outputs:
- attn_out: bfloat16 [256, 2048], P('tok', 'kv')
The draws below stay inside these ranges and needn't reach their ends.
Inputs may be any that keep to these rules, and one draw needn't show every extreme that they name: `own_len`: some request has exactly 1024 live positions. `req_group`: ids never fall along the requests; every id is used by 1 to 16 consecutive requests, some by exactly 16. `pre_len`: some shared prompt has exactly 15872 live positions.
All inputs are finite; a program needn't handle non-finite values.
Results may differ from the reference program's by a relative error of at most 0.025.
Values may be sent and summed in bfloat16 or wider, within the bound.
A program may use at most 64 MiB of HBM per device.

```python
import math
import jax
import jax.numpy as jnp
import numpy as np
from jax import lax

D = 2048
QH = 32
KVH = 8
HD = 64
OWN_LEN = 1024
PRE_DEV = 248
SHARE = 16
REQS = 256
GROUPS = 21
PRE_LEN = 15872
N_TOK = 64


def draw_cache(key, shape):
    base = jax.random.truncated_normal(key, -6.0, 6.0, shape, jnp.float32)
    lane = jnp.arange(shape[-1]) < HD
    return jnp.where(lane, 28.0 * base, 4.0 * base)


def draw_lengths(key, count, most):
    values = jax.random.randint(key, (count,), 1, most + 1)
    spot = jax.random.randint(jax.random.fold_in(key, 7), (), 0, count)
    return jnp.where(jnp.arange(count) == spot, most, values).astype(jnp.int32)


def draw_w_keyval(key, part):
    base = jax.random.truncated_normal(key, -6.0, 6.0, (D, KVH, 2 * HD), jnp.float32)
    lane = jnp.arange(2 * HD) < HD
    factor = jnp.where(lane, 36.0, 4.0) / jnp.sqrt(jnp.float32(D))
    return (base * factor).astype(jnp.bfloat16)


def draw_own_cache(key, part):
    return draw_cache(key, (KVH, REQS, OWN_LEN, 2 * HD)).astype(jnp.bfloat16)


def draw_prefix_cache(key, part):
    return draw_cache(key, (KVH, GROUPS, PRE_LEN, 2 * HD)).astype(jnp.bfloat16)


def draw_own_len(key, part):
    return draw_lengths(key, REQS, OWN_LEN)


def draw_pre_len(key, part):
    return draw_lengths(key, GROUPS, PRE_LEN)


def shard_levels(own_key, extent, split, smallest, high):
    loudness = 1.0
    for axis_at, parts in split:
        draws = jax.random.uniform(jax.random.fold_in(jax.random.fold_in(own_key, 6), axis_at), (parts,), jnp.float32, smallest / len(split), high / len(split))
        loudness = loudness * jnp.repeat(jnp.exp(draws), extent[axis_at] // parts).reshape((-1,) + (1,) * (len(extent) - 1 - axis_at))
    return loudness


def profile(number_of, total, limit, slope):
    weights = [(1 << 20) // math.isqrt(standing ** slope) + 1 for standing in range(2, number_of + 1)]
    surplus, counts = total - limit - (number_of - 1), [1] * (number_of - 1)
    while surplus > 0:
        candidates = [i for i in range(number_of - 1) if counts[i] < limit]
        whole, left = sum([weights[i] for i in candidates]), surplus
        for i in candidates:
            addition = min(limit - counts[i], max(1, left * weights[i] // whole), surplus)
            counts[i] = counts[i] + addition
            surplus = surplus - addition
    return np.array([limit] + counts)


def ragged(key, number_of, total, reach, lean):
    if number_of == 2:
        one = jax.random.randint(key, (), max(1, total - reach), min(reach, total - 1) + 1)
        return jnp.stack([one, total - one])
    tallies = jnp.asarray(profile(number_of, total, reach, lean), jnp.int32)
    couples = (number_of - 1) // 2
    source_of, taker = tallies[1:1 + 2 * couples:2], tallies[2:2 + 2 * couples:2]
    margin = jnp.minimum(source_of - 1, reach - taker)
    passed = jax.random.randint(jax.random.fold_in(key, 1), (couples,), 0, 1 << 20) % (margin + 1)
    tallies = tallies.at[1:1 + 2 * couples:2].set(source_of - passed).at[2:2 + 2 * couples:2].set(taker + passed)
    return tallies[jax.random.permutation(jax.random.fold_in(key, 2), number_of)]


def gaussian(rng, shape, scale, limit, pieces=(), kind=jnp.bfloat16):
    drawn = jax.random.normal(rng, shape, jnp.float32) * scale
    if len(pieces) > 0:
        drawn = shard_levels(rng, shape, pieces, -0.22, 0.18) * drawn
    return jnp.clip(drawn, min=-limit, max=limit).astype(kind)


def setup_inputs(seed: int = 0) -> dict:
    seeds = jax.random.split(jax.random.key(seed), 10)
    return {
        "hidden_in": gaussian(seeds[0], (REQS, D), 1.0, 6.0, ((0, 64),)),
        "w_query": gaussian(seeds[1], (D, QH * HD), D ** -0.5, 0.125, ((1, 8),)),
        "w_keyval": draw_w_keyval(jax.random.fold_in(seeds[9], 71), 0),
        "w_out": gaussian(seeds[3], (QH * HD, D), (QH * HD) ** -0.5, 0.125, ((0, 8),)),
        "own_cache": draw_own_cache(jax.random.fold_in(seeds[9], 71), 0),
        "prefix_cache": draw_prefix_cache(jax.random.fold_in(seeds[9], 71), 0),
        "own_len": draw_own_len(jax.random.fold_in(seeds[9], 71), 0),
        "req_group": jnp.searchsorted(jnp.cumsum(ragged(seeds[7], GROUPS, REQS, SHARE, 0)), jnp.arange(REQS), side="right").astype(jnp.int32),
        "pre_len": draw_pre_len(jax.random.fold_in(seeds[9], 71), 0),
    }


SCALE = 0.015625
NEG = -1e+30

def block_stats(query, keyval, live):
    width = query.shape[-1]
    keys = keyval[..., :width].astype(jnp.float32)
    values = keyval[..., width:].astype(jnp.float32)
    scores = jnp.einsum('rge,rpe->rgp', query.astype(jnp.float32), keys) * SCALE
    mask = live[:, None, :]
    scores = jnp.where(mask, scores, NEG)
    top = lax.optimization_barrier(jnp.max(scores, axis=-1))
    weights = jnp.where(mask, jnp.exp(scores - top[..., None]), 0.0)
    total = lax.optimization_barrier(jnp.sum(weights, axis=-1))
    rounded = weights.astype(jnp.bfloat16).astype(jnp.float32)
    numer = jnp.einsum('rgp,rpe->rge', rounded, values)
    return (top, total, numer)

def reference(hidden_in, w_query, w_keyval, w_out, own_cache, prefix_cache, own_len, req_group, pre_len):
    per_kv = QH // KVH
    inputs = hidden_in.astype(jnp.float32)
    normed = (inputs * lax.rsqrt(lax.optimization_barrier(jnp.mean(inputs * inputs, axis=1, keepdims=True)) + 1e-05)).astype(jnp.bfloat16)
    query = jnp.dot(normed, w_query, preferred_element_type=jnp.float32).astype(jnp.bfloat16)
    query = query.reshape(REQS, KVH, per_kv, HD)
    newkv = jnp.einsum('rd,dhe->rhe', normed.astype(jnp.float32), w_keyval.astype(jnp.float32)).astype(jnp.bfloat16)
    match = req_group[:, None] == jnp.arange(GROUPS, dtype=jnp.int32)[None, :]
    group_len = lax.optimization_barrier(jnp.sum(jnp.where(match, pre_len[None, :], 0), axis=1)).astype(jnp.int32)
    own_live = jnp.arange(OWN_LEN, dtype=jnp.int32)[None, :] < own_len[:, None]
    heads_out = []
    for head in range(KVH):
        head_query = query[:, head]
        pre_head = prefix_cache[head]

        def per_block(index):
            pre_part = lax.dynamic_slice_in_dim(pre_head, (index * PRE_DEV).astype(jnp.int32), PRE_DEV, 1)
            pre_rows = jnp.take(pre_part, req_group, axis=0)
            pre_pos = index * PRE_DEV + jnp.arange(PRE_DEV, dtype=jnp.int32)
            return block_stats(head_query, pre_rows, pre_pos[None, :] < group_len[:, None])
        tops, totals, numers = lax.map(per_block, jnp.arange(N_TOK, dtype=jnp.int32))
        own_top, own_total, own_numer = block_stats(head_query, own_cache[head], own_live)
        tops = jnp.concatenate([tops, own_top[None]], axis=0)
        totals = jnp.concatenate([totals, own_total[None]], axis=0)
        numers = jnp.concatenate([numers, own_numer[None]], axis=0)
        new_key = newkv[:, head, :HD].astype(jnp.float32)
        new_value = newkv[:, head, HD:].astype(jnp.float32)
        s_new = lax.optimization_barrier(jnp.sum(head_query.astype(jnp.float32) * new_key[:, None, :], axis=-1)) * SCALE
        largest = jnp.maximum(lax.optimization_barrier(jnp.max(tops, axis=0)), s_new)
        coefs = jnp.exp(tops - largest)
        own_coef = jnp.exp(s_new - largest)
        denom = lax.optimization_barrier(jnp.sum(coefs * totals, axis=0)) + own_coef
        numer = lax.optimization_barrier(jnp.sum(coefs[..., None] * numers, axis=0)) + own_coef[..., None] * new_value[:, None, :]
        heads_out.append(numer / denom[..., None])
    attn = jnp.stack(heads_out, axis=1).reshape(REQS, QH * HD).astype(jnp.bfloat16)
    return jnp.dot(attn, w_out, preferred_element_type=jnp.float32).astype(jnp.bfloat16)
```

```python
import jax
import jax.numpy as jnp
from jax import lax
from jax.sharding import PartitionSpec as P

SHARE = 16


SCALE = 0.015625
NEG = -1e30


def block_stats(query, keyval, live):
    width = query.shape[-1]
    keys = keyval[..., :width]
    values = keyval[..., width:]
    scores = jnp.einsum("rhge,hrpe->rhgp", query, keys, preferred_element_type=jnp.float32) * SCALE
    mask = live[:, None, None, :]
    scores = jnp.where(mask, scores, NEG)
    top = jnp.max(scores, axis=-1)
    weights = jnp.where(mask, jnp.exp(scores - top[..., None]), 0.0)
    total = jnp.sum(weights, axis=-1)
    numer = jnp.einsum(
        "rhgp,hrpe->rhge", weights.astype(jnp.bfloat16), values, preferred_element_type=jnp.float32
    )
    return (top, total, numer)


def prompt_stats(all_query, prefix_cache, req_group, pre_len, block):
    all_rows, heads, per_kv, width = all_query.shape
    groups = prefix_cache.shape[1]
    pre_dev = prefix_cache.shape[2]
    group_ids = jnp.arange(groups, dtype=jnp.int32)
    starts = jnp.sum((req_group[None, :] < group_ids[:, None]).astype(jnp.int32), axis=1)
    slot_ids = jnp.arange(SHARE, dtype=jnp.int32)
    source = jnp.minimum(starts[:, None] + slot_ids[None, :], all_rows - 1).reshape(-1)
    slotted = jnp.take(all_query, source, axis=0).reshape(groups, SHARE, heads, per_kv, width)
    keys = prefix_cache[..., :width]
    values = prefix_cache[..., width:]
    scores = (
        jnp.einsum("gshqe,hgpe->hgsqp", slotted, keys, preferred_element_type=jnp.float32) * SCALE
    )
    pre_pos = block * pre_dev + jnp.arange(pre_dev, dtype=jnp.int32)
    live = pre_pos[None, :] < pre_len[:, None]
    mask = live[None, :, None, None, :]
    scores = jnp.where(mask, scores, NEG)
    top = jnp.max(scores, axis=-1)
    weights = jnp.where(mask, jnp.exp(scores - top[..., None]), 0.0)
    total = jnp.sum(weights, axis=-1)
    numer = jnp.einsum(
        "hgsqp,hgpe->hgsqe",
        weights.astype(jnp.bfloat16),
        values,
        preferred_element_type=jnp.float32,
    )
    match = req_group[:, None] == group_ids[None, :]
    start_req = jnp.sum(jnp.where(match, starts[None, :], 0), axis=1)
    place = req_group * SHARE + jnp.arange(all_rows, dtype=jnp.int32) - start_req
    columns = heads * per_kv
    top = jnp.take(top.reshape(heads, groups * SHARE, per_kv), place, axis=1)
    total = jnp.take(total.reshape(heads, groups * SHARE, per_kv), place, axis=1)
    numer = jnp.take(numer.reshape(heads, groups * SHARE, per_kv, width), place, axis=1)
    top = jnp.transpose(top, (1, 0, 2)).reshape(all_rows, columns)
    total = jnp.transpose(total, (1, 0, 2)).reshape(all_rows, columns)
    numer = jnp.transpose(numer, (1, 0, 2, 3)).reshape(all_rows, columns * width)
    return (top, total, numer)


def body(hidden_in, w_query, w_keyval, w_out, own_cache, prefix_cache, own_len, req_group, pre_len):
    rows = hidden_in.shape[0]
    heads = w_keyval.shape[1]
    width = w_keyval.shape[2] // 2
    per_kv = w_query.shape[1] // (heads * width)
    columns = heads * per_kv
    inputs = hidden_in.astype(jnp.float32)
    normed = (inputs * lax.rsqrt(jnp.mean(inputs * inputs, axis=1, keepdims=True) + 1e-05)).astype(
        jnp.bfloat16
    )
    query = jnp.dot(normed, w_query, preferred_element_type=jnp.float32).astype(jnp.bfloat16)
    newkv = jnp.einsum("rd,dhe->rhe", normed, w_keyval, preferred_element_type=jnp.float32).astype(
        jnp.bfloat16
    )
    gathered = lax.all_gather(query, "tok", axis=0, tiled=True)
    all_rows = gathered.shape[0]
    all_query = gathered.reshape(all_rows, heads, per_kv, width)
    block = lax.axis_index("tok")
    n_tok = all_rows // rows
    pre_top, pre_total, pre_numer = prompt_stats(all_query, prefix_cache, req_group, pre_len, block)
    packed = jnp.concatenate([pre_numer, pre_top, pre_total], axis=1)
    recv = lax.all_to_all(packed, "tok", 0, 0, tiled=True).reshape(n_tok, rows, -1)
    cw = columns * width
    r_numer = recv[..., :cw].reshape(n_tok, rows, columns, width)
    r_top = recv[..., cw : cw + columns]
    r_total = recv[..., cw + columns :]

    local_query = query.reshape(rows, heads, per_kv, width)
    own_cap = own_cache.shape[2]
    own_live = jnp.arange(own_cap, dtype=jnp.int32)[None, :] < own_len[:, None]
    own_top, own_total, own_numer = block_stats(local_query, own_cache, own_live)
    own_top = own_top.reshape(rows, columns)
    own_total = own_total.reshape(rows, columns)
    own_numer = own_numer.reshape(rows, columns, width)
    s_new = (
        jnp.einsum(
            "rhge,rhe->rhg", local_query, newkv[..., :width], preferred_element_type=jnp.float32
        )
        * SCALE
    )
    s_new = s_new.reshape(rows, columns)
    new_value = jnp.broadcast_to(
        newkv[:, :, None, width:].astype(jnp.float32), (rows, heads, per_kv, width)
    ).reshape(rows, columns, width)
    largest = jnp.maximum(jnp.maximum(jnp.max(r_top, axis=0), own_top), s_new)
    coef_pre = jnp.exp(r_top - largest[None])
    coef_own = jnp.exp(own_top - largest)
    coef_new = jnp.exp(s_new - largest)
    denom = jnp.sum(coef_pre * r_total, axis=0) + coef_own * own_total + coef_new
    numer = (
        jnp.sum(coef_pre[..., None] * r_numer, axis=0)
        + coef_own[..., None] * own_numer
        + coef_new[..., None] * new_value
    )
    attn = (numer / denom[..., None]).reshape(rows, columns * width).astype(jnp.bfloat16)
    partial_out = jnp.dot(attn, w_out, preferred_element_type=jnp.float32)
    return lax.psum_scatter(partial_out, "kv", scatter_dimension=1, tiled=True).astype(jnp.bfloat16)


def solution(mesh):
    in_specs = (
        P("tok", None),
        P(None, "kv"),
        P(None, "kv", None),
        P("kv", None),
        P("kv", "tok", None, None),
        P("kv", None, "tok", None),
        P("tok"),
        P(),
        P(),
    )
    out_specs = P("tok", "kv")
    return jax.shard_map(body, mesh=mesh, in_specs=in_specs, out_specs=out_specs, check_vma=False)
```

```python
import jax
import jax.numpy as jnp
from jax import lax
from jax.sharding import PartitionSpec as P
from jax.experimental import pallas as pl
from jax.experimental.pallas import tpu as pltpu

SHARE = 16


SCALE = 0.015625
NEG = -1e30


def exchange(slabs, axis, other, n, broadcast, cid):
    slab_shape = slabs.shape[1:] if not broadcast else slabs.shape
    mesh_id = pl.DeviceIdType.MESH

    def kernel(x_ref, out_ref, send_sems, recv_sems, local_sem):
        me = lax.axis_index(axis)
        keep = lax.axis_index(other)

        def dev(peer):
            return (peer, keep) if axis == "tok" else (keep, peer)

        def src(peer):
            return x_ref if broadcast else x_ref.at[peer]

        barrier = pltpu.get_barrier_semaphore()

        def greet(i, c):
            peer = lax.rem(me + i, n)
            pl.semaphore_signal(barrier, inc=1, device_id=dev(peer), device_id_type=mesh_id)
            return c

        lax.fori_loop(1, n, greet, 0)
        pl.semaphore_wait(barrier, n - 1)
        local = pltpu.make_async_copy(src(me), out_ref.at[me], local_sem)
        local.start()

        def send(i, c):
            peer = lax.rem(me + i, n)
            pltpu.make_async_remote_copy(
                src(peer), out_ref.at[me], send_sems.at[i], recv_sems.at[i],
                device_id=dev(peer), device_id_type=mesh_id,
            ).start()
            return c

        lax.fori_loop(1, n, send, 0)

        def finish(i, c):
            peer = lax.rem(me + i, n)
            origin = lax.rem(me + n - i, n)
            pltpu.make_async_remote_copy(
                src(peer), out_ref.at[me], send_sems.at[i], recv_sems.at[i],
                device_id=dev(peer), device_id_type=mesh_id,
            ).wait_send()
            pltpu.make_async_remote_copy(
                src(peer), out_ref.at[origin], send_sems.at[i], recv_sems.at[i],
                device_id=dev(origin), device_id_type=mesh_id,
            ).wait_recv()
            return c

        lax.fori_loop(1, n, finish, 0)
        local.wait()

    return pl.pallas_call(
        kernel,
        out_shape=jax.ShapeDtypeStruct((n,) + tuple(slab_shape), slabs.dtype),
        in_specs=[pl.BlockSpec(memory_space=pltpu.VMEM)],
        out_specs=pl.BlockSpec(memory_space=pltpu.VMEM),
        scratch_shapes=[
            pltpu.SemaphoreType.DMA((n,)),
            pltpu.SemaphoreType.DMA((n,)),
            pltpu.SemaphoreType.DMA(()),
        ],
        compiler_params=pltpu.CompilerParams(collective_id=cid, has_side_effects=True),
    )(slabs)


def block_stats(query, keyval, live):
    width = query.shape[-1]
    keys = keyval[..., :width]
    values = keyval[..., width:]
    scores = jnp.einsum("rhge,hrpe->rhgp", query, keys, preferred_element_type=jnp.float32) * SCALE
    mask = live[:, None, None, :]
    scores = jnp.where(mask, scores, NEG)
    top = jnp.max(scores, axis=-1)
    weights = jnp.where(mask, jnp.exp(scores - top[..., None]), 0.0)
    total = jnp.sum(weights, axis=-1)
    numer = jnp.einsum(
        "rhgp,hrpe->rhge", weights.astype(jnp.bfloat16), values, preferred_element_type=jnp.float32
    )
    return (top, total, numer)


def prompt_stats(all_query, prefix_cache, req_group, pre_len, block):
    all_rows, heads, per_kv, width = all_query.shape
    groups = prefix_cache.shape[1]
    pre_dev = prefix_cache.shape[2]
    group_ids = jnp.arange(groups, dtype=jnp.int32)
    starts = jnp.sum((req_group[None, :] < group_ids[:, None]).astype(jnp.int32), axis=1)
    slot_ids = jnp.arange(SHARE, dtype=jnp.int32)
    source = jnp.minimum(starts[:, None] + slot_ids[None, :], all_rows - 1).reshape(-1)
    slotted = jnp.take(all_query, source, axis=0).reshape(groups, SHARE, heads, per_kv, width)
    keys = prefix_cache[..., :width]
    values = prefix_cache[..., width:]
    scores = (
        jnp.einsum("gshqe,hgpe->hgsqp", slotted, keys, preferred_element_type=jnp.float32) * SCALE
    )
    pre_pos = block * pre_dev + jnp.arange(pre_dev, dtype=jnp.int32)
    live = pre_pos[None, :] < pre_len[:, None]
    mask = live[None, :, None, None, :]
    scores = jnp.where(mask, scores, NEG)
    top = jnp.max(scores, axis=-1)
    weights = jnp.where(mask, jnp.exp(scores - top[..., None]), 0.0)
    total = jnp.sum(weights, axis=-1)
    numer = jnp.einsum(
        "hgsqp,hgpe->hgsqe",
        weights.astype(jnp.bfloat16),
        values,
        preferred_element_type=jnp.float32,
    )
    match = req_group[:, None] == group_ids[None, :]
    start_req = jnp.sum(jnp.where(match, starts[None, :], 0), axis=1)
    place = req_group * SHARE + jnp.arange(all_rows, dtype=jnp.int32) - start_req
    columns = heads * per_kv
    top = jnp.take(top.reshape(heads, groups * SHARE, per_kv), place, axis=1)
    total = jnp.take(total.reshape(heads, groups * SHARE, per_kv), place, axis=1)
    numer = jnp.take(numer.reshape(heads, groups * SHARE, per_kv, width), place, axis=1)
    top = jnp.transpose(top, (1, 0, 2)).reshape(all_rows, columns)
    total = jnp.transpose(total, (1, 0, 2)).reshape(all_rows, columns)
    numer = jnp.transpose(numer, (1, 0, 2, 3)).reshape(all_rows, columns * width)
    return (top, total, numer)


def body(hidden_in, w_query, w_keyval, w_out, own_cache, prefix_cache, own_len, req_group, pre_len):
    rows = hidden_in.shape[0]
    heads = w_keyval.shape[1]
    width = w_keyval.shape[2] // 2
    per_kv = w_query.shape[1] // (heads * width)
    columns = heads * per_kv
    inputs = hidden_in.astype(jnp.float32)
    normed = (inputs * lax.rsqrt(jnp.mean(inputs * inputs, axis=1, keepdims=True) + 1e-05)).astype(
        jnp.bfloat16
    )
    query = jnp.dot(normed, w_query, preferred_element_type=jnp.float32).astype(jnp.bfloat16)
    newkv = jnp.einsum("rd,dhe->rhe", normed, w_keyval, preferred_element_type=jnp.float32).astype(
        jnp.bfloat16
    )
    n_tok = lax.axis_size("tok")
    n_kv = lax.axis_size("kv")
    q_slab = query.reshape(-1, 128)
    gathered = exchange(q_slab, "tok", "kv", n_tok, True, 0).reshape(n_tok * rows, -1)
    all_rows = gathered.shape[0]
    all_query = gathered.reshape(all_rows, heads, per_kv, width)
    block = lax.axis_index("tok")
    pre_top, pre_total, pre_numer = prompt_stats(all_query, prefix_cache, req_group, pre_len, block)
    cw = columns * width
    per_dest = rows * (cw + 2 * columns)
    lanes = -(-per_dest // 128) * 128
    packed = jnp.concatenate(
        [
            pre_numer.reshape(n_tok, rows * cw),
            pre_top.reshape(n_tok, rows * columns),
            pre_total.reshape(n_tok, rows * columns),
            jnp.zeros((n_tok, lanes - per_dest), jnp.float32),
        ],
        axis=1,
    ).reshape(n_tok, lanes // 128, 128)
    recv = exchange(packed, "tok", "kv", n_tok, False, 1).reshape(n_tok, lanes)
    r_numer = recv[:, : rows * cw].reshape(n_tok, rows, columns, width)
    r_top = recv[:, rows * cw : rows * (cw + columns)].reshape(n_tok, rows, columns)
    r_total = recv[:, rows * (cw + columns) : per_dest].reshape(n_tok, rows, columns)

    local_query = query.reshape(rows, heads, per_kv, width)
    own_cap = own_cache.shape[2]
    own_live = jnp.arange(own_cap, dtype=jnp.int32)[None, :] < own_len[:, None]
    own_top, own_total, own_numer = block_stats(local_query, own_cache, own_live)
    own_top = own_top.reshape(rows, columns)
    own_total = own_total.reshape(rows, columns)
    own_numer = own_numer.reshape(rows, columns, width)
    s_new = (
        jnp.einsum(
            "rhge,rhe->rhg", local_query, newkv[..., :width], preferred_element_type=jnp.float32
        )
        * SCALE
    )
    s_new = s_new.reshape(rows, columns)
    new_value = jnp.broadcast_to(
        newkv[:, :, None, width:].astype(jnp.float32), (rows, heads, per_kv, width)
    ).reshape(rows, columns, width)
    largest = jnp.maximum(jnp.maximum(jnp.max(r_top, axis=0), own_top), s_new)
    coef_pre = jnp.exp(r_top - largest[None])
    coef_own = jnp.exp(own_top - largest)
    coef_new = jnp.exp(s_new - largest)
    denom = jnp.sum(coef_pre * r_total, axis=0) + coef_own * own_total + coef_new
    numer = (
        jnp.sum(coef_pre[..., None] * r_numer, axis=0)
        + coef_own[..., None] * own_numer
        + coef_new[..., None] * new_value
    )
    attn = (numer / denom[..., None]).reshape(rows, columns * width).astype(jnp.bfloat16)
    partial_out = jnp.dot(attn, w_out, preferred_element_type=jnp.float32)
    out_cols = partial_out.shape[1] // n_kv
    pieces = jnp.transpose(partial_out.reshape(rows, n_kv, out_cols), (1, 0, 2))
    pieces = pieces.reshape(n_kv, rows * out_cols // 128, 128)
    summed = jnp.sum(exchange(pieces, "kv", "tok", n_kv, False, 2), axis=0)
    return summed.reshape(rows, out_cols).astype(jnp.bfloat16)


def solution(mesh):
    in_specs = (
        P("tok", None),
        P(None, "kv"),
        P(None, "kv", None),
        P("kv", None),
        P("kv", "tok", None, None),
        P("kv", None, "tok", None),
        P("tok"),
        P(),
        P(),
    )
    out_specs = P("tok", "kv")
    return jax.shard_map(body, mesh=mesh, in_specs=in_specs, out_specs=out_specs, check_vma=False)
```

```python
import jax
import jax.numpy as jnp
from jax import lax
from jax.sharding import PartitionSpec as P
from jax.experimental import pallas as pl
from jax.experimental.pallas import tpu as pltpu

SHARE = 16


SCALE = 0.015625
NEG = -1e30


def exchange(slabs, axis, other, n, broadcast, cid):
    slab_shape = slabs.shape[1:] if not broadcast else slabs.shape
    mesh_id = pl.DeviceIdType.MESH

    def kernel(x_ref, out_ref, send_sems, recv_sems, local_sem):
        me = lax.axis_index(axis)
        keep = lax.axis_index(other)

        def dev(peer):
            return (peer, keep) if axis == "tok" else (keep, peer)

        def src(peer):
            return x_ref if broadcast else x_ref.at[peer]

        local = pltpu.make_async_copy(src(me), out_ref.at[me], local_sem)
        local.start()

        def send(i, c):
            peer = lax.rem(me + i, n)
            pltpu.make_async_remote_copy(
                src(peer), out_ref.at[me], send_sems.at[i], recv_sems.at[i],
                device_id=dev(peer), device_id_type=mesh_id,
            ).start()
            return c

        lax.fori_loop(1, n, send, 0)

        def finish(i, c):
            peer = lax.rem(me + i, n)
            origin = lax.rem(me + n - i, n)
            pltpu.make_async_remote_copy(
                src(peer), out_ref.at[me], send_sems.at[i], recv_sems.at[i],
                device_id=dev(peer), device_id_type=mesh_id,
            ).wait_send()
            pltpu.make_async_remote_copy(
                src(peer), out_ref.at[origin], send_sems.at[i], recv_sems.at[i],
                device_id=dev(origin), device_id_type=mesh_id,
            ).wait_recv()
            return c

        lax.fori_loop(1, n, finish, 0)
        local.wait()

    return pl.pallas_call(
        kernel,
        out_shape=jax.ShapeDtypeStruct((n,) + tuple(slab_shape), slabs.dtype),
        in_specs=[pl.BlockSpec(memory_space=pltpu.VMEM)],
        out_specs=pl.BlockSpec(memory_space=pltpu.VMEM),
        scratch_shapes=[
            pltpu.SemaphoreType.DMA((n,)),
            pltpu.SemaphoreType.DMA((n,)),
            pltpu.SemaphoreType.DMA(()),
        ],
        compiler_params=pltpu.CompilerParams(has_side_effects=True),
    )(slabs)


def block_stats(query, keyval, live):
    width = query.shape[-1]
    keys = keyval[..., :width]
    values = keyval[..., width:]
    scores = jnp.einsum("rhge,hrpe->rhgp", query, keys, preferred_element_type=jnp.float32) * SCALE
    mask = live[:, None, None, :]
    scores = jnp.where(mask, scores, NEG)
    top = jnp.max(scores, axis=-1)
    weights = jnp.where(mask, jnp.exp(scores - top[..., None]), 0.0)
    total = jnp.sum(weights, axis=-1)
    numer = jnp.einsum(
        "rhgp,hrpe->rhge", weights.astype(jnp.bfloat16), values, preferred_element_type=jnp.float32
    )
    return (top, total, numer)


def prompt_stats(all_query, prefix_cache, req_group, pre_len, block):
    all_rows, heads, per_kv, width = all_query.shape
    groups = prefix_cache.shape[1]
    pre_dev = prefix_cache.shape[2]
    group_ids = jnp.arange(groups, dtype=jnp.int32)
    starts = jnp.sum((req_group[None, :] < group_ids[:, None]).astype(jnp.int32), axis=1)
    slot_ids = jnp.arange(SHARE, dtype=jnp.int32)
    source = jnp.minimum(starts[:, None] + slot_ids[None, :], all_rows - 1).reshape(-1)
    slotted = jnp.take(all_query, source, axis=0).reshape(groups, SHARE, heads, per_kv, width)
    keys = prefix_cache[..., :width]
    values = prefix_cache[..., width:]
    scores = (
        jnp.einsum("gshqe,hgpe->hgsqp", slotted, keys, preferred_element_type=jnp.float32) * SCALE
    )
    pre_pos = block * pre_dev + jnp.arange(pre_dev, dtype=jnp.int32)
    live = pre_pos[None, :] < pre_len[:, None]
    mask = live[None, :, None, None, :]
    scores = jnp.where(mask, scores, NEG)
    top = jnp.max(scores, axis=-1)
    weights = jnp.where(mask, jnp.exp(scores - top[..., None]), 0.0)
    total = jnp.sum(weights, axis=-1)
    numer = jnp.einsum(
        "hgsqp,hgpe->hgsqe",
        weights.astype(jnp.bfloat16),
        values,
        preferred_element_type=jnp.float32,
    )
    match = req_group[:, None] == group_ids[None, :]
    start_req = jnp.sum(jnp.where(match, starts[None, :], 0), axis=1)
    place = req_group * SHARE + jnp.arange(all_rows, dtype=jnp.int32) - start_req
    columns = heads * per_kv
    top = jnp.take(top.reshape(heads, groups * SHARE, per_kv), place, axis=1)
    total = jnp.take(total.reshape(heads, groups * SHARE, per_kv), place, axis=1)
    numer = jnp.take(numer.reshape(heads, groups * SHARE, per_kv, width), place, axis=1)
    top = jnp.transpose(top, (1, 0, 2)).reshape(all_rows, columns)
    total = jnp.transpose(total, (1, 0, 2)).reshape(all_rows, columns)
    numer = jnp.transpose(numer, (1, 0, 2, 3)).reshape(all_rows, columns * width)
    return (top, total, numer)


def body(hidden_in, w_query, w_keyval, w_out, own_cache, prefix_cache, own_len, req_group, pre_len):
    rows = hidden_in.shape[0]
    heads = w_keyval.shape[1]
    width = w_keyval.shape[2] // 2
    per_kv = w_query.shape[1] // (heads * width)
    columns = heads * per_kv
    inputs = hidden_in.astype(jnp.float32)
    normed = (inputs * lax.rsqrt(jnp.mean(inputs * inputs, axis=1, keepdims=True) + 1e-05)).astype(
        jnp.bfloat16
    )
    query = jnp.dot(normed, w_query, preferred_element_type=jnp.float32).astype(jnp.bfloat16)
    newkv = jnp.einsum("rd,dhe->rhe", normed, w_keyval, preferred_element_type=jnp.float32).astype(
        jnp.bfloat16
    )
    n_tok = lax.axis_size("tok")
    n_kv = lax.axis_size("kv")
    q_slab = query.reshape(-1, 128)
    gathered = exchange(q_slab, "tok", "kv", n_tok, True, 0).reshape(n_tok * rows, -1)
    all_rows = gathered.shape[0]
    all_query = gathered.reshape(all_rows, heads, per_kv, width)
    block = lax.axis_index("tok")
    pre_top, pre_total, pre_numer = prompt_stats(all_query, prefix_cache, req_group, pre_len, block)
    cw = columns * width
    per_dest = rows * (cw + 2 * columns)
    lanes = -(-per_dest // 128) * 128
    packed = jnp.concatenate(
        [
            pre_numer.reshape(n_tok, rows * cw),
            pre_top.reshape(n_tok, rows * columns),
            pre_total.reshape(n_tok, rows * columns),
            jnp.zeros((n_tok, lanes - per_dest), jnp.float32),
        ],
        axis=1,
    ).reshape(n_tok, lanes // 128, 128)
    recv = exchange(packed, "tok", "kv", n_tok, False, 1).reshape(n_tok, lanes)
    r_numer = recv[:, : rows * cw].reshape(n_tok, rows, columns, width)
    r_top = recv[:, rows * cw : rows * (cw + columns)].reshape(n_tok, rows, columns)
    r_total = recv[:, rows * (cw + columns) : per_dest].reshape(n_tok, rows, columns)

    local_query = query.reshape(rows, heads, per_kv, width)
    own_cap = own_cache.shape[2]
    own_live = jnp.arange(own_cap, dtype=jnp.int32)[None, :] < own_len[:, None]
    own_top, own_total, own_numer = block_stats(local_query, own_cache, own_live)
    own_top = own_top.reshape(rows, columns)
    own_total = own_total.reshape(rows, columns)
    own_numer = own_numer.reshape(rows, columns, width)
    s_new = (
        jnp.einsum(
            "rhge,rhe->rhg", local_query, newkv[..., :width], preferred_element_type=jnp.float32
        )
        * SCALE
    )
    s_new = s_new.reshape(rows, columns)
    new_value = jnp.broadcast_to(
        newkv[:, :, None, width:].astype(jnp.float32), (rows, heads, per_kv, width)
    ).reshape(rows, columns, width)
    largest = jnp.maximum(jnp.maximum(jnp.max(r_top, axis=0), own_top), s_new)
    coef_pre = jnp.exp(r_top - largest[None])
    coef_own = jnp.exp(own_top - largest)
    coef_new = jnp.exp(s_new - largest)
    denom = jnp.sum(coef_pre * r_total, axis=0) + coef_own * own_total + coef_new
    numer = (
        jnp.sum(coef_pre[..., None] * r_numer, axis=0)
        + coef_own[..., None] * own_numer
        + coef_new[..., None] * new_value
    )
    attn = (numer / denom[..., None]).reshape(rows, columns * width).astype(jnp.bfloat16)
    partial_out = jnp.dot(attn, w_out, preferred_element_type=jnp.float32)
    out_cols = partial_out.shape[1] // n_kv
    pieces = jnp.transpose(partial_out.reshape(rows, n_kv, out_cols), (1, 0, 2))
    pieces = pieces.reshape(n_kv, rows * out_cols // 128, 128)
    summed = jnp.sum(exchange(pieces, "kv", "tok", n_kv, False, 2), axis=0)
    return summed.reshape(rows, out_cols).astype(jnp.bfloat16)


def solution(mesh):
    in_specs = (
        P("tok", None),
        P(None, "kv"),
        P(None, "kv", None),
        P("kv", None),
        P("kv", "tok", None, None),
        P("kv", None, "tok", None),
        P("tok"),
        P(),
        P(),
    )
    out_specs = P("tok", "kv")
    return jax.shard_map(body, mesh=mesh, in_specs=in_specs, out_specs=out_specs, check_vma=False)
```

```python
import jax
import jax.numpy as jnp
from jax import lax
from jax.sharding import PartitionSpec as P
from jax.experimental import pallas as pl
from jax.experimental.pallas import tpu as pltpu

SHARE = 16


SCALE = 0.015625
NEG = -1e30


def exchange(slabs, axis, other, n, broadcast, cid):
    slab_shape = slabs.shape[1:] if not broadcast else slabs.shape
    mesh_id = pl.DeviceIdType.MESH

    def kernel(x_ref, out_ref, send_sems, recv_sems, local_sem):
        me = lax.axis_index(axis)
        keep = lax.axis_index(other)

        def dev(peer):
            return (peer, keep) if axis == "tok" else (keep, peer)

        def src(peer):
            return x_ref if broadcast else x_ref.at[peer]

        barrier = pltpu.get_barrier_semaphore()

        def greet(i, c):
            peer = lax.rem(me + i, n)
            pl.semaphore_signal(barrier, inc=1, device_id=dev(peer), device_id_type=mesh_id)
            return c

        lax.fori_loop(1, n, greet, 0)
        pl.semaphore_wait(barrier, n - 1)
        local = pltpu.make_async_copy(src(me), out_ref.at[me], local_sem)
        local.start()

        def send(i, c):
            peer = lax.rem(me + i, n)
            pltpu.make_async_remote_copy(
                src(peer), out_ref.at[me], send_sems.at[i], recv_sems.at[i],
                device_id=dev(peer), device_id_type=mesh_id,
            ).start()
            return c

        lax.fori_loop(1, n, send, 0)

        def finish(i, c):
            peer = lax.rem(me + i, n)
            origin = lax.rem(me + n - i, n)
            pltpu.make_async_remote_copy(
                src(peer), out_ref.at[me], send_sems.at[i], recv_sems.at[i],
                device_id=dev(peer), device_id_type=mesh_id,
            ).wait_send()
            pltpu.make_async_remote_copy(
                src(peer), out_ref.at[origin], send_sems.at[i], recv_sems.at[i],
                device_id=dev(origin), device_id_type=mesh_id,
            ).wait_recv()
            return c

        lax.fori_loop(1, n, finish, 0)
        local.wait()

    return pl.pallas_call(
        kernel,
        out_shape=jax.ShapeDtypeStruct((n,) + tuple(slab_shape), slabs.dtype),
        in_specs=[pl.BlockSpec(memory_space=pltpu.VMEM)],
        out_specs=pl.BlockSpec(memory_space=pltpu.VMEM),
        scratch_shapes=[
            pltpu.SemaphoreType.DMA((n,)),
            pltpu.SemaphoreType.DMA((n,)),
            pltpu.SemaphoreType.DMA(()),
        ],
        compiler_params=pltpu.CompilerParams(collective_id=cid, has_side_effects=True),
    )(slabs)


def finish_kernel_call(packed, local, w_out, n_tok, n_kv):
    slab_rows = packed.shape[1]
    rows = slab_rows // 4
    heads = 4
    width = 64
    d_model = w_out.shape[1]
    cols = d_model // n_kv
    mesh_id = pl.DeviceIdType.MESH

    def kernel(packed_ref, local_ref, w_ref, out_ref, recv_scr, acc_scr, part_scr, kv_recv,
               tsend, trecv, ksend, krecv, loc_sems):
        me = lax.axis_index("tok")
        mk = lax.axis_index("kv")
        barrier = pltpu.get_barrier_semaphore()

        def greet_tok(i, c):
            pl.semaphore_signal(barrier, inc=1, device_id=(lax.rem(me + i, n_tok), mk), device_id_type=mesh_id)
            return c

        def greet_kv(i, c):
            pl.semaphore_signal(barrier, inc=1, device_id=(me, lax.rem(mk + i, n_kv)), device_id_type=mesh_id)
            return c

        lax.fori_loop(1, n_tok, greet_tok, 0)
        lax.fori_loop(1, n_kv, greet_kv, 0)
        pl.semaphore_wait(barrier, n_tok - 1 + n_kv - 1)

        local_copy = pltpu.make_async_copy(packed_ref.at[me], recv_scr.at[me], loc_sems.at[0])
        local_copy.start()

        def tok_copy(i, target, slot):
            return pltpu.make_async_remote_copy(
                packed_ref.at[target], recv_scr.at[slot], tsend.at[i], trecv.at[i],
                device_id=(target, mk), device_id_type=mesh_id,
            )

        def send_tok(i, c):
            tok_copy(i, lax.rem(me + i, n_tok), me).start()
            return c

        lax.fori_loop(1, n_tok, send_tok, 0)

        def finish_tok(i, c):
            tok_copy(i, lax.rem(me + i, n_tok), me).wait_send()
            origin = lax.rem(me + n_tok - i, n_tok)
            pltpu.make_async_remote_copy(
                packed_ref.at[origin], recv_scr.at[origin], tsend.at[i], trecv.at[i],
                device_id=(origin, mk), device_id_type=mesh_id,
            ).wait_recv()
            return c

        lax.fori_loop(1, n_tok, finish_tok, 0)
        local_copy.wait()

        x = recv_scr[...]
        lane = lax.broadcasted_iota(jnp.int32, x.shape, 2)
        top = jnp.max(jnp.where(lane == width, x, NEG), axis=2, keepdims=True)
        tot = jnp.sum(jnp.where(lane == width + 1, x, 0.0), axis=2, keepdims=True)
        loc = local_ref[...]
        llane = lax.broadcasted_iota(jnp.int32, loc.shape, 1)
        ltop = jnp.max(jnp.where(llane == width, loc, NEG), axis=1, keepdims=True)
        ltot = jnp.sum(jnp.where(llane == width + 1, loc, 0.0), axis=1, keepdims=True)
        big = jnp.maximum(jnp.max(top, axis=0), ltop)
        coef = jnp.exp(top - big[None])
        lcoef = jnp.exp(ltop - big)
        denom = jnp.sum(coef * tot, axis=0) + lcoef * ltot
        numer = jnp.sum(coef * x, axis=0) + lcoef * loc
        attn = jnp.where(llane < width, numer / denom, 0.0).astype(jnp.bfloat16).astype(jnp.float32)
        shifted = pltpu.roll(attn, width, 1)
        row = lax.broadcasted_iota(jnp.int32, attn.shape, 0)
        head_of = row // rows
        acc = jnp.zeros((slab_rows, d_model), jnp.float32)
        for pair in range(heads // 2):
            lhs = jnp.where(head_of == 2 * pair, attn, jnp.where(head_of == 2 * pair + 1, shifted, 0.0))
            acc = acc + jnp.dot(
                lhs.astype(jnp.bfloat16), w_ref[pl.ds(pair * 2 * width, 2 * width), :],
                preferred_element_type=jnp.float32,
            )
        acc_scr[...] = acc
        partial = acc_scr[pl.ds(0, rows), :]
        for h in range(1, heads):
            partial = partial + acc_scr[pl.ds(h * rows, rows), :]
        part_scr[...] = partial

        def kv_src(target):
            return part_scr.at[:, pl.ds(pl.multiple_of(target * cols, cols), cols)]

        kv_local = pltpu.make_async_copy(kv_src(mk), kv_recv.at[mk], loc_sems.at[1])
        kv_local.start()

        def kv_copy(j, target, slot):
            return pltpu.make_async_remote_copy(
                kv_src(target), kv_recv.at[slot], ksend.at[j], krecv.at[j],
                device_id=(me, target), device_id_type=mesh_id,
            )

        def send_kv(j, c):
            kv_copy(j, lax.rem(mk + j, n_kv), mk).start()
            return c

        lax.fori_loop(1, n_kv, send_kv, 0)

        def finish_kv(j, c):
            kv_copy(j, lax.rem(mk + j, n_kv), mk).wait_send()
            origin = lax.rem(mk + n_kv - j, n_kv)
            pltpu.make_async_remote_copy(
                kv_src(origin), kv_recv.at[origin], ksend.at[j], krecv.at[j],
                device_id=(me, origin), device_id_type=mesh_id,
            ).wait_recv()
            return c

        lax.fori_loop(1, n_kv, finish_kv, 0)
        kv_local.wait()
        out_ref[...] = jnp.sum(kv_recv[...], axis=0).astype(out_ref.dtype)

    return pl.pallas_call(
        kernel,
        out_shape=jax.ShapeDtypeStruct((rows, cols), jnp.bfloat16),
        in_specs=[pl.BlockSpec(memory_space=pltpu.VMEM)] * 3,
        out_specs=pl.BlockSpec(memory_space=pltpu.VMEM),
        scratch_shapes=[
            pltpu.VMEM(packed.shape, jnp.float32),
            pltpu.VMEM((slab_rows, d_model), jnp.float32),
            pltpu.VMEM((rows, d_model), jnp.float32),
            pltpu.VMEM((n_kv, rows, cols), jnp.float32),
            pltpu.SemaphoreType.DMA((n_tok,)),
            pltpu.SemaphoreType.DMA((n_tok,)),
            pltpu.SemaphoreType.DMA((n_kv,)),
            pltpu.SemaphoreType.DMA((n_kv,)),
            pltpu.SemaphoreType.DMA((2,)),
        ],
        compiler_params=pltpu.CompilerParams(collective_id=1, has_side_effects=True),
    )(packed, local, w_out)


def block_stats(query, keyval, live):
    width = query.shape[-1]
    keys = keyval[..., :width]
    values = keyval[..., width:]
    scores = jnp.einsum("rhge,hrpe->rhgp", query, keys, preferred_element_type=jnp.float32) * SCALE
    mask = live[:, None, None, :]
    scores = jnp.where(mask, scores, NEG)
    top = jnp.max(scores, axis=-1)
    weights = jnp.where(mask, jnp.exp(scores - top[..., None]), 0.0)
    total = jnp.sum(weights, axis=-1)
    numer = jnp.einsum(
        "rhgp,hrpe->rhge", weights.astype(jnp.bfloat16), values, preferred_element_type=jnp.float32
    )
    return (top, total, numer)


def prompt_stats(all_query, prefix_cache, req_group, pre_len, block):
    all_rows, heads, per_kv, width = all_query.shape
    groups = prefix_cache.shape[1]
    pre_dev = prefix_cache.shape[2]
    group_ids = jnp.arange(groups, dtype=jnp.int32)
    starts = jnp.sum((req_group[None, :] < group_ids[:, None]).astype(jnp.int32), axis=1)
    slot_ids = jnp.arange(SHARE, dtype=jnp.int32)
    source = jnp.minimum(starts[:, None] + slot_ids[None, :], all_rows - 1).reshape(-1)
    slotted = jnp.take(all_query, source, axis=0).reshape(groups, SHARE, heads, per_kv, width)
    keys = prefix_cache[..., :width]
    values = prefix_cache[..., width:]
    scores = (
        jnp.einsum("gshqe,hgpe->hgsqp", slotted, keys, preferred_element_type=jnp.float32) * SCALE
    )
    pre_pos = block * pre_dev + jnp.arange(pre_dev, dtype=jnp.int32)
    live = pre_pos[None, :] < pre_len[:, None]
    mask = live[None, :, None, None, :]
    scores = jnp.where(mask, scores, NEG)
    top = jnp.max(scores, axis=-1)
    weights = jnp.where(mask, jnp.exp(scores - top[..., None]), 0.0)
    total = jnp.sum(weights, axis=-1)
    numer = jnp.einsum(
        "hgsqp,hgpe->hgsqe",
        weights.astype(jnp.bfloat16),
        values,
        preferred_element_type=jnp.float32,
    )
    match = req_group[:, None] == group_ids[None, :]
    start_req = jnp.sum(jnp.where(match, starts[None, :], 0), axis=1)
    place = req_group * SHARE + jnp.arange(all_rows, dtype=jnp.int32) - start_req
    columns = heads * per_kv
    top = jnp.take(top.reshape(heads, groups * SHARE, per_kv), place, axis=1)
    total = jnp.take(total.reshape(heads, groups * SHARE, per_kv), place, axis=1)
    numer = jnp.take(numer.reshape(heads, groups * SHARE, per_kv, width), place, axis=1)
    top = jnp.transpose(top, (1, 0, 2)).reshape(all_rows, columns)
    total = jnp.transpose(total, (1, 0, 2)).reshape(all_rows, columns)
    numer = jnp.transpose(numer, (1, 0, 2, 3)).reshape(all_rows, columns * width)
    return (top, total, numer)


def body(hidden_in, w_query, w_keyval, w_out, own_cache, prefix_cache, own_len, req_group, pre_len):
    rows = hidden_in.shape[0]
    heads = w_keyval.shape[1]
    width = w_keyval.shape[2] // 2
    per_kv = w_query.shape[1] // (heads * width)
    columns = heads * per_kv
    inputs = hidden_in.astype(jnp.float32)
    normed = (inputs * lax.rsqrt(jnp.mean(inputs * inputs, axis=1, keepdims=True) + 1e-05)).astype(
        jnp.bfloat16
    )
    query = jnp.dot(normed, w_query, preferred_element_type=jnp.float32).astype(jnp.bfloat16)
    newkv = jnp.einsum("rd,dhe->rhe", normed, w_keyval, preferred_element_type=jnp.float32).astype(
        jnp.bfloat16
    )
    n_tok = lax.axis_size("tok")
    n_kv = lax.axis_size("kv")
    q_slab = query.reshape(-1, 128)
    gathered = exchange(q_slab, "tok", "kv", n_tok, True, 0).reshape(n_tok * rows, -1)
    all_rows = gathered.shape[0]
    all_query = gathered.reshape(all_rows, heads, per_kv, width)
    block = lax.axis_index("tok")
    pre_top, pre_total, pre_numer = prompt_stats(all_query, prefix_cache, req_group, pre_len, block)
    local_query = query.reshape(rows, heads, per_kv, width)
    own_cap = own_cache.shape[2]
    own_live = jnp.arange(own_cap, dtype=jnp.int32)[None, :] < own_len[:, None]
    own_top, own_total, own_numer = block_stats(local_query, own_cache, own_live)
    own_top = own_top.reshape(rows, columns)
    own_total = own_total.reshape(rows, columns)
    own_numer = own_numer.reshape(rows, columns, width)
    s_new = (
        jnp.einsum(
            "rhge,rhe->rhg", local_query, newkv[..., :width], preferred_element_type=jnp.float32
        )
        * SCALE
    )
    s_new = s_new.reshape(rows, columns)
    new_value = jnp.broadcast_to(
        newkv[:, :, None, width:].astype(jnp.float32), (rows, heads, per_kv, width)
    ).reshape(rows, columns, width)
    l_top = jnp.maximum(own_top, s_new)
    c_own = jnp.exp(own_top - l_top)
    c_new = jnp.exp(s_new - l_top)
    l_total = c_own * own_total + c_new
    l_numer = c_own[..., None] * own_numer + c_new[..., None] * new_value

    def slab(numer, top, total):
        lead = numer.shape[:-3]
        parts = [numer, top[..., None], total[..., None]]
        parts.append(jnp.zeros(numer.shape[:-1] + (128 - width - 2,), jnp.float32))
        full = jnp.concatenate(parts, axis=-1)
        axes = tuple(range(len(lead)))
        full = jnp.transpose(full, axes + (len(lead) + 1, len(lead), len(lead) + 2))
        return full.reshape(lead + (columns * rows, 128))

    packed = slab(
        pre_numer.reshape(n_tok, rows, columns, width),
        pre_top.reshape(n_tok, rows, columns),
        pre_total.reshape(n_tok, rows, columns),
    )
    local = slab(l_numer, l_top, l_total)
    return finish_kernel_call(packed, local, w_out, n_tok, n_kv)


def solution(mesh):
    in_specs = (
        P("tok", None),
        P(None, "kv"),
        P(None, "kv", None),
        P("kv", None),
        P("kv", "tok", None, None),
        P("kv", None, "tok", None),
        P("tok"),
        P(),
        P(),
    )
    out_specs = P("tok", "kv")
    return jax.shard_map(body, mesh=mesh, in_specs=in_specs, out_specs=out_specs, check_vma=False)
```

```python
import jax
import jax.numpy as jnp
from jax import lax
from jax.sharding import PartitionSpec as P
from jax.experimental import pallas as pl
from jax.experimental.pallas import tpu as pltpu

SHARE = 16


SCALE = 0.015625
NEG = -1e30


def exchange(slabs, axis, other, n, broadcast, cid):
    slab_shape = slabs.shape[1:] if not broadcast else slabs.shape
    mesh_id = pl.DeviceIdType.MESH

    def kernel(x_ref, out_ref, send_sems, recv_sems, local_sem):
        me = lax.axis_index(axis)
        keep = lax.axis_index(other)

        def dev(peer):
            return (peer, keep) if axis == "tok" else (keep, peer)

        def src(peer):
            return x_ref if broadcast else x_ref.at[peer]

        barrier = pltpu.get_barrier_semaphore()

        def greet(i, c):
            peer = lax.rem(me + i, n)
            pl.semaphore_signal(barrier, inc=1, device_id=dev(peer), device_id_type=mesh_id)
            return c

        lax.fori_loop(1, n, greet, 0)
        pl.semaphore_wait(barrier, n - 1)
        local = pltpu.make_async_copy(src(me), out_ref.at[me], local_sem)
        local.start()

        def send(i, c):
            peer = lax.rem(me + i, n)
            pltpu.make_async_remote_copy(
                src(peer), out_ref.at[me], send_sems.at[i], recv_sems.at[i],
                device_id=dev(peer), device_id_type=mesh_id,
            ).start()
            return c

        lax.fori_loop(1, n, send, 0)

        def finish(i, c):
            peer = lax.rem(me + i, n)
            origin = lax.rem(me + n - i, n)
            pltpu.make_async_remote_copy(
                src(peer), out_ref.at[me], send_sems.at[i], recv_sems.at[i],
                device_id=dev(peer), device_id_type=mesh_id,
            ).wait_send()
            pltpu.make_async_remote_copy(
                src(peer), out_ref.at[origin], send_sems.at[i], recv_sems.at[i],
                device_id=dev(origin), device_id_type=mesh_id,
            ).wait_recv()
            return c

        lax.fori_loop(1, n, finish, 0)
        local.wait()

    return pl.pallas_call(
        kernel,
        out_shape=jax.ShapeDtypeStruct((n,) + tuple(slab_shape), slabs.dtype),
        in_specs=[pl.BlockSpec(memory_space=pltpu.VMEM)],
        out_specs=pl.BlockSpec(memory_space=pltpu.VMEM),
        scratch_shapes=[
            pltpu.SemaphoreType.DMA((n,)),
            pltpu.SemaphoreType.DMA((n,)),
            pltpu.SemaphoreType.DMA(()),
        ],
        compiler_params=pltpu.CompilerParams(collective_id=cid, has_side_effects=True),
    )(slabs)


def finish_kernel_call(packed, local, w_out, n_tok, n_kv):
    slab_rows = packed.shape[1]
    rows = slab_rows // 4
    heads = 4
    width = 64
    d_model = w_out.shape[1]
    cols = d_model // n_kv
    mesh_id = pl.DeviceIdType.MESH

    def kernel(packed_ref, local_ref, w_ref, out_ref, recv_scr, acc_scr, part_scr, kv_recv,
               tsend, trecv, ksend, krecv, loc_sems):
        me = lax.axis_index("tok")
        mk = lax.axis_index("kv")
        barrier = pltpu.get_barrier_semaphore()

        def greet_tok(i, c):
            pl.semaphore_signal(barrier, inc=1, device_id=(lax.rem(me + i, n_tok), mk), device_id_type=mesh_id)
            return c

        def greet_kv(i, c):
            pl.semaphore_signal(barrier, inc=1, device_id=(me, lax.rem(mk + i, n_kv)), device_id_type=mesh_id)
            return c

        lax.fori_loop(1, n_tok, greet_tok, 0)
        lax.fori_loop(1, n_kv, greet_kv, 0)
        pl.semaphore_wait(barrier, n_tok - 1 + n_kv - 1)

        local_copy = pltpu.make_async_copy(packed_ref.at[me], recv_scr.at[me], loc_sems.at[0])
        local_copy.start()

        def tok_copy(i, target, slot):
            return pltpu.make_async_remote_copy(
                packed_ref.at[target], recv_scr.at[slot], tsend.at[i], trecv.at[i],
                device_id=(target, mk), device_id_type=mesh_id,
            )

        def send_tok(i, c):
            tok_copy(i, lax.rem(me + i, n_tok), me).start()
            return c

        lax.fori_loop(1, n_tok, send_tok, 0)

        def finish_tok(i, c):
            tok_copy(i, lax.rem(me + i, n_tok), me).wait_send()
            origin = lax.rem(me + n_tok - i, n_tok)
            pltpu.make_async_remote_copy(
                packed_ref.at[origin], recv_scr.at[origin], tsend.at[i], trecv.at[i],
                device_id=(origin, mk), device_id_type=mesh_id,
            ).wait_recv()
            return c

        lax.fori_loop(1, n_tok, finish_tok, 0)
        local_copy.wait()

        x = recv_scr[...]
        lane = lax.broadcasted_iota(jnp.int32, x.shape, 2)
        top = jnp.max(jnp.where(lane == width, x, NEG), axis=2, keepdims=True)
        tot = jnp.sum(jnp.where(lane == width + 1, x, 0.0), axis=2, keepdims=True)
        loc = local_ref[...]
        llane = lax.broadcasted_iota(jnp.int32, loc.shape, 1)
        ltop = jnp.max(jnp.where(llane == width, loc, NEG), axis=1, keepdims=True)
        ltot = jnp.sum(jnp.where(llane == width + 1, loc, 0.0), axis=1, keepdims=True)
        big = jnp.maximum(jnp.max(top, axis=0), ltop)
        coef = jnp.exp(top - big[None])
        lcoef = jnp.exp(ltop - big)
        denom = jnp.sum(coef * tot, axis=0) + lcoef * ltot
        numer = jnp.sum(coef * x, axis=0) + lcoef * loc
        attn = jnp.where(llane < width, numer / denom, 0.0).astype(jnp.bfloat16)
        pi = lax.broadcasted_iota(jnp.int32, (slab_rows, slab_rows), 0)
        pj = lax.broadcasted_iota(jnp.int32, (slab_rows, slab_rows), 1)
        perm = jnp.where(pj == (pi % rows) * heads + pi // rows, 1.0, 0.0).astype(jnp.bfloat16)
        attn = jnp.dot(perm, attn, preferred_element_type=jnp.float32)
        shifted = pltpu.roll(attn, width, 1)
        row = lax.broadcasted_iota(jnp.int32, attn.shape, 0)
        head_of = row // rows
        acc = jnp.zeros((slab_rows, d_model), jnp.float32)
        for pair in range(heads // 2):
            lhs = jnp.where(head_of == 2 * pair, attn, jnp.where(head_of == 2 * pair + 1, shifted, 0.0))
            acc = acc + jnp.dot(
                lhs.astype(jnp.bfloat16), w_ref[pl.ds(pair * 2 * width, 2 * width), :],
                preferred_element_type=jnp.float32,
            )
        acc_scr[...] = acc
        partial = acc_scr[pl.ds(0, rows), :]
        for h in range(1, heads):
            partial = partial + acc_scr[pl.ds(h * rows, rows), :]
        part_scr[...] = partial

        def kv_src(target):
            return part_scr.at[:, pl.ds(pl.multiple_of(target * cols, cols), cols)]

        kv_local = pltpu.make_async_copy(kv_src(mk), kv_recv.at[mk], loc_sems.at[1])
        kv_local.start()

        def kv_copy(j, target, slot):
            return pltpu.make_async_remote_copy(
                kv_src(target), kv_recv.at[slot], ksend.at[j], krecv.at[j],
                device_id=(me, target), device_id_type=mesh_id,
            )

        def send_kv(j, c):
            kv_copy(j, lax.rem(mk + j, n_kv), mk).start()
            return c

        lax.fori_loop(1, n_kv, send_kv, 0)

        def finish_kv(j, c):
            kv_copy(j, lax.rem(mk + j, n_kv), mk).wait_send()
            origin = lax.rem(mk + n_kv - j, n_kv)
            pltpu.make_async_remote_copy(
                kv_src(origin), kv_recv.at[origin], ksend.at[j], krecv.at[j],
                device_id=(me, origin), device_id_type=mesh_id,
            ).wait_recv()
            return c

        lax.fori_loop(1, n_kv, finish_kv, 0)
        kv_local.wait()
        out_ref[...] = jnp.sum(kv_recv[...], axis=0).astype(out_ref.dtype)

    return pl.pallas_call(
        kernel,
        out_shape=jax.ShapeDtypeStruct((rows, cols), jnp.bfloat16),
        in_specs=[pl.BlockSpec(memory_space=pltpu.VMEM)] * 3,
        out_specs=pl.BlockSpec(memory_space=pltpu.VMEM),
        scratch_shapes=[
            pltpu.VMEM(packed.shape, jnp.float32),
            pltpu.VMEM((slab_rows, d_model), jnp.float32),
            pltpu.VMEM((rows, d_model), jnp.float32),
            pltpu.VMEM((n_kv, rows, cols), jnp.float32),
            pltpu.SemaphoreType.DMA((n_tok,)),
            pltpu.SemaphoreType.DMA((n_tok,)),
            pltpu.SemaphoreType.DMA((n_kv,)),
            pltpu.SemaphoreType.DMA((n_kv,)),
            pltpu.SemaphoreType.DMA((2,)),
        ],
        compiler_params=pltpu.CompilerParams(collective_id=1, has_side_effects=True),
    )(packed, local, w_out)


def block_stats(query, keyval, live):
    width = query.shape[-1]
    keys = keyval[..., :width]
    values = keyval[..., width:]
    scores = jnp.einsum("rhge,hrpe->rhgp", query, keys, preferred_element_type=jnp.float32) * SCALE
    mask = live[:, None, None, :]
    scores = jnp.where(mask, scores, NEG)
    top = jnp.max(scores, axis=-1)
    weights = jnp.where(mask, jnp.exp(scores - top[..., None]), 0.0)
    total = jnp.sum(weights, axis=-1)
    numer = jnp.einsum(
        "rhgp,hrpe->rhge", weights.astype(jnp.bfloat16), values, preferred_element_type=jnp.float32
    )
    return (top, total, numer)


def prompt_stats(all_query, prefix_cache, req_group, pre_len, block):
    all_rows, heads, per_kv, width = all_query.shape
    groups = prefix_cache.shape[1]
    pre_dev = prefix_cache.shape[2]
    group_ids = jnp.arange(groups, dtype=jnp.int32)
    starts = jnp.sum((req_group[None, :] < group_ids[:, None]).astype(jnp.int32), axis=1)
    slot_ids = jnp.arange(SHARE, dtype=jnp.int32)
    source = jnp.minimum(starts[:, None] + slot_ids[None, :], all_rows - 1).reshape(-1)
    slotted = jnp.take(all_query, source, axis=0).reshape(groups, SHARE, heads, per_kv, width)
    keys = prefix_cache[..., :width]
    values = prefix_cache[..., width:]
    scores = (
        jnp.einsum("gshqe,hgpe->hgsqp", slotted, keys, preferred_element_type=jnp.float32) * SCALE
    )
    pre_pos = block * pre_dev + jnp.arange(pre_dev, dtype=jnp.int32)
    live = pre_pos[None, :] < pre_len[:, None]
    mask = live[None, :, None, None, :]
    scores = jnp.where(mask, scores, NEG)
    top = jnp.max(scores, axis=-1)
    weights = jnp.where(mask, jnp.exp(scores - top[..., None]), 0.0)
    total = jnp.sum(weights, axis=-1)
    numer = jnp.einsum(
        "hgsqp,hgpe->hgsqe",
        weights.astype(jnp.bfloat16),
        values,
        preferred_element_type=jnp.float32,
    )
    match = req_group[:, None] == group_ids[None, :]
    start_req = jnp.sum(jnp.where(match, starts[None, :], 0), axis=1)
    place = req_group * SHARE + jnp.arange(all_rows, dtype=jnp.int32) - start_req
    packed = jnp.concatenate(
        [numer, top[..., None], total[..., None],
         jnp.zeros(top.shape + (128 - width - 2,), jnp.float32)],
        axis=-1,
    ).reshape(heads, groups * SHARE, per_kv, 128)
    packed = jnp.take(packed, place, axis=1)
    return jnp.transpose(packed, (1, 0, 2, 3)).reshape(all_rows * heads * per_kv, 128)


def body(hidden_in, w_query, w_keyval, w_out, own_cache, prefix_cache, own_len, req_group, pre_len):
    rows = hidden_in.shape[0]
    heads = w_keyval.shape[1]
    width = w_keyval.shape[2] // 2
    per_kv = w_query.shape[1] // (heads * width)
    columns = heads * per_kv
    inputs = hidden_in.astype(jnp.float32)
    normed = (inputs * lax.rsqrt(jnp.mean(inputs * inputs, axis=1, keepdims=True) + 1e-05)).astype(
        jnp.bfloat16
    )
    query = jnp.dot(normed, w_query, preferred_element_type=jnp.float32).astype(jnp.bfloat16)
    newkv = jnp.einsum("rd,dhe->rhe", normed, w_keyval, preferred_element_type=jnp.float32).astype(
        jnp.bfloat16
    )
    n_tok = lax.axis_size("tok")
    n_kv = lax.axis_size("kv")
    q_slab = query.reshape(-1, 128)
    gathered = exchange(q_slab, "tok", "kv", n_tok, True, 0).reshape(n_tok * rows, -1)
    all_rows = gathered.shape[0]
    all_query = gathered.reshape(all_rows, heads, per_kv, width)
    block = lax.axis_index("tok")
    packed = prompt_stats(all_query, prefix_cache, req_group, pre_len, block)
    packed = packed.reshape(n_tok, -1, 128)
    local_query = query.reshape(rows, heads, per_kv, width)
    own_cap = own_cache.shape[2]
    own_live = jnp.arange(own_cap, dtype=jnp.int32)[None, :] < own_len[:, None]
    own_top, own_total, own_numer = block_stats(local_query, own_cache, own_live)
    own_top = own_top.reshape(rows, columns)
    own_total = own_total.reshape(rows, columns)
    own_numer = own_numer.reshape(rows, columns, width)
    s_new = (
        jnp.einsum(
            "rhge,rhe->rhg", local_query, newkv[..., :width], preferred_element_type=jnp.float32
        )
        * SCALE
    )
    s_new = s_new.reshape(rows, columns)
    new_value = jnp.broadcast_to(
        newkv[:, :, None, width:].astype(jnp.float32), (rows, heads, per_kv, width)
    ).reshape(rows, columns, width)
    l_top = jnp.maximum(own_top, s_new)
    c_own = jnp.exp(own_top - l_top)
    c_new = jnp.exp(s_new - l_top)
    l_total = c_own * own_total + c_new
    l_numer = c_own[..., None] * own_numer + c_new[..., None] * new_value

    local = jnp.concatenate(
        [l_numer, l_top[..., None], l_total[..., None],
         jnp.zeros((rows, columns, 128 - width - 2), jnp.float32)],
        axis=-1,
    ).reshape(rows * columns, 128)
    return finish_kernel_call(packed, local, w_out, n_tok, n_kv)


def solution(mesh):
    in_specs = (
        P("tok", None),
        P(None, "kv"),
        P(None, "kv", None),
        P("kv", None),
        P("kv", "tok", None, None),
        P("kv", None, "tok", None),
        P("tok"),
        P(),
        P(),
    )
    out_specs = P("tok", "kv")
    return jax.shard_map(body, mesh=mesh, in_specs=in_specs, out_specs=out_specs, check_vma=False)
```

```python
import jax
import jax.numpy as jnp
from jax import lax
from jax.sharding import PartitionSpec as P
from jax.experimental import pallas as pl
from jax.experimental.pallas import tpu as pltpu

SHARE = 16


SCALE = 0.015625
NEG = -1e30


def exchange(slabs, axis, other, n, broadcast, cid):
    slab_shape = slabs.shape[1:] if not broadcast else slabs.shape
    mesh_id = pl.DeviceIdType.MESH

    def kernel(x_ref, out_ref, send_sems, recv_sems, local_sem):
        me = lax.axis_index(axis)
        keep = lax.axis_index(other)

        def dev(peer):
            return (peer, keep) if axis == "tok" else (keep, peer)

        def src(peer):
            return x_ref if broadcast else x_ref.at[peer]

        barrier = pltpu.get_barrier_semaphore()

        def greet(i, c):
            peer = lax.rem(me + i, n)
            pl.semaphore_signal(barrier, inc=1, device_id=dev(peer), device_id_type=mesh_id)
            return c

        lax.fori_loop(1, n, greet, 0)
        pl.semaphore_wait(barrier, n - 1)
        local = pltpu.make_async_copy(src(me), out_ref.at[me], local_sem)
        local.start()

        def send(i, c):
            peer = lax.rem(me + i, n)
            pltpu.make_async_remote_copy(
                src(peer), out_ref.at[me], send_sems.at[i], recv_sems.at[i],
                device_id=dev(peer), device_id_type=mesh_id,
            ).start()
            return c

        lax.fori_loop(1, n, send, 0)

        def finish(i, c):
            peer = lax.rem(me + i, n)
            origin = lax.rem(me + n - i, n)
            pltpu.make_async_remote_copy(
                src(peer), out_ref.at[me], send_sems.at[i], recv_sems.at[i],
                device_id=dev(peer), device_id_type=mesh_id,
            ).wait_send()
            pltpu.make_async_remote_copy(
                src(peer), out_ref.at[origin], send_sems.at[i], recv_sems.at[i],
                device_id=dev(origin), device_id_type=mesh_id,
            ).wait_recv()
            return c

        lax.fori_loop(1, n, finish, 0)
        local.wait()

    return pl.pallas_call(
        kernel,
        out_shape=jax.ShapeDtypeStruct((n,) + tuple(slab_shape), slabs.dtype),
        in_specs=[pl.BlockSpec(memory_space=pltpu.VMEM)],
        out_specs=pl.BlockSpec(memory_space=pltpu.VMEM),
        scratch_shapes=[
            pltpu.SemaphoreType.DMA((n,)),
            pltpu.SemaphoreType.DMA((n,)),
            pltpu.SemaphoreType.DMA(()),
        ],
        compiler_params=pltpu.CompilerParams(collective_id=cid, has_side_effects=True),
    )(slabs)


def broadcast_with_own(q_slab, q16, lens16, own_cache, n, scale):
    mesh_id = pl.DeviceIdType.MESH
    reqs, cap, lanes = own_cache.shape[1:]
    half = lanes // 2
    per = q16.shape[0] // reqs

    def kernel(x_ref, q_ref, len_ref, own_hbm, out_ref, own_out, own_vmem,
               send_sems, recv_sems, local_sem, own_sem):
        me = lax.axis_index("tok")
        keep = lax.axis_index("kv")
        own_copy = pltpu.make_async_copy(own_hbm.at[0], own_vmem, own_sem)
        own_copy.start()
        barrier = pltpu.get_barrier_semaphore()

        def greet(i, c):
            pl.semaphore_signal(barrier, inc=1, device_id=(lax.rem(me + i, n), keep), device_id_type=mesh_id)
            return c

        lax.fori_loop(1, n, greet, 0)
        pl.semaphore_wait(barrier, n - 1)
        local = pltpu.make_async_copy(x_ref, out_ref.at[me], local_sem)
        local.start()

        def send(i, c):
            peer = lax.rem(me + i, n)
            pltpu.make_async_remote_copy(
                x_ref, out_ref.at[me], send_sems.at[i], recv_sems.at[i],
                device_id=(peer, keep), device_id_type=mesh_id,
            ).start()
            return c

        lax.fori_loop(1, n, send, 0)
        own_copy.wait()
        q = q_ref[...]
        row = lax.broadcasted_iota(jnp.int32, (q.shape[0], cap), 0)
        pos = lax.broadcasted_iota(jnp.int32, (q.shape[0], cap), 1)
        scores = jnp.zeros((q.shape[0], cap), jnp.float32)
        for r in range(reqs):
            part = lax.dot_general(q, own_vmem[r], (((1,), (1,)), ((), ())),
                                   preferred_element_type=jnp.float32)
            scores = jnp.where(row // per == r, part, scores)
        scores = scores * scale
        live = pos < len_ref[...]
        scores = jnp.where(live, scores, NEG)
        top = jnp.max(scores, axis=1, keepdims=True)
        weights = jnp.where(live, jnp.exp(scores - top), 0.0)
        total = jnp.sum(weights, axis=1, keepdims=True)
        wb = weights.astype(jnp.bfloat16)
        acc = jnp.zeros((q.shape[0], lanes), jnp.float32)
        for r in range(reqs):
            acc = acc + jnp.dot(jnp.where(row // per == r, wb, jnp.zeros_like(wb)), own_vmem[r],
                                preferred_element_type=jnp.float32)
        numer = pltpu.roll(acc, half, 1)
        lane = lax.broadcasted_iota(jnp.int32, acc.shape, 1)
        own_out[...] = jnp.where(lane < half, numer,
                                 jnp.where(lane == half, top, jnp.where(lane == half + 1, total, 0.0)))

        def finish(i, c):
            peer = lax.rem(me + i, n)
            origin = lax.rem(me + n - i, n)
            pltpu.make_async_remote_copy(
                x_ref, out_ref.at[me], send_sems.at[i], recv_sems.at[i],
                device_id=(peer, keep), device_id_type=mesh_id,
            ).wait_send()
            pltpu.make_async_remote_copy(
                x_ref, out_ref.at[origin], send_sems.at[i], recv_sems.at[i],
                device_id=(origin, keep), device_id_type=mesh_id,
            ).wait_recv()
            return c

        lax.fori_loop(1, n, finish, 0)
        local.wait()

    return pl.pallas_call(
        kernel,
        out_shape=(
            jax.ShapeDtypeStruct((n,) + tuple(q_slab.shape), q_slab.dtype),
            jax.ShapeDtypeStruct((q16.shape[0], lanes), jnp.float32),
        ),
        in_specs=[pl.BlockSpec(memory_space=pltpu.VMEM)] * 3 + [pl.BlockSpec(memory_space=pl.ANY)],
        out_specs=(pl.BlockSpec(memory_space=pltpu.VMEM), pl.BlockSpec(memory_space=pltpu.VMEM)),
        scratch_shapes=[
            pltpu.VMEM((reqs, cap, lanes), own_cache.dtype),
            pltpu.SemaphoreType.DMA((n,)),
            pltpu.SemaphoreType.DMA((n,)),
            pltpu.SemaphoreType.DMA(()),
            pltpu.SemaphoreType.DMA(()),
        ],
        compiler_params=pltpu.CompilerParams(collective_id=0, has_side_effects=True),
    )(q_slab, q16, lens16, own_cache)


def finish_kernel_call(packed, own, new, w_out, n_tok, n_kv):
    slab_rows = packed.shape[1]
    rows = slab_rows // 4
    heads = 4
    width = 64
    d_model = w_out.shape[1]
    cols = d_model // n_kv
    mesh_id = pl.DeviceIdType.MESH

    def kernel(packed_ref, own_ref, new_ref, w_ref, out_ref, recv_scr, acc_scr, part_scr, kv_recv,
               tsend, trecv, ksend, krecv, loc_sems):
        me = lax.axis_index("tok")
        mk = lax.axis_index("kv")
        barrier = pltpu.get_barrier_semaphore()

        def greet_tok(i, c):
            pl.semaphore_signal(barrier, inc=1, device_id=(lax.rem(me + i, n_tok), mk), device_id_type=mesh_id)
            return c

        def greet_kv(i, c):
            pl.semaphore_signal(barrier, inc=1, device_id=(me, lax.rem(mk + i, n_kv)), device_id_type=mesh_id)
            return c

        lax.fori_loop(1, n_tok, greet_tok, 0)
        lax.fori_loop(1, n_kv, greet_kv, 0)
        pl.semaphore_wait(barrier, n_tok - 1 + n_kv - 1)

        local_copy = pltpu.make_async_copy(packed_ref.at[me], recv_scr.at[me], loc_sems.at[0])
        local_copy.start()

        def tok_copy(i, target, slot):
            return pltpu.make_async_remote_copy(
                packed_ref.at[target], recv_scr.at[slot], tsend.at[i], trecv.at[i],
                device_id=(target, mk), device_id_type=mesh_id,
            )

        def send_tok(i, c):
            tok_copy(i, lax.rem(me + i, n_tok), me).start()
            return c

        lax.fori_loop(1, n_tok, send_tok, 0)

        def finish_tok(i, c):
            tok_copy(i, lax.rem(me + i, n_tok), me).wait_send()
            origin = lax.rem(me + n_tok - i, n_tok)
            pltpu.make_async_remote_copy(
                packed_ref.at[origin], recv_scr.at[origin], tsend.at[i], trecv.at[i],
                device_id=(origin, mk), device_id_type=mesh_id,
            ).wait_recv()
            return c

        lax.fori_loop(1, n_tok, finish_tok, 0)
        local_copy.wait()

        x = recv_scr[...]
        lane = lax.broadcasted_iota(jnp.int32, x.shape, 2)
        top = jnp.max(jnp.where(lane == width, x, NEG), axis=2, keepdims=True)
        tot = jnp.sum(jnp.where(lane == width + 1, x, 0.0), axis=2, keepdims=True)
        loc = own_ref[...]
        nloc = new_ref[...]
        llane = lax.broadcasted_iota(jnp.int32, loc.shape, 1)
        ltop = jnp.max(jnp.where(llane == width, loc, NEG), axis=1, keepdims=True)
        ltot = jnp.sum(jnp.where(llane == width + 1, loc, 0.0), axis=1, keepdims=True)
        ntop = jnp.max(jnp.where(llane == width, nloc, NEG), axis=1, keepdims=True)
        big = jnp.maximum(jnp.maximum(jnp.max(top, axis=0), ltop), ntop)
        coef = jnp.exp(top - big[None])
        lcoef = jnp.exp(ltop - big)
        ncoef = jnp.exp(ntop - big)
        denom = jnp.sum(coef * tot, axis=0) + lcoef * ltot + ncoef
        numer = jnp.sum(coef * x, axis=0) + lcoef * loc + ncoef * nloc
        attn = jnp.where(llane < width, numer / denom, 0.0).astype(jnp.bfloat16)
        pi = lax.broadcasted_iota(jnp.int32, (slab_rows, slab_rows), 0)
        pj = lax.broadcasted_iota(jnp.int32, (slab_rows, slab_rows), 1)
        perm = jnp.where(pj == (pi % rows) * heads + pi // rows, 1.0, 0.0).astype(jnp.bfloat16)
        attn = jnp.dot(perm, attn, preferred_element_type=jnp.float32)
        shifted = pltpu.roll(attn, width, 1)
        row = lax.broadcasted_iota(jnp.int32, attn.shape, 0)
        head_of = row // rows
        acc = jnp.zeros((slab_rows, d_model), jnp.float32)
        for pair in range(heads // 2):
            lhs = jnp.where(head_of == 2 * pair, attn, jnp.where(head_of == 2 * pair + 1, shifted, 0.0))
            acc = acc + jnp.dot(
                lhs.astype(jnp.bfloat16), w_ref[pl.ds(pair * 2 * width, 2 * width), :],
                preferred_element_type=jnp.float32,
            )
        acc_scr[...] = acc
        partial = acc_scr[pl.ds(0, rows), :]
        for h in range(1, heads):
            partial = partial + acc_scr[pl.ds(h * rows, rows), :]
        part_scr[...] = partial

        def kv_src(target):
            return part_scr.at[:, pl.ds(pl.multiple_of(target * cols, cols), cols)]

        kv_local = pltpu.make_async_copy(kv_src(mk), kv_recv.at[mk], loc_sems.at[1])
        kv_local.start()

        def kv_copy(j, target, slot):
            return pltpu.make_async_remote_copy(
                kv_src(target), kv_recv.at[slot], ksend.at[j], krecv.at[j],
                device_id=(me, target), device_id_type=mesh_id,
            )

        def send_kv(j, c):
            kv_copy(j, lax.rem(mk + j, n_kv), mk).start()
            return c

        lax.fori_loop(1, n_kv, send_kv, 0)

        def finish_kv(j, c):
            kv_copy(j, lax.rem(mk + j, n_kv), mk).wait_send()
            origin = lax.rem(mk + n_kv - j, n_kv)
            pltpu.make_async_remote_copy(
                kv_src(origin), kv_recv.at[origin], ksend.at[j], krecv.at[j],
                device_id=(me, origin), device_id_type=mesh_id,
            ).wait_recv()
            return c

        lax.fori_loop(1, n_kv, finish_kv, 0)
        kv_local.wait()
        out_ref[...] = jnp.sum(kv_recv[...], axis=0).astype(out_ref.dtype)

    return pl.pallas_call(
        kernel,
        out_shape=jax.ShapeDtypeStruct((rows, cols), jnp.bfloat16),
        in_specs=[pl.BlockSpec(memory_space=pltpu.VMEM)] * 4,
        out_specs=pl.BlockSpec(memory_space=pltpu.VMEM),
        scratch_shapes=[
            pltpu.VMEM(packed.shape, jnp.float32),
            pltpu.VMEM((slab_rows, d_model), jnp.float32),
            pltpu.VMEM((rows, d_model), jnp.float32),
            pltpu.VMEM((n_kv, rows, cols), jnp.float32),
            pltpu.SemaphoreType.DMA((n_tok,)),
            pltpu.SemaphoreType.DMA((n_tok,)),
            pltpu.SemaphoreType.DMA((n_kv,)),
            pltpu.SemaphoreType.DMA((n_kv,)),
            pltpu.SemaphoreType.DMA((2,)),
        ],
        compiler_params=pltpu.CompilerParams(collective_id=1, has_side_effects=True),
    )(packed, own, new, w_out)


def block_stats(query, keyval, live):
    width = query.shape[-1]
    keys = keyval[..., :width]
    values = keyval[..., width:]
    scores = jnp.einsum("rhge,hrpe->rhgp", query, keys, preferred_element_type=jnp.float32) * SCALE
    mask = live[:, None, None, :]
    scores = jnp.where(mask, scores, NEG)
    top = jnp.max(scores, axis=-1)
    weights = jnp.where(mask, jnp.exp(scores - top[..., None]), 0.0)
    total = jnp.sum(weights, axis=-1)
    numer = jnp.einsum(
        "rhgp,hrpe->rhge", weights.astype(jnp.bfloat16), values, preferred_element_type=jnp.float32
    )
    return (top, total, numer)


def prompt_stats(all_query, prefix_cache, req_group, pre_len, block):
    all_rows, heads, per_kv, width = all_query.shape
    groups = prefix_cache.shape[1]
    pre_dev = prefix_cache.shape[2]
    group_ids = jnp.arange(groups, dtype=jnp.int32)
    starts = jnp.sum((req_group[None, :] < group_ids[:, None]).astype(jnp.int32), axis=1)
    slot_ids = jnp.arange(SHARE, dtype=jnp.int32)
    source = jnp.minimum(starts[:, None] + slot_ids[None, :], all_rows - 1).reshape(-1)
    slotted = jnp.take(all_query, source, axis=0).reshape(groups, SHARE, heads, per_kv, width)
    keys = prefix_cache[..., :width]
    values = prefix_cache[..., width:]
    scores = (
        jnp.einsum("gshqe,hgpe->hgsqp", slotted, keys, preferred_element_type=jnp.float32) * SCALE
    )
    pre_pos = block * pre_dev + jnp.arange(pre_dev, dtype=jnp.int32)
    live = pre_pos[None, :] < pre_len[:, None]
    mask = live[None, :, None, None, :]
    scores = jnp.where(mask, scores, NEG)
    top = jnp.max(scores, axis=-1)
    weights = jnp.where(mask, jnp.exp(scores - top[..., None]), 0.0)
    total = jnp.sum(weights, axis=-1)
    numer = jnp.einsum(
        "hgsqp,hgpe->hgsqe",
        weights.astype(jnp.bfloat16),
        values,
        preferred_element_type=jnp.float32,
    )
    match = req_group[:, None] == group_ids[None, :]
    start_req = jnp.sum(jnp.where(match, starts[None, :], 0), axis=1)
    place = req_group * SHARE + jnp.arange(all_rows, dtype=jnp.int32) - start_req
    packed = jnp.concatenate(
        [numer, top[..., None], total[..., None],
         jnp.zeros(top.shape + (128 - width - 2,), jnp.float32)],
        axis=-1,
    ).reshape(heads, groups * SHARE, per_kv, 128)
    packed = jnp.take(packed, place, axis=1)
    return jnp.transpose(packed, (1, 0, 2, 3)).reshape(all_rows * heads * per_kv, 128)


def body(hidden_in, w_query, w_keyval, w_out, own_cache, prefix_cache, own_len, req_group, pre_len):
    rows = hidden_in.shape[0]
    heads = w_keyval.shape[1]
    width = w_keyval.shape[2] // 2
    per_kv = w_query.shape[1] // (heads * width)
    columns = heads * per_kv
    inputs = hidden_in.astype(jnp.float32)
    normed = (inputs * lax.rsqrt(jnp.mean(inputs * inputs, axis=1, keepdims=True) + 1e-05)).astype(
        jnp.bfloat16
    )
    query = jnp.dot(normed, w_query, preferred_element_type=jnp.float32).astype(jnp.bfloat16)
    newkv = jnp.einsum("rd,dhe->rhe", normed, w_keyval, preferred_element_type=jnp.float32).astype(
        jnp.bfloat16
    )
    n_tok = lax.axis_size("tok")
    n_kv = lax.axis_size("kv")
    q_slab = query.reshape(-1, 128)
    q16 = jnp.concatenate(
        [query.reshape(rows * columns, width), jnp.zeros((rows * columns, width), query.dtype)], axis=1
    )
    lens16 = jnp.repeat(own_len, columns).reshape(rows * columns, 1)
    gathered, own_block = broadcast_with_own(q_slab, q16, lens16, own_cache, n_tok, SCALE)
    gathered = gathered.reshape(n_tok * rows, -1)
    all_rows = gathered.shape[0]
    all_query = gathered.reshape(all_rows, heads, per_kv, width)
    block = lax.axis_index("tok")
    packed = prompt_stats(all_query, prefix_cache, req_group, pre_len, block)
    packed = packed.reshape(n_tok, -1, 128)
    local_query = query.reshape(rows, heads, per_kv, width)
    s_new = (
        jnp.einsum(
            "rhge,rhe->rhg", local_query, newkv[..., :width], preferred_element_type=jnp.float32
        )
        * SCALE
    )
    s_new = s_new.reshape(rows, columns)
    new_value = jnp.broadcast_to(
        newkv[:, :, None, width:].astype(jnp.float32), (rows, heads, per_kv, width)
    ).reshape(rows, columns, width)
    new_block = jnp.concatenate(
        [new_value, s_new[..., None], jnp.ones((rows, columns, 1), jnp.float32),
         jnp.zeros((rows, columns, 128 - width - 2), jnp.float32)],
        axis=-1,
    ).reshape(rows * columns, 128)
    return finish_kernel_call(packed, own_block, new_block, w_out, n_tok, n_kv)


def solution(mesh):
    in_specs = (
        P("tok", None),
        P(None, "kv"),
        P(None, "kv", None),
        P("kv", None),
        P("kv", "tok", None, None),
        P("kv", None, "tok", None),
        P("tok"),
        P(),
        P(),
    )
    out_specs = P("tok", "kv")
    return jax.shard_map(body, mesh=mesh, in_specs=in_specs, out_specs=out_specs, check_vma=False)
```

```python
import jax
import jax.numpy as jnp
from jax import lax
from jax.sharding import PartitionSpec as P
from jax.experimental import pallas as pl
from jax.experimental.pallas import tpu as pltpu

SHARE = 16


SCALE = 0.015625
NEG = -1e30


def exchange(slabs, axis, other, n, broadcast, cid):
    slab_shape = slabs.shape[1:] if not broadcast else slabs.shape
    mesh_id = pl.DeviceIdType.MESH

    def kernel(x_ref, out_ref, send_sems, recv_sems, local_sem):
        me = lax.axis_index(axis)
        keep = lax.axis_index(other)

        def dev(peer):
            return (peer, keep) if axis == "tok" else (keep, peer)

        def src(peer):
            return x_ref if broadcast else x_ref.at[peer]

        barrier = pltpu.get_barrier_semaphore()

        def greet(i, c):
            peer = lax.rem(me + i, n)
            pl.semaphore_signal(barrier, inc=1, device_id=dev(peer), device_id_type=mesh_id)
            return c

        lax.fori_loop(1, n, greet, 0)
        pl.semaphore_wait(barrier, n - 1)
        local = pltpu.make_async_copy(src(me), out_ref.at[me], local_sem)
        local.start()

        def send(i, c):
            peer = lax.rem(me + i, n)
            pltpu.make_async_remote_copy(
                src(peer), out_ref.at[me], send_sems.at[i], recv_sems.at[i],
                device_id=dev(peer), device_id_type=mesh_id,
            ).start()
            return c

        lax.fori_loop(1, n, send, 0)

        def finish(i, c):
            peer = lax.rem(me + i, n)
            origin = lax.rem(me + n - i, n)
            pltpu.make_async_remote_copy(
                src(peer), out_ref.at[me], send_sems.at[i], recv_sems.at[i],
                device_id=dev(peer), device_id_type=mesh_id,
            ).wait_send()
            pltpu.make_async_remote_copy(
                src(peer), out_ref.at[origin], send_sems.at[i], recv_sems.at[i],
                device_id=dev(origin), device_id_type=mesh_id,
            ).wait_recv()
            return c

        lax.fori_loop(1, n, finish, 0)
        local.wait()

    return pl.pallas_call(
        kernel,
        out_shape=jax.ShapeDtypeStruct((n,) + tuple(slab_shape), slabs.dtype),
        in_specs=[pl.BlockSpec(memory_space=pltpu.VMEM)],
        out_specs=pl.BlockSpec(memory_space=pltpu.VMEM),
        scratch_shapes=[
            pltpu.SemaphoreType.DMA((n,)),
            pltpu.SemaphoreType.DMA((n,)),
            pltpu.SemaphoreType.DMA(()),
        ],
        compiler_params=pltpu.CompilerParams(collective_id=cid, has_side_effects=True),
    )(slabs)


def broadcast_with_own(q_slab, q16, lens16, own_cache, n, scale):
    mesh_id = pl.DeviceIdType.MESH
    reqs, cap, lanes = own_cache.shape[1:]
    half = lanes // 2
    per = q16.shape[0] // reqs

    def kernel(x_ref, q_ref, len_ref, own_hbm, out_ref, own_out, own_vmem,
               send_sems, recv_sems, local_sem, own_sem):
        me = lax.axis_index("tok")
        keep = lax.axis_index("kv")
        own_copy = pltpu.make_async_copy(own_hbm.at[0], own_vmem, own_sem)
        own_copy.start()
        barrier = pltpu.get_barrier_semaphore()

        def greet(i, c):
            pl.semaphore_signal(barrier, inc=1, device_id=(lax.rem(me + i, n), keep), device_id_type=mesh_id)
            return c

        lax.fori_loop(1, n, greet, 0)
        pl.semaphore_wait(barrier, n - 1)
        local = pltpu.make_async_copy(x_ref, out_ref.at[me], local_sem)
        local.start()

        def send(i, c):
            peer = lax.rem(me + i, n)
            pltpu.make_async_remote_copy(
                x_ref, out_ref.at[me], send_sems.at[i], recv_sems.at[i],
                device_id=(peer, keep), device_id_type=mesh_id,
            ).start()
            return c

        lax.fori_loop(1, n, send, 0)
        own_copy.wait()
        q = q_ref[...]
        row = lax.broadcasted_iota(jnp.int32, (q.shape[0], cap), 0)
        pos = lax.broadcasted_iota(jnp.int32, (q.shape[0], cap), 1)
        scores = jnp.zeros((q.shape[0], cap), jnp.float32)
        for r in range(reqs):
            part = lax.dot_general(q, own_vmem[r], (((1,), (1,)), ((), ())),
                                   preferred_element_type=jnp.float32)
            scores = jnp.where(row // per == r, part, scores)
        scores = scores * scale
        live = pos < len_ref[...]
        scores = jnp.where(live, scores, NEG)
        top = jnp.max(scores, axis=1, keepdims=True)
        weights = jnp.where(live, jnp.exp(scores - top), 0.0)
        total = jnp.sum(weights, axis=1, keepdims=True)
        wb = weights.astype(jnp.bfloat16)
        acc = jnp.zeros((q.shape[0], lanes), jnp.float32)
        for r in range(reqs):
            acc = acc + jnp.dot(jnp.where(row // per == r, wb, jnp.zeros_like(wb)), own_vmem[r],
                                preferred_element_type=jnp.float32)
        numer = pltpu.roll(acc, half, 1)
        lane = lax.broadcasted_iota(jnp.int32, acc.shape, 1)
        alive = total > 0.0
        safe = jnp.where(alive, total, 1.0)
        level = jnp.where(alive, top + jnp.log(safe), NEG)
        own_out[...] = jnp.where(lane < half, jnp.where(alive, numer / safe, 0.0), level)

        def finish(i, c):
            peer = lax.rem(me + i, n)
            origin = lax.rem(me + n - i, n)
            pltpu.make_async_remote_copy(
                x_ref, out_ref.at[me], send_sems.at[i], recv_sems.at[i],
                device_id=(peer, keep), device_id_type=mesh_id,
            ).wait_send()
            pltpu.make_async_remote_copy(
                x_ref, out_ref.at[origin], send_sems.at[i], recv_sems.at[i],
                device_id=(origin, keep), device_id_type=mesh_id,
            ).wait_recv()
            return c

        lax.fori_loop(1, n, finish, 0)
        local.wait()

    return pl.pallas_call(
        kernel,
        out_shape=(
            jax.ShapeDtypeStruct((n,) + tuple(q_slab.shape), q_slab.dtype),
            jax.ShapeDtypeStruct((q16.shape[0], lanes), jnp.float32),
        ),
        in_specs=[pl.BlockSpec(memory_space=pltpu.VMEM)] * 3 + [pl.BlockSpec(memory_space=pl.ANY)],
        out_specs=(pl.BlockSpec(memory_space=pltpu.VMEM), pl.BlockSpec(memory_space=pltpu.VMEM)),
        scratch_shapes=[
            pltpu.VMEM((reqs, cap, lanes), own_cache.dtype),
            pltpu.SemaphoreType.DMA((n,)),
            pltpu.SemaphoreType.DMA((n,)),
            pltpu.SemaphoreType.DMA(()),
            pltpu.SemaphoreType.DMA(()),
        ],
        compiler_params=pltpu.CompilerParams(collective_id=0, has_side_effects=True),
    )(q_slab, q16, lens16, own_cache)


def finish_kernel_call(packed, own, new, w_out, n_tok, n_kv):
    slab_rows = packed.shape[1]
    rows = slab_rows // 4
    heads = 4
    width = 64
    d_model = w_out.shape[1]
    cols = d_model // n_kv
    mesh_id = pl.DeviceIdType.MESH

    def kernel(packed_ref, own_ref, new_ref, w_ref, out_ref, recv_scr, acc_scr, part_scr, kv_recv,
               tsend, trecv, ksend, krecv, loc_sems):
        me = lax.axis_index("tok")
        mk = lax.axis_index("kv")
        barrier = pltpu.get_barrier_semaphore()

        def greet_tok(i, c):
            pl.semaphore_signal(barrier, inc=1, device_id=(lax.rem(me + i, n_tok), mk), device_id_type=mesh_id)
            return c

        def greet_kv(i, c):
            pl.semaphore_signal(barrier, inc=1, device_id=(me, lax.rem(mk + i, n_kv)), device_id_type=mesh_id)
            return c

        lax.fori_loop(1, n_tok, greet_tok, 0)
        lax.fori_loop(1, n_kv, greet_kv, 0)
        pl.semaphore_wait(barrier, n_tok - 1 + n_kv - 1)

        local_copy = pltpu.make_async_copy(packed_ref.at[me], recv_scr.at[me], loc_sems.at[0])
        local_copy.start()

        def tok_copy(i, target, slot):
            return pltpu.make_async_remote_copy(
                packed_ref.at[target], recv_scr.at[slot], tsend.at[i], trecv.at[i],
                device_id=(target, mk), device_id_type=mesh_id,
            )

        def send_tok(i, c):
            tok_copy(i, lax.rem(me + i, n_tok), me).start()
            return c

        lax.fori_loop(1, n_tok, send_tok, 0)

        def finish_tok(i, c):
            tok_copy(i, lax.rem(me + i, n_tok), me).wait_send()
            origin = lax.rem(me + n_tok - i, n_tok)
            pltpu.make_async_remote_copy(
                packed_ref.at[origin], recv_scr.at[origin], tsend.at[i], trecv.at[i],
                device_id=(origin, mk), device_id_type=mesh_id,
            ).wait_recv()
            return c

        lax.fori_loop(1, n_tok, finish_tok, 0)
        local_copy.wait()

        x = recv_scr[...]
        loc = own_ref[...]
        nloc = new_ref[...]
        llane = lax.broadcasted_iota(jnp.int32, loc.shape, 1)
        big = jnp.maximum(jnp.maximum(jnp.max(x, axis=0), loc), nloc)
        keep_hi = llane >= width
        weight = jnp.where(keep_hi[None], jnp.exp(x - big[None]), 0.0)
        lweight = jnp.where(keep_hi, jnp.exp(loc - big), 0.0)
        nweight = jnp.where(keep_hi, jnp.exp(nloc - big), 0.0)
        weight = pltpu.roll(weight.reshape(-1, 128), width, 1).reshape(x.shape)
        lweight = pltpu.roll(lweight, width, 1)
        nweight = pltpu.roll(nweight, width, 1)
        denom = jnp.sum(weight, axis=0) + lweight + nweight
        numer = jnp.sum(weight * x, axis=0) + lweight * loc + nweight * nloc
        attn = jnp.where(llane < width, numer / jnp.where(llane < width, denom, 1.0), 0.0).astype(jnp.bfloat16)
        pi = lax.broadcasted_iota(jnp.int32, (slab_rows, slab_rows), 0)
        pj = lax.broadcasted_iota(jnp.int32, (slab_rows, slab_rows), 1)
        perm = jnp.where(pj == (pi % rows) * heads + pi // rows, 1.0, 0.0).astype(jnp.bfloat16)
        attn = jnp.dot(perm, attn, preferred_element_type=jnp.float32)
        shifted = pltpu.roll(attn, width, 1)
        row = lax.broadcasted_iota(jnp.int32, attn.shape, 0)
        head_of = row // rows
        acc = jnp.zeros((slab_rows, d_model), jnp.float32)
        for pair in range(heads // 2):
            lhs = jnp.where(head_of == 2 * pair, attn, jnp.where(head_of == 2 * pair + 1, shifted, 0.0))
            acc = acc + jnp.dot(
                lhs.astype(jnp.bfloat16), w_ref[pl.ds(pair * 2 * width, 2 * width), :],
                preferred_element_type=jnp.float32,
            )
        acc_scr[...] = acc
        partial = acc_scr[pl.ds(0, rows), :]
        for h in range(1, heads):
            partial = partial + acc_scr[pl.ds(h * rows, rows), :]
        part_scr[...] = partial

        def kv_src(target):
            return part_scr.at[:, pl.ds(pl.multiple_of(target * cols, cols), cols)]

        kv_local = pltpu.make_async_copy(kv_src(mk), kv_recv.at[mk], loc_sems.at[1])
        kv_local.start()

        def kv_copy(j, target, slot):
            return pltpu.make_async_remote_copy(
                kv_src(target), kv_recv.at[slot], ksend.at[j], krecv.at[j],
                device_id=(me, target), device_id_type=mesh_id,
            )

        def send_kv(j, c):
            kv_copy(j, lax.rem(mk + j, n_kv), mk).start()
            return c

        lax.fori_loop(1, n_kv, send_kv, 0)

        def finish_kv(j, c):
            kv_copy(j, lax.rem(mk + j, n_kv), mk).wait_send()
            origin = lax.rem(mk + n_kv - j, n_kv)
            pltpu.make_async_remote_copy(
                kv_src(origin), kv_recv.at[origin], ksend.at[j], krecv.at[j],
                device_id=(me, origin), device_id_type=mesh_id,
            ).wait_recv()
            return c

        lax.fori_loop(1, n_kv, finish_kv, 0)
        kv_local.wait()
        out_ref[...] = jnp.sum(kv_recv[...], axis=0).astype(out_ref.dtype)

    return pl.pallas_call(
        kernel,
        out_shape=jax.ShapeDtypeStruct((rows, cols), jnp.bfloat16),
        in_specs=[pl.BlockSpec(memory_space=pltpu.VMEM)] * 4,
        out_specs=pl.BlockSpec(memory_space=pltpu.VMEM),
        scratch_shapes=[
            pltpu.VMEM(packed.shape, jnp.float32),
            pltpu.VMEM((slab_rows, d_model), jnp.float32),
            pltpu.VMEM((rows, d_model), jnp.float32),
            pltpu.VMEM((n_kv, rows, cols), jnp.float32),
            pltpu.SemaphoreType.DMA((n_tok,)),
            pltpu.SemaphoreType.DMA((n_tok,)),
            pltpu.SemaphoreType.DMA((n_kv,)),
            pltpu.SemaphoreType.DMA((n_kv,)),
            pltpu.SemaphoreType.DMA((2,)),
        ],
        compiler_params=pltpu.CompilerParams(collective_id=1, has_side_effects=True),
    )(packed, own, new, w_out)


def block_stats(query, keyval, live):
    width = query.shape[-1]
    keys = keyval[..., :width]
    values = keyval[..., width:]
    scores = jnp.einsum("rhge,hrpe->rhgp", query, keys, preferred_element_type=jnp.float32) * SCALE
    mask = live[:, None, None, :]
    scores = jnp.where(mask, scores, NEG)
    top = jnp.max(scores, axis=-1)
    weights = jnp.where(mask, jnp.exp(scores - top[..., None]), 0.0)
    total = jnp.sum(weights, axis=-1)
    numer = jnp.einsum(
        "rhgp,hrpe->rhge", weights.astype(jnp.bfloat16), values, preferred_element_type=jnp.float32
    )
    return (top, total, numer)


def prompt_stats(all_query, prefix_cache, req_group, pre_len, block):
    all_rows, heads, per_kv, width = all_query.shape
    groups = prefix_cache.shape[1]
    pre_dev = prefix_cache.shape[2]
    group_ids = jnp.arange(groups, dtype=jnp.int32)
    starts = jnp.sum((req_group[None, :] < group_ids[:, None]).astype(jnp.int32), axis=1)
    slot_ids = jnp.arange(SHARE, dtype=jnp.int32)
    source = jnp.minimum(starts[:, None] + slot_ids[None, :], all_rows - 1).reshape(-1)
    slotted = jnp.take(all_query, source, axis=0).reshape(groups, SHARE, heads, per_kv, width)
    keys = prefix_cache[..., :width]
    values = prefix_cache[..., width:]
    scores = (
        jnp.einsum("gshqe,hgpe->hgsqp", slotted, keys, preferred_element_type=jnp.float32) * SCALE
    )
    pre_pos = block * pre_dev + jnp.arange(pre_dev, dtype=jnp.int32)
    live = pre_pos[None, :] < pre_len[:, None]
    mask = live[None, :, None, None, :]
    scores = jnp.where(mask, scores, NEG)
    top = jnp.max(scores, axis=-1)
    weights = jnp.where(mask, jnp.exp(scores - top[..., None]), 0.0)
    total = jnp.sum(weights, axis=-1)
    numer = jnp.einsum(
        "hgsqp,hgpe->hgsqe",
        weights.astype(jnp.bfloat16),
        values,
        preferred_element_type=jnp.float32,
    )
    match = req_group[:, None] == group_ids[None, :]
    start_req = jnp.sum(jnp.where(match, starts[None, :], 0), axis=1)
    place = req_group * SHARE + jnp.arange(all_rows, dtype=jnp.int32) - start_req
    alive = total > 0.0
    safe = jnp.where(alive, total, 1.0)
    level = jnp.where(alive, top + jnp.log(safe), NEG)
    packed = jnp.concatenate(
        [jnp.where(alive[..., None], numer / safe[..., None], 0.0),
         jnp.broadcast_to(level[..., None], top.shape + (128 - width,))],
        axis=-1,
    ).reshape(heads, groups * SHARE, per_kv, 128)
    packed = jnp.take(packed, place, axis=1)
    return jnp.transpose(packed, (1, 0, 2, 3)).reshape(all_rows * heads * per_kv, 128)


def body(hidden_in, w_query, w_keyval, w_out, own_cache, prefix_cache, own_len, req_group, pre_len):
    rows = hidden_in.shape[0]
    heads = w_keyval.shape[1]
    width = w_keyval.shape[2] // 2
    per_kv = w_query.shape[1] // (heads * width)
    columns = heads * per_kv
    inputs = hidden_in.astype(jnp.float32)
    normed = (inputs * lax.rsqrt(jnp.mean(inputs * inputs, axis=1, keepdims=True) + 1e-05)).astype(
        jnp.bfloat16
    )
    query = jnp.dot(normed, w_query, preferred_element_type=jnp.float32).astype(jnp.bfloat16)
    newkv = jnp.einsum("rd,dhe->rhe", normed, w_keyval, preferred_element_type=jnp.float32).astype(
        jnp.bfloat16
    )
    n_tok = lax.axis_size("tok")
    n_kv = lax.axis_size("kv")
    q_slab = query.reshape(-1, 128)
    q16 = jnp.concatenate(
        [query.reshape(rows * columns, width), jnp.zeros((rows * columns, width), query.dtype)], axis=1
    )
    lens16 = jnp.repeat(own_len, columns).reshape(rows * columns, 1)
    gathered, own_block = broadcast_with_own(q_slab, q16, lens16, own_cache, n_tok, SCALE)
    gathered = gathered.reshape(n_tok * rows, -1)
    all_rows = gathered.shape[0]
    all_query = gathered.reshape(all_rows, heads, per_kv, width)
    block = lax.axis_index("tok")
    packed = prompt_stats(all_query, prefix_cache, req_group, pre_len, block)
    packed = packed.reshape(n_tok, -1, 128)
    local_query = query.reshape(rows, heads, per_kv, width)
    s_new = (
        jnp.einsum(
            "rhge,rhe->rhg", local_query, newkv[..., :width], preferred_element_type=jnp.float32
        )
        * SCALE
    )
    s_new = s_new.reshape(rows, columns)
    new_value = jnp.broadcast_to(
        newkv[:, :, None, width:].astype(jnp.float32), (rows, heads, per_kv, width)
    ).reshape(rows, columns, width)
    new_block = jnp.concatenate(
        [new_value, jnp.broadcast_to(s_new[..., None], (rows, columns, 128 - width))],
        axis=-1,
    ).reshape(rows * columns, 128)
    return finish_kernel_call(packed, own_block, new_block, w_out, n_tok, n_kv)


def solution(mesh):
    in_specs = (
        P("tok", None),
        P(None, "kv"),
        P(None, "kv", None),
        P("kv", None),
        P("kv", "tok", None, None),
        P("kv", None, "tok", None),
        P("tok"),
        P(),
        P(),
    )
    out_specs = P("tok", "kv")
    return jax.shard_map(body, mesh=mesh, in_specs=in_specs, out_specs=out_specs, check_vma=False)
```

```python
import jax
import jax.numpy as jnp
from jax import lax
from jax.sharding import PartitionSpec as P
from jax.experimental import pallas as pl
from jax.experimental.pallas import tpu as pltpu

SHARE = 16


SCALE = 0.015625
NEG = -1e30


def exchange(slabs, axis, other, n, broadcast, cid):
    slab_shape = slabs.shape[1:] if not broadcast else slabs.shape
    mesh_id = pl.DeviceIdType.MESH

    def kernel(x_ref, out_ref, send_sems, recv_sems, local_sem):
        me = lax.axis_index(axis)
        keep = lax.axis_index(other)

        def dev(peer):
            return (peer, keep) if axis == "tok" else (keep, peer)

        def src(peer):
            return x_ref if broadcast else x_ref.at[peer]

        barrier = pltpu.get_barrier_semaphore()

        def greet(i, c):
            peer = lax.rem(me + i, n)
            pl.semaphore_signal(barrier, inc=1, device_id=dev(peer), device_id_type=mesh_id)
            return c

        lax.fori_loop(1, n, greet, 0)
        pl.semaphore_wait(barrier, n - 1)
        local = pltpu.make_async_copy(src(me), out_ref.at[me], local_sem)
        local.start()

        def send(i, c):
            peer = lax.rem(me + i, n)
            pltpu.make_async_remote_copy(
                src(peer), out_ref.at[me], send_sems.at[i], recv_sems.at[i],
                device_id=dev(peer), device_id_type=mesh_id,
            ).start()
            return c

        lax.fori_loop(1, n, send, 0)

        def finish(i, c):
            peer = lax.rem(me + i, n)
            origin = lax.rem(me + n - i, n)
            pltpu.make_async_remote_copy(
                src(peer), out_ref.at[me], send_sems.at[i], recv_sems.at[i],
                device_id=dev(peer), device_id_type=mesh_id,
            ).wait_send()
            pltpu.make_async_remote_copy(
                src(peer), out_ref.at[origin], send_sems.at[i], recv_sems.at[i],
                device_id=dev(origin), device_id_type=mesh_id,
            ).wait_recv()
            return c

        lax.fori_loop(1, n, finish, 0)
        local.wait()

    return pl.pallas_call(
        kernel,
        out_shape=jax.ShapeDtypeStruct((n,) + tuple(slab_shape), slabs.dtype),
        in_specs=[pl.BlockSpec(memory_space=pltpu.VMEM)],
        out_specs=pl.BlockSpec(memory_space=pltpu.VMEM),
        scratch_shapes=[
            pltpu.SemaphoreType.DMA((n,)),
            pltpu.SemaphoreType.DMA((n,)),
            pltpu.SemaphoreType.DMA(()),
        ],
        compiler_params=pltpu.CompilerParams(collective_id=cid, has_side_effects=True),
    )(slabs)


def broadcast_with_own(q_slab, q16, lens16, own_cache, n, scale):
    mesh_id = pl.DeviceIdType.MESH
    reqs, cap, lanes = own_cache.shape[1:]
    half = lanes // 2
    per = q16.shape[0] // reqs

    def kernel(x_ref, q_ref, len_ref, own_hbm, out_ref, own_out, own_vmem,
               send_sems, recv_sems, local_sem, own_sem):
        me = lax.axis_index("tok")
        keep = lax.axis_index("kv")
        own_copy = pltpu.make_async_copy(own_hbm.at[0], own_vmem, own_sem)
        own_copy.start()
        barrier = pltpu.get_barrier_semaphore()

        def greet(i, c):
            pl.semaphore_signal(barrier, inc=1, device_id=(lax.rem(me + i, n), keep), device_id_type=mesh_id)
            return c

        lax.fori_loop(1, n, greet, 0)
        pl.semaphore_wait(barrier, n - 1)
        local = pltpu.make_async_copy(x_ref, out_ref.at[me], local_sem)
        local.start()

        def send(i, c):
            peer = lax.rem(me + i, n)
            pltpu.make_async_remote_copy(
                x_ref, out_ref.at[me], send_sems.at[i], recv_sems.at[i],
                device_id=(peer, keep), device_id_type=mesh_id,
            ).start()
            return c

        lax.fori_loop(1, n, send, 0)
        own_copy.wait()
        q = q_ref[...]
        row = lax.broadcasted_iota(jnp.int32, (q.shape[0], cap), 0)
        pos = lax.broadcasted_iota(jnp.int32, (q.shape[0], cap), 1)
        scores = jnp.zeros((q.shape[0], cap), jnp.float32)
        for r in range(reqs):
            part = lax.dot_general(q, own_vmem[r], (((1,), (1,)), ((), ())),
                                   preferred_element_type=jnp.float32)
            scores = jnp.where(row // per == r, part, scores)
        scores = scores * scale
        live = pos < len_ref[...]
        scores = jnp.where(live, scores, NEG)
        top = jnp.max(scores, axis=1, keepdims=True)
        weights = jnp.where(live, jnp.exp(scores - top), 0.0)
        total = jnp.sum(weights, axis=1, keepdims=True)
        wb = weights.astype(jnp.bfloat16)
        acc = jnp.zeros((q.shape[0], lanes), jnp.float32)
        for r in range(reqs):
            acc = acc + jnp.dot(jnp.where(row // per == r, wb, jnp.zeros_like(wb)), own_vmem[r],
                                preferred_element_type=jnp.float32)
        numer = pltpu.roll(acc, half, 1)
        lane = lax.broadcasted_iota(jnp.int32, acc.shape, 1)
        alive = total > 0.0
        safe = jnp.where(alive, total, 1.0)
        level = jnp.where(alive, top + jnp.log(safe), NEG)
        own_out[...] = jnp.where(lane < half, jnp.where(alive, numer / safe, 0.0), level)

        def finish(i, c):
            peer = lax.rem(me + i, n)
            origin = lax.rem(me + n - i, n)
            pltpu.make_async_remote_copy(
                x_ref, out_ref.at[me], send_sems.at[i], recv_sems.at[i],
                device_id=(peer, keep), device_id_type=mesh_id,
            ).wait_send()
            pltpu.make_async_remote_copy(
                x_ref, out_ref.at[origin], send_sems.at[i], recv_sems.at[i],
                device_id=(origin, keep), device_id_type=mesh_id,
            ).wait_recv()
            return c

        lax.fori_loop(1, n, finish, 0)
        local.wait()

    return pl.pallas_call(
        kernel,
        out_shape=(
            jax.ShapeDtypeStruct((n,) + tuple(q_slab.shape), q_slab.dtype),
            jax.ShapeDtypeStruct((q16.shape[0], lanes), jnp.float32),
        ),
        in_specs=[pl.BlockSpec(memory_space=pltpu.VMEM)] * 3 + [pl.BlockSpec(memory_space=pl.ANY)],
        out_specs=(pl.BlockSpec(memory_space=pltpu.VMEM), pl.BlockSpec(memory_space=pltpu.VMEM)),
        scratch_shapes=[
            pltpu.VMEM((reqs, cap, lanes), own_cache.dtype),
            pltpu.SemaphoreType.DMA((n,)),
            pltpu.SemaphoreType.DMA((n,)),
            pltpu.SemaphoreType.DMA(()),
            pltpu.SemaphoreType.DMA(()),
        ],
        compiler_params=pltpu.CompilerParams(collective_id=0, has_side_effects=True),
    )(q_slab, q16, lens16, own_cache)


def finish_kernel_call(qrows, prefix, base, req_group, jrow, pre_len, own, new, w_out, n_tok, n_kv):
    slab_rows = 16
    rows = slab_rows // 4
    groups, pre_dev, kv_lanes = prefix.shape
    window = 16 * 8
    heads = 4
    width = 64
    d_model = w_out.shape[1]
    cols = d_model // n_kv
    mesh_id = pl.DeviceIdType.MESH

    def kernel(q_ref, pre_ref, base_ref, rg_ref, j_ref, len_ref, own_ref, new_ref, w_ref, out_ref,
               recv_scr, acc_scr, part_scr, kv_recv, res_scr, packed_ref,
               tsend, trecv, ksend, krecv, loc_sems):
        me = lax.axis_index("tok")
        mk = lax.axis_index("kv")
        barrier = pltpu.get_barrier_semaphore()

        def greet_tok(i, c):
            pl.semaphore_signal(barrier, inc=1, device_id=(lax.rem(me + i, n_tok), mk), device_id_type=mesh_id)
            return c

        def greet_kv(i, c):
            pl.semaphore_signal(barrier, inc=1, device_id=(me, lax.rem(mk + i, n_kv)), device_id_type=mesh_id)
            return c

        lax.fori_loop(1, n_tok, greet_tok, 0)
        lax.fori_loop(1, n_kv, greet_kv, 0)

        glane = lax.broadcasted_iota(jnp.int32, (window, pre_dev), 1) + me * pre_dev
        olane = lax.broadcasted_iota(jnp.int32, (window, kv_lanes), 1)
        for g in range(groups):
            first = base_ref[g]
            qb = jnp.concatenate([q_ref[first + k] for k in range(window // 8)], axis=0)
            qb = qb.astype(jnp.bfloat16)
            kv = pre_ref[g]
            s = lax.dot_general(qb, kv, (((1,), (1,)), ((), ())), preferred_element_type=jnp.float32)
            s = s * SCALE
            live = glane < len_ref[g]
            s = jnp.where(live, s, NEG)
            top = jnp.max(s, axis=1, keepdims=True)
            e = jnp.where(live, jnp.exp(s - top), 0.0)
            total = jnp.sum(e, axis=1, keepdims=True)
            nm = jnp.dot(e.astype(jnp.bfloat16), kv, preferred_element_type=jnp.float32)
            nm = pltpu.roll(nm, width, 1)
            alive = total > 0.0
            safe = jnp.where(alive, total, 1.0)
            level = jnp.where(alive, top + jnp.log(safe), NEG)
            res_scr[pl.ds(g * (window // 8), window // 8)] = jnp.where(
                olane < width, jnp.where(alive, nm / safe, 0.0), level).reshape(window // 8, 8, kv_lanes)

        prow = lax.broadcasted_iota(jnp.int32, (8, kv_lanes), 0)

        def place(m, c):
            blocks = []
            for t in range(2):
                r = 2 * m + t
                blocks.append(res_scr[rg_ref[r] * (window // 8) + j_ref[r]])
            both = jnp.where(prow < 4, blocks[0], pltpu.roll(blocks[1], 4, 0))
            packed_ref[m // 2, pl.ds(pl.multiple_of((m % 2) * 8, 8), 8), :] = both
            return c

        lax.fori_loop(0, n_tok * 2, place, 0)
        pl.semaphore_wait(barrier, n_tok - 1 + n_kv - 1)

        local_copy = pltpu.make_async_copy(packed_ref.at[me], recv_scr.at[me], loc_sems.at[0])
        local_copy.start()

        def tok_copy(i, target, slot):
            return pltpu.make_async_remote_copy(
                packed_ref.at[target], recv_scr.at[slot], tsend.at[i], trecv.at[i],
                device_id=(target, mk), device_id_type=mesh_id,
            )

        def send_tok(i, c):
            tok_copy(i, lax.rem(me + i, n_tok), me).start()
            return c

        lax.fori_loop(1, n_tok, send_tok, 0)

        def finish_tok(i, c):
            tok_copy(i, lax.rem(me + i, n_tok), me).wait_send()
            origin = lax.rem(me + n_tok - i, n_tok)
            pltpu.make_async_remote_copy(
                packed_ref.at[origin], recv_scr.at[origin], tsend.at[i], trecv.at[i],
                device_id=(origin, mk), device_id_type=mesh_id,
            ).wait_recv()
            return c

        lax.fori_loop(1, n_tok, finish_tok, 0)
        local_copy.wait()

        x = recv_scr[...]
        loc = own_ref[...]
        nloc = new_ref[...]
        llane = lax.broadcasted_iota(jnp.int32, loc.shape, 1)
        big = jnp.maximum(jnp.maximum(jnp.max(x, axis=0), loc), nloc)
        keep_hi = llane >= width
        weight = jnp.where(keep_hi[None], jnp.exp(x - big[None]), 0.0)
        lweight = jnp.where(keep_hi, jnp.exp(loc - big), 0.0)
        nweight = jnp.where(keep_hi, jnp.exp(nloc - big), 0.0)
        weight = pltpu.roll(weight.reshape(-1, 128), width, 1).reshape(x.shape)
        lweight = pltpu.roll(lweight, width, 1)
        nweight = pltpu.roll(nweight, width, 1)
        denom = jnp.sum(weight, axis=0) + lweight + nweight
        numer = jnp.sum(weight * x, axis=0) + lweight * loc + nweight * nloc
        attn = jnp.where(llane < width, numer / jnp.where(llane < width, denom, 1.0), 0.0).astype(jnp.bfloat16)
        pi = lax.broadcasted_iota(jnp.int32, (slab_rows, slab_rows), 0)
        pj = lax.broadcasted_iota(jnp.int32, (slab_rows, slab_rows), 1)
        perm = jnp.where(pj == (pi % rows) * heads + pi // rows, 1.0, 0.0).astype(jnp.bfloat16)
        attn = jnp.dot(perm, attn, preferred_element_type=jnp.float32)
        shifted = pltpu.roll(attn, width, 1)
        row = lax.broadcasted_iota(jnp.int32, attn.shape, 0)
        head_of = row // rows
        acc = jnp.zeros((slab_rows, d_model), jnp.float32)
        for pair in range(heads // 2):
            lhs = jnp.where(head_of == 2 * pair, attn, jnp.where(head_of == 2 * pair + 1, shifted, 0.0))
            acc = acc + jnp.dot(
                lhs.astype(jnp.bfloat16), w_ref[pl.ds(pair * 2 * width, 2 * width), :],
                preferred_element_type=jnp.float32,
            )
        acc_scr[...] = acc
        partial = acc_scr[pl.ds(0, rows), :]
        for h in range(1, heads):
            partial = partial + acc_scr[pl.ds(h * rows, rows), :]
        part_scr[...] = partial

        def kv_src(target):
            return part_scr.at[:, pl.ds(pl.multiple_of(target * cols, cols), cols)]

        kv_local = pltpu.make_async_copy(kv_src(mk), kv_recv.at[mk], loc_sems.at[1])
        kv_local.start()

        def kv_copy(j, target, slot):
            return pltpu.make_async_remote_copy(
                kv_src(target), kv_recv.at[slot], ksend.at[j], krecv.at[j],
                device_id=(me, target), device_id_type=mesh_id,
            )

        def send_kv(j, c):
            kv_copy(j, lax.rem(mk + j, n_kv), mk).start()
            return c

        lax.fori_loop(1, n_kv, send_kv, 0)

        def finish_kv(j, c):
            kv_copy(j, lax.rem(mk + j, n_kv), mk).wait_send()
            origin = lax.rem(mk + n_kv - j, n_kv)
            pltpu.make_async_remote_copy(
                kv_src(origin), kv_recv.at[origin], ksend.at[j], krecv.at[j],
                device_id=(me, origin), device_id_type=mesh_id,
            ).wait_recv()
            return c

        lax.fori_loop(1, n_kv, finish_kv, 0)
        kv_local.wait()
        out_ref[...] = jnp.sum(kv_recv[...], axis=0).astype(out_ref.dtype)

    return pl.pallas_call(
        kernel,
        out_shape=jax.ShapeDtypeStruct((rows, cols), jnp.bfloat16),
        in_specs=[pl.BlockSpec(memory_space=pltpu.VMEM)] * 2
        + [pl.BlockSpec(memory_space=pltpu.SMEM)] * 4
        + [pl.BlockSpec(memory_space=pltpu.VMEM)] * 3,
        out_specs=pl.BlockSpec(memory_space=pltpu.VMEM),
        scratch_shapes=[
            pltpu.VMEM((n_tok, slab_rows, 128), jnp.float32),
            pltpu.VMEM((slab_rows, d_model), jnp.float32),
            pltpu.VMEM((rows, d_model), jnp.float32),
            pltpu.VMEM((n_kv, rows, cols), jnp.float32),
            pltpu.VMEM((groups * (window // 8), 8, 128), jnp.float32),
            pltpu.VMEM((n_tok, slab_rows, 128), jnp.float32),
            pltpu.SemaphoreType.DMA((n_tok,)),
            pltpu.SemaphoreType.DMA((n_tok,)),
            pltpu.SemaphoreType.DMA((n_kv,)),
            pltpu.SemaphoreType.DMA((n_kv,)),
            pltpu.SemaphoreType.DMA((2,)),
        ],
        compiler_params=pltpu.CompilerParams(collective_id=1, has_side_effects=True),
    )(qrows, prefix, base, req_group, jrow, pre_len, own, new, w_out)


def block_stats(query, keyval, live):
    width = query.shape[-1]
    keys = keyval[..., :width]
    values = keyval[..., width:]
    scores = jnp.einsum("rhge,hrpe->rhgp", query, keys, preferred_element_type=jnp.float32) * SCALE
    mask = live[:, None, None, :]
    scores = jnp.where(mask, scores, NEG)
    top = jnp.max(scores, axis=-1)
    weights = jnp.where(mask, jnp.exp(scores - top[..., None]), 0.0)
    total = jnp.sum(weights, axis=-1)
    numer = jnp.einsum(
        "rhgp,hrpe->rhge", weights.astype(jnp.bfloat16), values, preferred_element_type=jnp.float32
    )
    return (top, total, numer)


def prompt_stats(all_query, prefix_cache, req_group, pre_len, block):
    all_rows, heads, per_kv, width = all_query.shape
    groups = prefix_cache.shape[1]
    pre_dev = prefix_cache.shape[2]
    group_ids = jnp.arange(groups, dtype=jnp.int32)
    starts = jnp.sum((req_group[None, :] < group_ids[:, None]).astype(jnp.int32), axis=1)
    slot_ids = jnp.arange(SHARE, dtype=jnp.int32)
    source = jnp.minimum(starts[:, None] + slot_ids[None, :], all_rows - 1).reshape(-1)
    slotted = jnp.take(all_query, source, axis=0).reshape(groups, SHARE, heads, per_kv, width)
    keys = prefix_cache[..., :width]
    values = prefix_cache[..., width:]
    scores = (
        jnp.einsum("gshqe,hgpe->hgsqp", slotted, keys, preferred_element_type=jnp.float32) * SCALE
    )
    pre_pos = block * pre_dev + jnp.arange(pre_dev, dtype=jnp.int32)
    live = pre_pos[None, :] < pre_len[:, None]
    mask = live[None, :, None, None, :]
    scores = jnp.where(mask, scores, NEG)
    top = jnp.max(scores, axis=-1)
    weights = jnp.where(mask, jnp.exp(scores - top[..., None]), 0.0)
    total = jnp.sum(weights, axis=-1)
    numer = jnp.einsum(
        "hgsqp,hgpe->hgsqe",
        weights.astype(jnp.bfloat16),
        values,
        preferred_element_type=jnp.float32,
    )
    match = req_group[:, None] == group_ids[None, :]
    start_req = jnp.sum(jnp.where(match, starts[None, :], 0), axis=1)
    place = req_group * SHARE + jnp.arange(all_rows, dtype=jnp.int32) - start_req
    alive = total > 0.0
    safe = jnp.where(alive, total, 1.0)
    level = jnp.where(alive, top + jnp.log(safe), NEG)
    packed = jnp.concatenate(
        [jnp.where(alive[..., None], numer / safe[..., None], 0.0),
         jnp.broadcast_to(level[..., None], top.shape + (128 - width,))],
        axis=-1,
    ).reshape(heads, groups * SHARE, per_kv, 128)
    packed = jnp.take(packed, place, axis=1)
    return jnp.transpose(packed, (1, 0, 2, 3)).reshape(all_rows * heads * per_kv, 128)


def body(hidden_in, w_query, w_keyval, w_out, own_cache, prefix_cache, own_len, req_group, pre_len):
    rows = hidden_in.shape[0]
    heads = w_keyval.shape[1]
    width = w_keyval.shape[2] // 2
    per_kv = w_query.shape[1] // (heads * width)
    columns = heads * per_kv
    inputs = hidden_in.astype(jnp.float32)
    normed = (inputs * lax.rsqrt(jnp.mean(inputs * inputs, axis=1, keepdims=True) + 1e-05)).astype(
        jnp.bfloat16
    )
    query = jnp.dot(normed, w_query, preferred_element_type=jnp.float32).astype(jnp.bfloat16)
    newkv = jnp.einsum("rd,dhe->rhe", normed, w_keyval, preferred_element_type=jnp.float32).astype(
        jnp.bfloat16
    )
    n_tok = lax.axis_size("tok")
    n_kv = lax.axis_size("kv")
    q_slab = query.reshape(-1, 128)
    q16 = jnp.concatenate(
        [query.reshape(rows * columns, width), jnp.zeros((rows * columns, width), query.dtype)], axis=1
    )
    lens16 = jnp.repeat(own_len, columns).reshape(rows * columns, 1)
    gathered, own_block = broadcast_with_own(q_slab, q16, lens16, own_cache, n_tok, SCALE)
    gathered = gathered.reshape(n_tok * rows, -1)
    all_rows = gathered.shape[0]
    qrows = jnp.concatenate(
        [gathered.reshape(all_rows, columns, width).astype(jnp.float32),
         jnp.zeros((all_rows, columns, 128 - width), jnp.float32)], axis=2)
    qrows = jnp.concatenate([qrows, jnp.zeros((all_rows, 8 - columns, 128), jnp.float32)], axis=1)
    groups = prefix_cache.shape[1]
    group_ids = jnp.arange(groups, dtype=jnp.int32)
    starts = jnp.sum((req_group[None, :] < group_ids[:, None]).astype(jnp.int32), axis=1)
    base = jnp.minimum(starts, all_rows - SHARE)
    rg = jnp.clip(req_group, 0, groups - 1)
    jrow = jnp.clip(jnp.arange(all_rows, dtype=jnp.int32) - jnp.take(base, rg), 0, SHARE - 1)
    local_query = query.reshape(rows, heads, per_kv, width)
    s_new = (
        jnp.einsum(
            "rhge,rhe->rhg", local_query, newkv[..., :width], preferred_element_type=jnp.float32
        )
        * SCALE
    )
    s_new = s_new.reshape(rows, columns)
    new_value = jnp.broadcast_to(
        newkv[:, :, None, width:].astype(jnp.float32), (rows, heads, per_kv, width)
    ).reshape(rows, columns, width)
    new_block = jnp.concatenate(
        [new_value, jnp.broadcast_to(s_new[..., None], (rows, columns, 128 - width))],
        axis=-1,
    ).reshape(rows * columns, 128)
    return finish_kernel_call(qrows, prefix_cache[0], base, rg, jrow, pre_len, own_block, new_block, w_out, n_tok, n_kv)


def solution(mesh):
    in_specs = (
        P("tok", None),
        P(None, "kv"),
        P(None, "kv", None),
        P("kv", None),
        P("kv", "tok", None, None),
        P("kv", None, "tok", None),
        P("tok"),
        P(),
        P(),
    )
    out_specs = P("tok", "kv")
    return jax.shard_map(body, mesh=mesh, in_specs=in_specs, out_specs=out_specs, check_vma=False)
```

```python
import jax
import jax.numpy as jnp
from jax import lax
from jax.sharding import PartitionSpec as P
from jax.experimental import pallas as pl
from jax.experimental.pallas import tpu as pltpu

SHARE = 16


SCALE = 0.015625
NEG = -1e30


def exchange(slabs, axis, other, n, broadcast, cid):
    slab_shape = slabs.shape[1:] if not broadcast else slabs.shape
    mesh_id = pl.DeviceIdType.MESH

    def kernel(x_ref, out_ref, send_sems, recv_sems, local_sem):
        me = lax.axis_index(axis)
        keep = lax.axis_index(other)

        def dev(peer):
            return (peer, keep) if axis == "tok" else (keep, peer)

        def src(peer):
            return x_ref if broadcast else x_ref.at[peer]

        barrier = pltpu.get_barrier_semaphore()

        def greet(i, c):
            peer = lax.rem(me + i, n)
            pl.semaphore_signal(barrier, inc=1, device_id=dev(peer), device_id_type=mesh_id)
            return c

        lax.fori_loop(1, n, greet, 0)
        pl.semaphore_wait(barrier, n - 1)
        local = pltpu.make_async_copy(src(me), out_ref.at[me], local_sem)
        local.start()

        def send(i, c):
            peer = lax.rem(me + i, n)
            pltpu.make_async_remote_copy(
                src(peer), out_ref.at[me], send_sems.at[i], recv_sems.at[i],
                device_id=dev(peer), device_id_type=mesh_id,
            ).start()
            return c

        lax.fori_loop(1, n, send, 0)

        def finish(i, c):
            peer = lax.rem(me + i, n)
            origin = lax.rem(me + n - i, n)
            pltpu.make_async_remote_copy(
                src(peer), out_ref.at[me], send_sems.at[i], recv_sems.at[i],
                device_id=dev(peer), device_id_type=mesh_id,
            ).wait_send()
            pltpu.make_async_remote_copy(
                src(peer), out_ref.at[origin], send_sems.at[i], recv_sems.at[i],
                device_id=dev(origin), device_id_type=mesh_id,
            ).wait_recv()
            return c

        lax.fori_loop(1, n, finish, 0)
        local.wait()

    return pl.pallas_call(
        kernel,
        out_shape=jax.ShapeDtypeStruct((n,) + tuple(slab_shape), slabs.dtype),
        in_specs=[pl.BlockSpec(memory_space=pltpu.VMEM)],
        out_specs=pl.BlockSpec(memory_space=pltpu.VMEM),
        scratch_shapes=[
            pltpu.SemaphoreType.DMA((n,)),
            pltpu.SemaphoreType.DMA((n,)),
            pltpu.SemaphoreType.DMA(()),
        ],
        compiler_params=pltpu.CompilerParams(collective_id=cid, has_side_effects=True),
    )(slabs)


def broadcast_with_own(q_slab, q16, lens16, own_cache, n, scale):
    mesh_id = pl.DeviceIdType.MESH
    reqs, cap, lanes = own_cache.shape[1:]
    half = lanes // 2
    per = q16.shape[0] // reqs

    def kernel(x_ref, q_ref, len_ref, own_hbm, out_ref, own_out, own_vmem,
               send_sems, recv_sems, local_sem, own_sem):
        me = lax.axis_index("tok")
        keep = lax.axis_index("kv")
        own_copy = pltpu.make_async_copy(own_hbm.at[0], own_vmem, own_sem)
        own_copy.start()
        barrier = pltpu.get_barrier_semaphore()

        def greet(i, c):
            pl.semaphore_signal(barrier, inc=1, device_id=(lax.rem(me + i, n), keep), device_id_type=mesh_id)
            return c

        lax.fori_loop(1, n, greet, 0)
        pl.semaphore_wait(barrier, n - 1)
        local = pltpu.make_async_copy(x_ref, out_ref.at[me], local_sem)
        local.start()

        def send(i, c):
            peer = lax.rem(me + i, n)
            pltpu.make_async_remote_copy(
                x_ref, out_ref.at[me], send_sems.at[i], recv_sems.at[i],
                device_id=(peer, keep), device_id_type=mesh_id,
            ).start()
            return c

        lax.fori_loop(1, n, send, 0)
        own_copy.wait()
        q = q_ref[...]
        row = lax.broadcasted_iota(jnp.int32, (q.shape[0], cap), 0)
        pos = lax.broadcasted_iota(jnp.int32, (q.shape[0], cap), 1)
        scores = jnp.zeros((q.shape[0], cap), jnp.float32)
        for r in range(reqs):
            part = lax.dot_general(q, own_vmem[r], (((1,), (1,)), ((), ())),
                                   preferred_element_type=jnp.float32)
            scores = jnp.where(row // per == r, part, scores)
        scores = scores * scale
        live = pos < len_ref[...]
        scores = jnp.where(live, scores, NEG)
        top = jnp.max(scores, axis=1, keepdims=True)
        weights = jnp.where(live, jnp.exp(scores - top), 0.0)
        total = jnp.sum(weights, axis=1, keepdims=True)
        wb = weights.astype(jnp.bfloat16)
        acc = jnp.zeros((q.shape[0], lanes), jnp.float32)
        for r in range(reqs):
            acc = acc + jnp.dot(jnp.where(row // per == r, wb, jnp.zeros_like(wb)), own_vmem[r],
                                preferred_element_type=jnp.float32)
        numer = pltpu.roll(acc, half, 1)
        lane = lax.broadcasted_iota(jnp.int32, acc.shape, 1)
        alive = total > 0.0
        safe = jnp.where(alive, total, 1.0)
        level = jnp.where(alive, top + jnp.log(safe), NEG)
        own_out[...] = jnp.where(lane < half, jnp.where(alive, numer / safe, 0.0), level)

        def finish(i, c):
            peer = lax.rem(me + i, n)
            origin = lax.rem(me + n - i, n)
            pltpu.make_async_remote_copy(
                x_ref, out_ref.at[me], send_sems.at[i], recv_sems.at[i],
                device_id=(peer, keep), device_id_type=mesh_id,
            ).wait_send()
            pltpu.make_async_remote_copy(
                x_ref, out_ref.at[origin], send_sems.at[i], recv_sems.at[i],
                device_id=(origin, keep), device_id_type=mesh_id,
            ).wait_recv()
            return c

        lax.fori_loop(1, n, finish, 0)
        local.wait()

    return pl.pallas_call(
        kernel,
        out_shape=(
            jax.ShapeDtypeStruct((n,) + tuple(q_slab.shape), q_slab.dtype),
            jax.ShapeDtypeStruct((q16.shape[0], lanes), jnp.float32),
        ),
        in_specs=[pl.BlockSpec(memory_space=pltpu.VMEM)] * 3 + [pl.BlockSpec(memory_space=pl.ANY)],
        out_specs=(pl.BlockSpec(memory_space=pltpu.VMEM), pl.BlockSpec(memory_space=pltpu.VMEM)),
        scratch_shapes=[
            pltpu.VMEM((reqs, cap, lanes), own_cache.dtype),
            pltpu.SemaphoreType.DMA((n,)),
            pltpu.SemaphoreType.DMA((n,)),
            pltpu.SemaphoreType.DMA(()),
            pltpu.SemaphoreType.DMA(()),
        ],
        compiler_params=pltpu.CompilerParams(collective_id=0, has_side_effects=True),
    )(q_slab, q16, lens16, own_cache)


def finish_kernel_call(qrows, prefix, base, req_group, jrow, pre_len, own, new, w_out, n_tok, n_kv):
    slab_rows = 16
    rows = slab_rows // 4
    groups, pre_dev, kv_lanes = prefix.shape
    window = 16 * 8
    heads = 4
    width = 64
    d_model = w_out.shape[1]
    cols = d_model // n_kv
    mesh_id = pl.DeviceIdType.MESH

    def kernel(q_ref, pre_ref, base_ref, rg_ref, j_ref, len_ref, own_ref, new_ref, w_ref, out_ref,
               recv_scr, acc_scr, part_scr, kv_recv, res_scr, packed_ref,
               tsend, trecv, ksend, krecv, loc_sems):
        me = lax.axis_index("tok")
        mk = lax.axis_index("kv")
        barrier = pltpu.get_barrier_semaphore()

        def greet_tok(i, c):
            pl.semaphore_signal(barrier, inc=1, device_id=(lax.rem(me + i, n_tok), mk), device_id_type=mesh_id)
            return c

        def greet_kv(i, c):
            pl.semaphore_signal(barrier, inc=1, device_id=(me, lax.rem(mk + i, n_kv)), device_id_type=mesh_id)
            return c

        lax.fori_loop(1, n_tok, greet_tok, 0)
        lax.fori_loop(1, n_kv, greet_kv, 0)

        glane = lax.broadcasted_iota(jnp.int32, (window, pre_dev), 1) + me * pre_dev
        olane = lax.broadcasted_iota(jnp.int32, (window, kv_lanes), 1)
        for g in range(groups):
            first = base_ref[g]
            qb = jnp.concatenate([q_ref[first + k] for k in range(window // 8)], axis=0)
            qb = qb.astype(jnp.bfloat16)
            kv = pre_ref[g]
            s = lax.dot_general(qb, kv, (((1,), (1,)), ((), ())), preferred_element_type=jnp.float32)
            s = s * SCALE
            live = glane < len_ref[g]
            s = jnp.where(live, s, NEG)
            top = jnp.max(s, axis=1, keepdims=True)
            e = jnp.where(live, jnp.exp(s - top), 0.0)
            total = jnp.sum(e, axis=1, keepdims=True)
            nm = jnp.dot(e.astype(jnp.bfloat16), kv, preferred_element_type=jnp.float32)
            nm = pltpu.roll(nm, width, 1)
            alive = total > 0.0
            safe = jnp.where(alive, total, 1.0)
            level = jnp.where(alive, top + jnp.log(safe), NEG)
            res_scr[pl.ds(g * (window // 8), window // 8)] = jnp.where(
                olane < width, jnp.where(alive, nm / safe, 0.0), level).reshape(window // 8, 8, kv_lanes)

        prow = lax.broadcasted_iota(jnp.int32, (8, kv_lanes), 0)

        def place(m, c):
            blocks = []
            for t in range(2):
                r = 2 * m + t
                blocks.append(res_scr[rg_ref[r] * (window // 8) + j_ref[r]])
            both = jnp.where(prow < 4, blocks[0], pltpu.roll(blocks[1], 4, 0))
            packed_ref[m // 2, pl.ds(pl.multiple_of((m % 2) * 8, 8), 8), :] = both
            return c

        lax.fori_loop(0, n_tok * 2, place, 0)
        pl.semaphore_wait(barrier, n_tok - 1 + n_kv - 1)

        local_copy = pltpu.make_async_copy(packed_ref.at[me], recv_scr.at[me], loc_sems.at[0])
        local_copy.start()

        def tok_copy(i, target, slot):
            return pltpu.make_async_remote_copy(
                packed_ref.at[target], recv_scr.at[slot], tsend.at[i], trecv.at[i],
                device_id=(target, mk), device_id_type=mesh_id,
            )

        def send_tok(i, c):
            tok_copy(i, lax.rem(me + i, n_tok), me).start()
            return c

        lax.fori_loop(1, n_tok, send_tok, 0)

        def finish_tok(i, c):
            tok_copy(i, lax.rem(me + i, n_tok), me).wait_send()
            origin = lax.rem(me + n_tok - i, n_tok)
            pltpu.make_async_remote_copy(
                packed_ref.at[origin], recv_scr.at[origin], tsend.at[i], trecv.at[i],
                device_id=(origin, mk), device_id_type=mesh_id,
            ).wait_recv()
            return c

        lax.fori_loop(1, n_tok, finish_tok, 0)
        local_copy.wait()

        x = recv_scr[...]
        loc = own_ref[...]
        nloc = new_ref[...]
        llane = lax.broadcasted_iota(jnp.int32, loc.shape, 1)
        big = jnp.maximum(jnp.maximum(jnp.max(x, axis=0), loc), nloc)
        keep_hi = llane >= width
        weight = jnp.where(keep_hi[None], jnp.exp(x - big[None]), 0.0)
        lweight = jnp.where(keep_hi, jnp.exp(loc - big), 0.0)
        nweight = jnp.where(keep_hi, jnp.exp(nloc - big), 0.0)
        weight = pltpu.roll(weight.reshape(-1, 128), width, 1).reshape(x.shape)
        lweight = pltpu.roll(lweight, width, 1)
        nweight = pltpu.roll(nweight, width, 1)
        denom = jnp.sum(weight, axis=0) + lweight + nweight
        numer = jnp.sum(weight * x, axis=0) + lweight * loc + nweight * nloc
        attn = jnp.where(llane < width, numer / jnp.where(llane < width, denom, 1.0), 0.0).astype(jnp.bfloat16)
        pi = lax.broadcasted_iota(jnp.int32, (slab_rows, slab_rows), 0)
        pj = lax.broadcasted_iota(jnp.int32, (slab_rows, slab_rows), 1)
        perm = jnp.where(pj == (pi % rows) * heads + pi // rows, 1.0, 0.0).astype(jnp.bfloat16)
        attn = jnp.dot(perm, attn, preferred_element_type=jnp.float32)
        shifted = pltpu.roll(attn, width, 1)
        row = lax.broadcasted_iota(jnp.int32, attn.shape, 0)
        head_of = row // rows
        acc = jnp.zeros((slab_rows, d_model), jnp.float32)
        for pair in range(heads // 2):
            lhs = jnp.where(head_of == 2 * pair, attn, jnp.where(head_of == 2 * pair + 1, shifted, 0.0))
            acc = acc + jnp.dot(
                lhs.astype(jnp.bfloat16), w_ref[pl.ds(pair * 2 * width, 2 * width), :],
                preferred_element_type=jnp.float32,
            )
        acc_scr[...] = acc
        partial = acc_scr[pl.ds(0, rows), :]
        for h in range(1, heads):
            partial = partial + acc_scr[pl.ds(h * rows, rows), :]
        part_scr[...] = partial

        def kv_src(target):
            return part_scr.at[:, pl.ds(pl.multiple_of(target * cols, cols), cols)]

        kv_local = pltpu.make_async_copy(kv_src(mk), kv_recv.at[mk], loc_sems.at[1])
        kv_local.start()

        def kv_copy(j, target, slot):
            return pltpu.make_async_remote_copy(
                kv_src(target), kv_recv.at[slot], ksend.at[j], krecv.at[j],
                device_id=(me, target), device_id_type=mesh_id,
            )

        def send_kv(j, c):
            kv_copy(j, lax.rem(mk + j, n_kv), mk).start()
            return c

        lax.fori_loop(1, n_kv, send_kv, 0)

        def finish_kv(j, c):
            kv_copy(j, lax.rem(mk + j, n_kv), mk).wait_send()
            origin = lax.rem(mk + n_kv - j, n_kv)
            pltpu.make_async_remote_copy(
                kv_src(origin), kv_recv.at[origin], ksend.at[j], krecv.at[j],
                device_id=(me, origin), device_id_type=mesh_id,
            ).wait_recv()
            return c

        lax.fori_loop(1, n_kv, finish_kv, 0)
        kv_local.wait()
        out_ref[...] = jnp.sum(kv_recv[...], axis=0).astype(out_ref.dtype)

    return pl.pallas_call(
        kernel,
        out_shape=jax.ShapeDtypeStruct((rows, cols), jnp.bfloat16),
        in_specs=[pl.BlockSpec(memory_space=pltpu.VMEM)] * 2
        + [pl.BlockSpec(memory_space=pltpu.SMEM)] * 4
        + [pl.BlockSpec(memory_space=pltpu.VMEM)] * 3,
        out_specs=pl.BlockSpec(memory_space=pltpu.VMEM),
        scratch_shapes=[
            pltpu.VMEM((n_tok, slab_rows, 128), jnp.float32),
            pltpu.VMEM((slab_rows, d_model), jnp.float32),
            pltpu.VMEM((rows, d_model), jnp.float32),
            pltpu.VMEM((n_kv, rows, cols), jnp.float32),
            pltpu.VMEM((groups * (window // 8), 8, 128), jnp.float32),
            pltpu.VMEM((n_tok, slab_rows, 128), jnp.float32),
            pltpu.SemaphoreType.DMA((n_tok,)),
            pltpu.SemaphoreType.DMA((n_tok,)),
            pltpu.SemaphoreType.DMA((n_kv,)),
            pltpu.SemaphoreType.DMA((n_kv,)),
            pltpu.SemaphoreType.DMA((2,)),
        ],
        compiler_params=pltpu.CompilerParams(collective_id=1, has_side_effects=True),
    )(qrows, prefix, base, req_group, jrow, pre_len, own, new, w_out)


def block_stats(query, keyval, live):
    width = query.shape[-1]
    keys = keyval[..., :width]
    values = keyval[..., width:]
    scores = jnp.einsum("rhge,hrpe->rhgp", query, keys, preferred_element_type=jnp.float32) * SCALE
    mask = live[:, None, None, :]
    scores = jnp.where(mask, scores, NEG)
    top = jnp.max(scores, axis=-1)
    weights = jnp.where(mask, jnp.exp(scores - top[..., None]), 0.0)
    total = jnp.sum(weights, axis=-1)
    numer = jnp.einsum(
        "rhgp,hrpe->rhge", weights.astype(jnp.bfloat16), values, preferred_element_type=jnp.float32
    )
    return (top, total, numer)


def prompt_stats(all_query, prefix_cache, req_group, pre_len, block):
    all_rows, heads, per_kv, width = all_query.shape
    groups = prefix_cache.shape[1]
    pre_dev = prefix_cache.shape[2]
    group_ids = jnp.arange(groups, dtype=jnp.int32)
    starts = jnp.sum((req_group[None, :] < group_ids[:, None]).astype(jnp.int32), axis=1)
    slot_ids = jnp.arange(SHARE, dtype=jnp.int32)
    source = jnp.minimum(starts[:, None] + slot_ids[None, :], all_rows - 1).reshape(-1)
    slotted = jnp.take(all_query, source, axis=0).reshape(groups, SHARE, heads, per_kv, width)
    keys = prefix_cache[..., :width]
    values = prefix_cache[..., width:]
    scores = (
        jnp.einsum("gshqe,hgpe->hgsqp", slotted, keys, preferred_element_type=jnp.float32) * SCALE
    )
    pre_pos = block * pre_dev + jnp.arange(pre_dev, dtype=jnp.int32)
    live = pre_pos[None, :] < pre_len[:, None]
    mask = live[None, :, None, None, :]
    scores = jnp.where(mask, scores, NEG)
    top = jnp.max(scores, axis=-1)
    weights = jnp.where(mask, jnp.exp(scores - top[..., None]), 0.0)
    total = jnp.sum(weights, axis=-1)
    numer = jnp.einsum(
        "hgsqp,hgpe->hgsqe",
        weights.astype(jnp.bfloat16),
        values,
        preferred_element_type=jnp.float32,
    )
    match = req_group[:, None] == group_ids[None, :]
    start_req = jnp.sum(jnp.where(match, starts[None, :], 0), axis=1)
    place = req_group * SHARE + jnp.arange(all_rows, dtype=jnp.int32) - start_req
    alive = total > 0.0
    safe = jnp.where(alive, total, 1.0)
    level = jnp.where(alive, top + jnp.log(safe), NEG)
    packed = jnp.concatenate(
        [jnp.where(alive[..., None], numer / safe[..., None], 0.0),
         jnp.broadcast_to(level[..., None], top.shape + (128 - width,))],
        axis=-1,
    ).reshape(heads, groups * SHARE, per_kv, 128)
    packed = jnp.take(packed, place, axis=1)
    return jnp.transpose(packed, (1, 0, 2, 3)).reshape(all_rows * heads * per_kv, 128)


def body(hidden_in, w_query, w_keyval, w_out, own_cache, prefix_cache, own_len, req_group, pre_len):
    rows = hidden_in.shape[0]
    heads = w_keyval.shape[1]
    width = w_keyval.shape[2] // 2
    per_kv = w_query.shape[1] // (heads * width)
    columns = heads * per_kv
    inputs = hidden_in.astype(jnp.float32)
    normed = (inputs * lax.rsqrt(jnp.mean(inputs * inputs, axis=1, keepdims=True) + 1e-05)).astype(
        jnp.bfloat16
    )
    query = jnp.dot(normed, w_query, preferred_element_type=jnp.float32).astype(jnp.bfloat16)
    newkv = jnp.einsum("rd,dhe->rhe", normed, w_keyval, preferred_element_type=jnp.float32).astype(
        jnp.bfloat16
    )
    n_tok = lax.axis_size("tok")
    n_kv = lax.axis_size("kv")
    q_slab = query.reshape(-1, 128)
    q16 = jnp.concatenate(
        [query.reshape(rows * columns, width), jnp.zeros((rows * columns, width), query.dtype)], axis=1
    )
    lens16 = jnp.repeat(own_len, columns).reshape(rows * columns, 1)
    gathered, own_block = broadcast_with_own(q_slab, q16, lens16, own_cache, n_tok, SCALE)
    gathered = gathered.reshape(n_tok * rows, -1)
    all_rows = gathered.shape[0]
    qrows = jnp.concatenate(
        [gathered.reshape(all_rows, columns, width).astype(jnp.float32),
         jnp.zeros((all_rows, columns, 128 - width), jnp.float32)], axis=2)
    qrows = jnp.concatenate([qrows, jnp.zeros((all_rows, 8 - columns, 128), jnp.float32)], axis=1)
    groups = prefix_cache.shape[1]
    group_ids = jnp.arange(groups, dtype=jnp.int32)
    starts = jnp.sum((req_group[None, :] < group_ids[:, None]).astype(jnp.int32), axis=1)
    base = jnp.minimum(starts, all_rows - SHARE)
    rg = jnp.clip(req_group, 0, groups - 1)
    own_start = jnp.sum((req_group[None, :] < req_group[:, None]).astype(jnp.int32), axis=1)
    own_base = jnp.minimum(own_start, all_rows - SHARE)
    jrow = jnp.clip(jnp.arange(all_rows, dtype=jnp.int32) - own_base, 0, SHARE - 1)
    local_query = query.reshape(rows, heads, per_kv, width)
    s_new = (
        jnp.einsum(
            "rhge,rhe->rhg", local_query, newkv[..., :width], preferred_element_type=jnp.float32
        )
        * SCALE
    )
    s_new = s_new.reshape(rows, columns)
    new_value = jnp.broadcast_to(
        newkv[:, :, None, width:].astype(jnp.float32), (rows, heads, per_kv, width)
    ).reshape(rows, columns, width)
    new_block = jnp.concatenate(
        [new_value, jnp.broadcast_to(s_new[..., None], (rows, columns, 128 - width))],
        axis=-1,
    ).reshape(rows * columns, 128)
    return finish_kernel_call(qrows, prefix_cache[0], base, rg, jrow, pre_len, own_block, new_block, w_out, n_tok, n_kv)


def solution(mesh):
    in_specs = (
        P("tok", None),
        P(None, "kv"),
        P(None, "kv", None),
        P("kv", None),
        P("kv", "tok", None, None),
        P("kv", None, "tok", None),
        P("tok"),
        P(),
        P(),
    )
    out_specs = P("tok", "kv")
    return jax.shard_map(body, mesh=mesh, in_specs=in_specs, out_specs=out_specs, check_vma=False)
```

```python
import jax
import jax.numpy as jnp
from jax import lax
from jax.sharding import PartitionSpec as P
from jax.experimental import pallas as pl
from jax.experimental.pallas import tpu as pltpu

SHARE = 16


SCALE = 0.015625
NEG = -1e30


def exchange(slabs, axis, other, n, broadcast, cid):
    slab_shape = slabs.shape[1:] if not broadcast else slabs.shape
    mesh_id = pl.DeviceIdType.MESH

    def kernel(x_ref, out_ref, send_sems, recv_sems, local_sem):
        me = lax.axis_index(axis)
        keep = lax.axis_index(other)

        def dev(peer):
            return (peer, keep) if axis == "tok" else (keep, peer)

        def src(peer):
            return x_ref if broadcast else x_ref.at[peer]

        barrier = pltpu.get_barrier_semaphore()

        def greet(i, c):
            peer = lax.rem(me + i, n)
            pl.semaphore_signal(barrier, inc=1, device_id=dev(peer), device_id_type=mesh_id)
            return c

        lax.fori_loop(1, n, greet, 0)
        pl.semaphore_wait(barrier, n - 1)
        local = pltpu.make_async_copy(src(me), out_ref.at[me], local_sem)
        local.start()

        def send(i, c):
            peer = lax.rem(me + i, n)
            pltpu.make_async_remote_copy(
                src(peer), out_ref.at[me], send_sems.at[i], recv_sems.at[i],
                device_id=dev(peer), device_id_type=mesh_id,
            ).start()
            return c

        lax.fori_loop(1, n, send, 0)

        def finish(i, c):
            peer = lax.rem(me + i, n)
            origin = lax.rem(me + n - i, n)
            pltpu.make_async_remote_copy(
                src(peer), out_ref.at[me], send_sems.at[i], recv_sems.at[i],
                device_id=dev(peer), device_id_type=mesh_id,
            ).wait_send()
            pltpu.make_async_remote_copy(
                src(peer), out_ref.at[origin], send_sems.at[i], recv_sems.at[i],
                device_id=dev(origin), device_id_type=mesh_id,
            ).wait_recv()
            return c

        lax.fori_loop(1, n, finish, 0)
        local.wait()

    return pl.pallas_call(
        kernel,
        out_shape=jax.ShapeDtypeStruct((n,) + tuple(slab_shape), slabs.dtype),
        in_specs=[pl.BlockSpec(memory_space=pltpu.VMEM)],
        out_specs=pl.BlockSpec(memory_space=pltpu.VMEM),
        scratch_shapes=[
            pltpu.SemaphoreType.DMA((n,)),
            pltpu.SemaphoreType.DMA((n,)),
            pltpu.SemaphoreType.DMA(()),
        ],
        compiler_params=pltpu.CompilerParams(collective_id=cid, has_side_effects=True),
    )(slabs)


def broadcast_with_own(q_slab, q16, lens16, own_cache, n, scale):
    mesh_id = pl.DeviceIdType.MESH
    reqs, cap, lanes = own_cache.shape[1:]
    half = lanes // 2
    per = q16.shape[0] // reqs

    def kernel(x_ref, q_ref, len_ref, own_hbm, out_ref, own_out, own_vmem,
               send_sems, recv_sems, local_sem, own_sem):
        me = lax.axis_index("tok")
        keep = lax.axis_index("kv")
        own_copy = pltpu.make_async_copy(own_hbm.at[0], own_vmem, own_sem)
        own_copy.start()
        barrier = pltpu.get_barrier_semaphore()

        def greet(i, c):
            pl.semaphore_signal(barrier, inc=1, device_id=(lax.rem(me + i, n), keep), device_id_type=mesh_id)
            return c

        lax.fori_loop(1, n, greet, 0)
        pl.semaphore_wait(barrier, n - 1)
        local = pltpu.make_async_copy(x_ref, out_ref.at[me], local_sem)
        local.start()

        def send(i, c):
            peer = lax.rem(me + i, n)
            pltpu.make_async_remote_copy(
                x_ref, out_ref.at[me], send_sems.at[i], recv_sems.at[i],
                device_id=(peer, keep), device_id_type=mesh_id,
            ).start()
            return c

        lax.fori_loop(1, n, send, 0)
        own_copy.wait()
        q = q_ref[...]
        row = lax.broadcasted_iota(jnp.int32, (q.shape[0], cap), 0)
        pos = lax.broadcasted_iota(jnp.int32, (q.shape[0], cap), 1)
        scores = jnp.zeros((q.shape[0], cap), jnp.float32)
        for r in range(reqs):
            part = lax.dot_general(q, own_vmem[r], (((1,), (1,)), ((), ())),
                                   preferred_element_type=jnp.float32)
            scores = jnp.where(row // per == r, part, scores)
        scores = scores * scale
        row_len = jnp.zeros((q.shape[0], cap), jnp.int32)
        for r in range(reqs):
            row_len = jnp.where(row // per == r, len_ref[r], row_len)
        live = pos < row_len
        scores = jnp.where(live, scores, NEG)
        top = jnp.max(scores, axis=1, keepdims=True)
        weights = jnp.where(live, jnp.exp(scores - top), 0.0)
        total = jnp.sum(weights, axis=1, keepdims=True)
        wb = weights.astype(jnp.bfloat16)
        acc = jnp.zeros((q.shape[0], lanes), jnp.float32)
        for r in range(reqs):
            acc = acc + jnp.dot(jnp.where(row // per == r, wb, jnp.zeros_like(wb)), own_vmem[r],
                                preferred_element_type=jnp.float32)
        numer = pltpu.roll(acc, half, 1)
        lane = lax.broadcasted_iota(jnp.int32, acc.shape, 1)
        alive = total > 0.0
        safe = jnp.where(alive, total, 1.0)
        level = jnp.where(alive, top + jnp.log(safe), NEG)
        own_out[...] = jnp.where(lane < half, jnp.where(alive, numer / safe, 0.0), level)

        def finish(i, c):
            peer = lax.rem(me + i, n)
            origin = lax.rem(me + n - i, n)
            pltpu.make_async_remote_copy(
                x_ref, out_ref.at[me], send_sems.at[i], recv_sems.at[i],
                device_id=(peer, keep), device_id_type=mesh_id,
            ).wait_send()
            pltpu.make_async_remote_copy(
                x_ref, out_ref.at[origin], send_sems.at[i], recv_sems.at[i],
                device_id=(origin, keep), device_id_type=mesh_id,
            ).wait_recv()
            return c

        lax.fori_loop(1, n, finish, 0)
        local.wait()

    return pl.pallas_call(
        kernel,
        out_shape=(
            jax.ShapeDtypeStruct((n,) + tuple(q_slab.shape), q_slab.dtype),
            jax.ShapeDtypeStruct((q16.shape[0], lanes), jnp.float32),
        ),
        in_specs=[pl.BlockSpec(memory_space=pltpu.VMEM)] * 2
        + [pl.BlockSpec(memory_space=pltpu.SMEM), pl.BlockSpec(memory_space=pl.ANY)],
        out_specs=(pl.BlockSpec(memory_space=pltpu.VMEM), pl.BlockSpec(memory_space=pltpu.VMEM)),
        scratch_shapes=[
            pltpu.VMEM((reqs, cap, lanes), own_cache.dtype),
            pltpu.SemaphoreType.DMA((n,)),
            pltpu.SemaphoreType.DMA((n,)),
            pltpu.SemaphoreType.DMA(()),
            pltpu.SemaphoreType.DMA(()),
        ],
        compiler_params=pltpu.CompilerParams(collective_id=0, has_side_effects=True),
    )(q_slab, q16, lens16, own_cache)


def finish_kernel_call(qrows, prefix, base, req_group, jrow, pre_len, own, new, w_out, n_tok, n_kv):
    slab_rows = 16
    rows = slab_rows // 4
    groups, pre_dev, kv_lanes = prefix.shape
    window = 16 * 8
    heads = 4
    width = 64
    d_model = w_out.shape[1]
    cols = d_model // n_kv
    mesh_id = pl.DeviceIdType.MESH

    def kernel(q_ref, pre_ref, base_ref, rg_ref, j_ref, len_ref, own_ref, new_ref, w_ref, out_ref,
               recv_scr, acc_scr, part_scr, kv_recv, res_scr, packed_ref,
               tsend, trecv, ksend, krecv, loc_sems):
        me = lax.axis_index("tok")
        mk = lax.axis_index("kv")
        barrier = pltpu.get_barrier_semaphore()

        def greet_tok(i, c):
            pl.semaphore_signal(barrier, inc=1, device_id=(lax.rem(me + i, n_tok), mk), device_id_type=mesh_id)
            return c

        def greet_kv(i, c):
            pl.semaphore_signal(barrier, inc=1, device_id=(me, lax.rem(mk + i, n_kv)), device_id_type=mesh_id)
            return c

        lax.fori_loop(1, n_tok, greet_tok, 0)
        lax.fori_loop(1, n_kv, greet_kv, 0)

        glane = lax.broadcasted_iota(jnp.int32, (window, pre_dev), 1) + me * pre_dev
        olane = lax.broadcasted_iota(jnp.int32, (window, kv_lanes), 1)
        for g in range(groups):
            first = base_ref[g]
            qb = jnp.concatenate([q_ref[first + k] for k in range(window // 8)], axis=0)
            qb = qb.astype(jnp.bfloat16)
            kv = pre_ref[g]
            s = lax.dot_general(qb, kv, (((1,), (1,)), ((), ())), preferred_element_type=jnp.float32)
            s = s * SCALE
            live = glane < len_ref[g]
            s = jnp.where(live, s, NEG)
            top = jnp.max(s, axis=1, keepdims=True)
            e = jnp.where(live, jnp.exp(s - top), 0.0)
            total = jnp.sum(e, axis=1, keepdims=True)
            nm = jnp.dot(e.astype(jnp.bfloat16), kv, preferred_element_type=jnp.float32)
            nm = pltpu.roll(nm, width, 1)
            alive = total > 0.0
            safe = jnp.where(alive, total, 1.0)
            level = jnp.where(alive, top + jnp.log(safe), NEG)
            res_scr[pl.ds(g * (window // 8), window // 8)] = jnp.where(
                olane < width, jnp.where(alive, nm / safe, 0.0), level).reshape(window // 8, 8, kv_lanes)

        prow = lax.broadcasted_iota(jnp.int32, (8, kv_lanes), 0)

        def place(m, c):
            blocks = []
            for t in range(2):
                r = 2 * m + t
                blocks.append(res_scr[rg_ref[r] * (window // 8) + j_ref[r]])
            both = jnp.where(prow < 4, blocks[0], pltpu.roll(blocks[1], 4, 0))
            packed_ref[m // 2, pl.ds(pl.multiple_of((m % 2) * 8, 8), 8), :] = both
            return c

        lax.fori_loop(0, n_tok * 2, place, 0)
        pl.semaphore_wait(barrier, n_tok - 1 + n_kv - 1)

        local_copy = pltpu.make_async_copy(packed_ref.at[me], recv_scr.at[me], loc_sems.at[0])
        local_copy.start()

        def tok_copy(i, target, slot):
            return pltpu.make_async_remote_copy(
                packed_ref.at[target], recv_scr.at[slot], tsend.at[i], trecv.at[i],
                device_id=(target, mk), device_id_type=mesh_id,
            )

        def send_tok(i, c):
            tok_copy(i, lax.rem(me + i, n_tok), me).start()
            return c

        lax.fori_loop(1, n_tok, send_tok, 0)

        def finish_tok(i, c):
            tok_copy(i, lax.rem(me + i, n_tok), me).wait_send()
            origin = lax.rem(me + n_tok - i, n_tok)
            pltpu.make_async_remote_copy(
                packed_ref.at[origin], recv_scr.at[origin], tsend.at[i], trecv.at[i],
                device_id=(origin, mk), device_id_type=mesh_id,
            ).wait_recv()
            return c

        lax.fori_loop(1, n_tok, finish_tok, 0)
        local_copy.wait()

        x = recv_scr[...]
        loc = own_ref[...]
        nloc = new_ref[...]
        llane = lax.broadcasted_iota(jnp.int32, loc.shape, 1)
        big = jnp.maximum(jnp.maximum(jnp.max(x, axis=0), loc), nloc)
        keep_hi = llane >= width
        weight = jnp.where(keep_hi[None], jnp.exp(x - big[None]), 0.0)
        lweight = jnp.where(keep_hi, jnp.exp(loc - big), 0.0)
        nweight = jnp.where(keep_hi, jnp.exp(nloc - big), 0.0)
        weight = pltpu.roll(weight.reshape(-1, 128), width, 1).reshape(x.shape)
        lweight = pltpu.roll(lweight, width, 1)
        nweight = pltpu.roll(nweight, width, 1)
        denom = jnp.sum(weight, axis=0) + lweight + nweight
        numer = jnp.sum(weight * x, axis=0) + lweight * loc + nweight * nloc
        attn = jnp.where(llane < width, numer / jnp.where(llane < width, denom, 1.0), 0.0).astype(jnp.bfloat16)
        pi = lax.broadcasted_iota(jnp.int32, (slab_rows, slab_rows), 0)
        pj = lax.broadcasted_iota(jnp.int32, (slab_rows, slab_rows), 1)
        perm = jnp.where(pj == (pi % rows) * heads + pi // rows, 1.0, 0.0).astype(jnp.bfloat16)
        attn = jnp.dot(perm, attn, preferred_element_type=jnp.float32)
        shifted = pltpu.roll(attn, width, 1)
        row = lax.broadcasted_iota(jnp.int32, attn.shape, 0)
        head_of = row // rows
        acc = jnp.zeros((slab_rows, d_model), jnp.float32)
        for pair in range(heads // 2):
            lhs = jnp.where(head_of == 2 * pair, attn, jnp.where(head_of == 2 * pair + 1, shifted, 0.0))
            acc = acc + jnp.dot(
                lhs.astype(jnp.bfloat16), w_ref[pl.ds(pair * 2 * width, 2 * width), :],
                preferred_element_type=jnp.float32,
            )
        acc_scr[...] = acc
        partial = acc_scr[pl.ds(0, rows), :]
        for h in range(1, heads):
            partial = partial + acc_scr[pl.ds(h * rows, rows), :]
        part_scr[...] = partial

        def kv_src(target):
            return part_scr.at[:, pl.ds(pl.multiple_of(target * cols, cols), cols)]

        kv_local = pltpu.make_async_copy(kv_src(mk), kv_recv.at[mk], loc_sems.at[1])
        kv_local.start()

        def kv_copy(j, target, slot):
            return pltpu.make_async_remote_copy(
                kv_src(target), kv_recv.at[slot], ksend.at[j], krecv.at[j],
                device_id=(me, target), device_id_type=mesh_id,
            )

        def send_kv(j, c):
            kv_copy(j, lax.rem(mk + j, n_kv), mk).start()
            return c

        lax.fori_loop(1, n_kv, send_kv, 0)

        def finish_kv(j, c):
            kv_copy(j, lax.rem(mk + j, n_kv), mk).wait_send()
            origin = lax.rem(mk + n_kv - j, n_kv)
            pltpu.make_async_remote_copy(
                kv_src(origin), kv_recv.at[origin], ksend.at[j], krecv.at[j],
                device_id=(me, origin), device_id_type=mesh_id,
            ).wait_recv()
            return c

        lax.fori_loop(1, n_kv, finish_kv, 0)
        kv_local.wait()
        out_ref[...] = jnp.sum(kv_recv[...], axis=0).astype(out_ref.dtype)

    return pl.pallas_call(
        kernel,
        out_shape=jax.ShapeDtypeStruct((rows, cols), jnp.bfloat16),
        in_specs=[pl.BlockSpec(memory_space=pltpu.VMEM)] * 2
        + [pl.BlockSpec(memory_space=pltpu.SMEM)] * 4
        + [pl.BlockSpec(memory_space=pltpu.VMEM)] * 3,
        out_specs=pl.BlockSpec(memory_space=pltpu.VMEM),
        scratch_shapes=[
            pltpu.VMEM((n_tok, slab_rows, 128), jnp.float32),
            pltpu.VMEM((slab_rows, d_model), jnp.float32),
            pltpu.VMEM((rows, d_model), jnp.float32),
            pltpu.VMEM((n_kv, rows, cols), jnp.float32),
            pltpu.VMEM((groups * (window // 8), 8, 128), jnp.float32),
            pltpu.VMEM((n_tok, slab_rows, 128), jnp.float32),
            pltpu.SemaphoreType.DMA((n_tok,)),
            pltpu.SemaphoreType.DMA((n_tok,)),
            pltpu.SemaphoreType.DMA((n_kv,)),
            pltpu.SemaphoreType.DMA((n_kv,)),
            pltpu.SemaphoreType.DMA((2,)),
        ],
        compiler_params=pltpu.CompilerParams(collective_id=1, has_side_effects=True),
    )(qrows, prefix, base, req_group, jrow, pre_len, own, new, w_out)


def block_stats(query, keyval, live):
    width = query.shape[-1]
    keys = keyval[..., :width]
    values = keyval[..., width:]
    scores = jnp.einsum("rhge,hrpe->rhgp", query, keys, preferred_element_type=jnp.float32) * SCALE
    mask = live[:, None, None, :]
    scores = jnp.where(mask, scores, NEG)
    top = jnp.max(scores, axis=-1)
    weights = jnp.where(mask, jnp.exp(scores - top[..., None]), 0.0)
    total = jnp.sum(weights, axis=-1)
    numer = jnp.einsum(
        "rhgp,hrpe->rhge", weights.astype(jnp.bfloat16), values, preferred_element_type=jnp.float32
    )
    return (top, total, numer)


def prompt_stats(all_query, prefix_cache, req_group, pre_len, block):
    all_rows, heads, per_kv, width = all_query.shape
    groups = prefix_cache.shape[1]
    pre_dev = prefix_cache.shape[2]
    group_ids = jnp.arange(groups, dtype=jnp.int32)
    starts = jnp.sum((req_group[None, :] < group_ids[:, None]).astype(jnp.int32), axis=1)
    slot_ids = jnp.arange(SHARE, dtype=jnp.int32)
    source = jnp.minimum(starts[:, None] + slot_ids[None, :], all_rows - 1).reshape(-1)
    slotted = jnp.take(all_query, source, axis=0).reshape(groups, SHARE, heads, per_kv, width)
    keys = prefix_cache[..., :width]
    values = prefix_cache[..., width:]
    scores = (
        jnp.einsum("gshqe,hgpe->hgsqp", slotted, keys, preferred_element_type=jnp.float32) * SCALE
    )
    pre_pos = block * pre_dev + jnp.arange(pre_dev, dtype=jnp.int32)
    live = pre_pos[None, :] < pre_len[:, None]
    mask = live[None, :, None, None, :]
    scores = jnp.where(mask, scores, NEG)
    top = jnp.max(scores, axis=-1)
    weights = jnp.where(mask, jnp.exp(scores - top[..., None]), 0.0)
    total = jnp.sum(weights, axis=-1)
    numer = jnp.einsum(
        "hgsqp,hgpe->hgsqe",
        weights.astype(jnp.bfloat16),
        values,
        preferred_element_type=jnp.float32,
    )
    match = req_group[:, None] == group_ids[None, :]
    start_req = jnp.sum(jnp.where(match, starts[None, :], 0), axis=1)
    place = req_group * SHARE + jnp.arange(all_rows, dtype=jnp.int32) - start_req
    alive = total > 0.0
    safe = jnp.where(alive, total, 1.0)
    level = jnp.where(alive, top + jnp.log(safe), NEG)
    packed = jnp.concatenate(
        [jnp.where(alive[..., None], numer / safe[..., None], 0.0),
         jnp.broadcast_to(level[..., None], top.shape + (128 - width,))],
        axis=-1,
    ).reshape(heads, groups * SHARE, per_kv, 128)
    packed = jnp.take(packed, place, axis=1)
    return jnp.transpose(packed, (1, 0, 2, 3)).reshape(all_rows * heads * per_kv, 128)


def body(hidden_in, w_query, w_keyval, w_out, own_cache, prefix_cache, own_len, req_group, pre_len):
    rows = hidden_in.shape[0]
    heads = w_keyval.shape[1]
    width = w_keyval.shape[2] // 2
    per_kv = w_query.shape[1] // (heads * width)
    columns = heads * per_kv
    inputs = hidden_in.astype(jnp.float32)
    normed = (inputs * lax.rsqrt(jnp.mean(inputs * inputs, axis=1, keepdims=True) + 1e-05)).astype(
        jnp.bfloat16
    )
    query = jnp.dot(normed, w_query, preferred_element_type=jnp.float32).astype(jnp.bfloat16)
    newkv = jnp.einsum("rd,dhe->rhe", normed, w_keyval, preferred_element_type=jnp.float32).astype(
        jnp.bfloat16
    )
    n_tok = lax.axis_size("tok")
    n_kv = lax.axis_size("kv")
    q_slab = query.reshape(-1, 128)
    q16 = jnp.concatenate(
        [query.reshape(rows * columns, width), jnp.zeros((rows * columns, width), query.dtype)], axis=1
    )
    gathered, own_block = broadcast_with_own(q_slab, q16, own_len, own_cache, n_tok, SCALE)
    gathered = gathered.reshape(n_tok * rows, -1)
    all_rows = gathered.shape[0]
    qrows = jnp.concatenate(
        [gathered.reshape(all_rows, columns, width).astype(jnp.float32),
         jnp.zeros((all_rows, columns, 128 - width), jnp.float32)], axis=2)
    qrows = jnp.concatenate([qrows, jnp.zeros((all_rows, 8 - columns, 128), jnp.float32)], axis=1)
    groups = prefix_cache.shape[1]
    group_ids = jnp.arange(groups, dtype=jnp.int32)
    starts = jnp.sum((req_group[None, :] < group_ids[:, None]).astype(jnp.int32), axis=1)
    base = jnp.minimum(starts, all_rows - SHARE)
    rg = jnp.clip(req_group, 0, groups - 1)
    own_start = jnp.sum((req_group[None, :] < req_group[:, None]).astype(jnp.int32), axis=1)
    own_base = jnp.minimum(own_start, all_rows - SHARE)
    jrow = jnp.clip(jnp.arange(all_rows, dtype=jnp.int32) - own_base, 0, SHARE - 1)
    local_query = query.reshape(rows, heads, per_kv, width)
    s_new = (
        jnp.einsum(
            "rhge,rhe->rhg", local_query, newkv[..., :width], preferred_element_type=jnp.float32
        )
        * SCALE
    )
    s_new = s_new.reshape(rows, columns)
    new_value = jnp.broadcast_to(
        newkv[:, :, None, width:].astype(jnp.float32), (rows, heads, per_kv, width)
    ).reshape(rows, columns, width)
    new_block = jnp.concatenate(
        [new_value, jnp.broadcast_to(s_new[..., None], (rows, columns, 128 - width))],
        axis=-1,
    ).reshape(rows * columns, 128)
    return finish_kernel_call(qrows, prefix_cache[0], base, rg, jrow, pre_len, own_block, new_block, w_out, n_tok, n_kv)


def solution(mesh):
    in_specs = (
        P("tok", None),
        P(None, "kv"),
        P(None, "kv", None),
        P("kv", None),
        P("kv", "tok", None, None),
        P("kv", None, "tok", None),
        P("tok"),
        P(),
        P(),
    )
    out_specs = P("tok", "kv")
    return jax.shard_map(body, mesh=mesh, in_specs=in_specs, out_specs=out_specs, check_vma=False)
```

```python
import jax
import jax.numpy as jnp
from jax import lax
from jax.sharding import PartitionSpec as P
from jax.experimental import pallas as pl
from jax.experimental.pallas import tpu as pltpu

SHARE = 16


SCALE = 0.015625
NEG = -1e30


def exchange(slabs, axis, other, n, broadcast, cid):
    slab_shape = slabs.shape[1:] if not broadcast else slabs.shape
    mesh_id = pl.DeviceIdType.MESH

    def kernel(x_ref, out_ref, send_sems, recv_sems, local_sem):
        me = lax.axis_index(axis)
        keep = lax.axis_index(other)

        def dev(peer):
            return (peer, keep) if axis == "tok" else (keep, peer)

        def src(peer):
            return x_ref if broadcast else x_ref.at[peer]

        barrier = pltpu.get_barrier_semaphore()

        def greet(i, c):
            peer = lax.rem(me + i, n)
            pl.semaphore_signal(barrier, inc=1, device_id=dev(peer), device_id_type=mesh_id)
            return c

        lax.fori_loop(1, n, greet, 0)
        pl.semaphore_wait(barrier, n - 1)
        local = pltpu.make_async_copy(src(me), out_ref.at[me], local_sem)
        local.start()

        def send(i, c):
            peer = lax.rem(me + i, n)
            pltpu.make_async_remote_copy(
                src(peer), out_ref.at[me], send_sems.at[i], recv_sems.at[i],
                device_id=dev(peer), device_id_type=mesh_id,
            ).start()
            return c

        lax.fori_loop(1, n, send, 0)

        def finish(i, c):
            peer = lax.rem(me + i, n)
            origin = lax.rem(me + n - i, n)
            pltpu.make_async_remote_copy(
                src(peer), out_ref.at[me], send_sems.at[i], recv_sems.at[i],
                device_id=dev(peer), device_id_type=mesh_id,
            ).wait_send()
            pltpu.make_async_remote_copy(
                src(peer), out_ref.at[origin], send_sems.at[i], recv_sems.at[i],
                device_id=dev(origin), device_id_type=mesh_id,
            ).wait_recv()
            return c

        lax.fori_loop(1, n, finish, 0)
        local.wait()

    return pl.pallas_call(
        kernel,
        out_shape=jax.ShapeDtypeStruct((n,) + tuple(slab_shape), slabs.dtype),
        in_specs=[pl.BlockSpec(memory_space=pltpu.VMEM)],
        out_specs=pl.BlockSpec(memory_space=pltpu.VMEM),
        scratch_shapes=[
            pltpu.SemaphoreType.DMA((n,)),
            pltpu.SemaphoreType.DMA((n,)),
            pltpu.SemaphoreType.DMA(()),
        ],
        compiler_params=pltpu.CompilerParams(collective_id=cid, has_side_effects=True),
    )(slabs)


def broadcast_with_own(q_slab, q16, lens16, own_cache, n, scale):
    mesh_id = pl.DeviceIdType.MESH
    reqs, cap, lanes = own_cache.shape[1:]
    half = lanes // 2
    per = q16.shape[0] // reqs

    def kernel(x_ref, q_ref, len_ref, own_hbm, out_ref, own_out, rows_out, own_vmem,
               send_sems, recv_sems, local_sem, own_sem):
        me = lax.axis_index("tok")
        keep = lax.axis_index("kv")
        own_copy = pltpu.make_async_copy(own_hbm.at[0], own_vmem, own_sem)
        own_copy.start()
        barrier = pltpu.get_barrier_semaphore()

        def greet(i, c):
            pl.semaphore_signal(barrier, inc=1, device_id=(lax.rem(me + i, n), keep), device_id_type=mesh_id)
            return c

        lax.fori_loop(1, n, greet, 0)
        pl.semaphore_wait(barrier, n - 1)
        local = pltpu.make_async_copy(x_ref, out_ref.at[me], local_sem)
        local.start()

        def send(i, c):
            peer = lax.rem(me + i, n)
            pltpu.make_async_remote_copy(
                x_ref, out_ref.at[me], send_sems.at[i], recv_sems.at[i],
                device_id=(peer, keep), device_id_type=mesh_id,
            ).start()
            return c

        lax.fori_loop(1, n, send, 0)
        own_copy.wait()
        q = q_ref[...]
        row = lax.broadcasted_iota(jnp.int32, (q.shape[0], cap), 0)
        pos = lax.broadcasted_iota(jnp.int32, (q.shape[0], cap), 1)
        scores = jnp.zeros((q.shape[0], cap), jnp.float32)
        for r in range(reqs):
            part = lax.dot_general(q, own_vmem[r], (((1,), (1,)), ((), ())),
                                   preferred_element_type=jnp.float32)
            scores = jnp.where(row // per == r, part, scores)
        scores = scores * scale
        row_len = jnp.zeros((q.shape[0], cap), jnp.int32)
        for r in range(reqs):
            row_len = jnp.where(row // per == r, len_ref[r], row_len)
        live = pos < row_len
        scores = jnp.where(live, scores, NEG)
        top = jnp.max(scores, axis=1, keepdims=True)
        weights = jnp.where(live, jnp.exp(scores - top), 0.0)
        total = jnp.sum(weights, axis=1, keepdims=True)
        wb = weights.astype(jnp.bfloat16)
        acc = jnp.zeros((q.shape[0], lanes), jnp.float32)
        for r in range(reqs):
            acc = acc + jnp.dot(jnp.where(row // per == r, wb, jnp.zeros_like(wb)), own_vmem[r],
                                preferred_element_type=jnp.float32)
        numer = pltpu.roll(acc, half, 1)
        lane = lax.broadcasted_iota(jnp.int32, acc.shape, 1)
        alive = total > 0.0
        safe = jnp.where(alive, total, 1.0)
        level = jnp.where(alive, top + jnp.log(safe), NEG)
        own_out[...] = jnp.where(lane < half, jnp.where(alive, numer / safe, 0.0), level)

        def finish(i, c):
            peer = lax.rem(me + i, n)
            origin = lax.rem(me + n - i, n)
            pltpu.make_async_remote_copy(
                x_ref, out_ref.at[me], send_sems.at[i], recv_sems.at[i],
                device_id=(peer, keep), device_id_type=mesh_id,
            ).wait_send()
            pltpu.make_async_remote_copy(
                x_ref, out_ref.at[origin], send_sems.at[i], recv_sems.at[i],
                device_id=(origin, keep), device_id_type=mesh_id,
            ).wait_recv()
            return c

        lax.fori_loop(1, n, finish, 0)
        local.wait()
        rows_out[...] = jnp.zeros(rows_out.shape, jnp.float32)
        got = out_ref[...]
        glane = lax.broadcasted_iota(jnp.int32, (n, q_slab.shape[1]), 1)
        for r in range(reqs):
            for h in range(per):
                line = got[:, r * 2 + h // 2, :]
                if h % 2:
                    line = pltpu.roll(line, half, 1)
                rows_out[:, r, h, :] = jnp.where(glane < half, line, 0.0)

    return pl.pallas_call(
        kernel,
        out_shape=(
            jax.ShapeDtypeStruct((n,) + tuple(q_slab.shape), q_slab.dtype),
            jax.ShapeDtypeStruct((q16.shape[0], lanes), jnp.float32),
            jax.ShapeDtypeStruct((n, reqs, 8, q_slab.shape[1]), jnp.float32),
        ),
        in_specs=[pl.BlockSpec(memory_space=pltpu.VMEM)] * 2
        + [pl.BlockSpec(memory_space=pltpu.SMEM), pl.BlockSpec(memory_space=pl.ANY)],
        out_specs=(pl.BlockSpec(memory_space=pltpu.VMEM),) * 3,
        scratch_shapes=[
            pltpu.VMEM((reqs, cap, lanes), own_cache.dtype),
            pltpu.SemaphoreType.DMA((n,)),
            pltpu.SemaphoreType.DMA((n,)),
            pltpu.SemaphoreType.DMA(()),
            pltpu.SemaphoreType.DMA(()),
        ],
        compiler_params=pltpu.CompilerParams(collective_id=0, has_side_effects=True),
    )(q_slab, q16, lens16, own_cache)


def finish_kernel_call(qrows, prefix, base, req_group, jrow, pre_len, own, new, w_out, n_tok, n_kv):
    slab_rows = 16
    rows = slab_rows // 4
    groups, pre_dev, kv_lanes = prefix.shape
    window = 16 * 8
    heads = 4
    width = 64
    d_model = w_out.shape[1]
    cols = d_model // n_kv
    mesh_id = pl.DeviceIdType.MESH

    def kernel(q_ref, pre_ref, base_ref, rg_ref, j_ref, len_ref, own_ref, new_ref, w_ref, out_ref,
               recv_scr, acc_scr, part_scr, kv_recv, res_scr, packed_ref,
               tsend, trecv, ksend, krecv, loc_sems):
        me = lax.axis_index("tok")
        mk = lax.axis_index("kv")
        barrier = pltpu.get_barrier_semaphore()

        def greet_tok(i, c):
            pl.semaphore_signal(barrier, inc=1, device_id=(lax.rem(me + i, n_tok), mk), device_id_type=mesh_id)
            return c

        def greet_kv(i, c):
            pl.semaphore_signal(barrier, inc=1, device_id=(me, lax.rem(mk + i, n_kv)), device_id_type=mesh_id)
            return c

        lax.fori_loop(1, n_tok, greet_tok, 0)
        lax.fori_loop(1, n_kv, greet_kv, 0)

        glane = lax.broadcasted_iota(jnp.int32, (window, pre_dev), 1) + me * pre_dev
        olane = lax.broadcasted_iota(jnp.int32, (window, kv_lanes), 1)
        for g in range(groups):
            first = base_ref[g]
            qb = jnp.concatenate([q_ref[first + k] for k in range(window // 8)], axis=0)
            qb = qb.astype(jnp.bfloat16)
            kv = pre_ref[g]
            s = lax.dot_general(qb, kv, (((1,), (1,)), ((), ())), preferred_element_type=jnp.float32)
            s = s * SCALE
            live = glane < len_ref[g]
            s = jnp.where(live, s, NEG)
            top = jnp.max(s, axis=1, keepdims=True)
            e = jnp.where(live, jnp.exp(s - top), 0.0)
            total = jnp.sum(e, axis=1, keepdims=True)
            nm = jnp.dot(e.astype(jnp.bfloat16), kv, preferred_element_type=jnp.float32)
            nm = pltpu.roll(nm, width, 1)
            alive = total > 0.0
            safe = jnp.where(alive, total, 1.0)
            level = jnp.where(alive, top + jnp.log(safe), NEG)
            res_scr[pl.ds(g * (window // 8), window // 8)] = jnp.where(
                olane < width, jnp.where(alive, nm / safe, 0.0), level).reshape(window // 8, 8, kv_lanes)

        prow = lax.broadcasted_iota(jnp.int32, (8, kv_lanes), 0)

        def place(m, c):
            blocks = []
            for t in range(2):
                r = 2 * m + t
                blocks.append(res_scr[rg_ref[r] * (window // 8) + j_ref[r]])
            both = jnp.where(prow < 4, blocks[0], pltpu.roll(blocks[1], 4, 0))
            packed_ref[m // 2, pl.ds(pl.multiple_of((m % 2) * 8, 8), 8), :] = both
            return c

        lax.fori_loop(0, n_tok * 2, place, 0)
        pl.semaphore_wait(barrier, n_tok - 1 + n_kv - 1)

        local_copy = pltpu.make_async_copy(packed_ref.at[me], recv_scr.at[me], loc_sems.at[0])
        local_copy.start()

        def tok_copy(i, target, slot):
            return pltpu.make_async_remote_copy(
                packed_ref.at[target], recv_scr.at[slot], tsend.at[i], trecv.at[i],
                device_id=(target, mk), device_id_type=mesh_id,
            )

        def send_tok(i, c):
            tok_copy(i, lax.rem(me + i, n_tok), me).start()
            return c

        lax.fori_loop(1, n_tok, send_tok, 0)

        def finish_tok(i, c):
            tok_copy(i, lax.rem(me + i, n_tok), me).wait_send()
            origin = lax.rem(me + n_tok - i, n_tok)
            pltpu.make_async_remote_copy(
                packed_ref.at[origin], recv_scr.at[origin], tsend.at[i], trecv.at[i],
                device_id=(origin, mk), device_id_type=mesh_id,
            ).wait_recv()
            return c

        lax.fori_loop(1, n_tok, finish_tok, 0)
        local_copy.wait()

        x = recv_scr[...]
        loc = own_ref[...]
        nloc = new_ref[...]
        llane = lax.broadcasted_iota(jnp.int32, loc.shape, 1)
        big = jnp.maximum(jnp.maximum(jnp.max(x, axis=0), loc), nloc)
        keep_hi = llane >= width
        weight = jnp.where(keep_hi[None], jnp.exp(x - big[None]), 0.0)
        lweight = jnp.where(keep_hi, jnp.exp(loc - big), 0.0)
        nweight = jnp.where(keep_hi, jnp.exp(nloc - big), 0.0)
        weight = pltpu.roll(weight.reshape(-1, 128), width, 1).reshape(x.shape)
        lweight = pltpu.roll(lweight, width, 1)
        nweight = pltpu.roll(nweight, width, 1)
        denom = jnp.sum(weight, axis=0) + lweight + nweight
        numer = jnp.sum(weight * x, axis=0) + lweight * loc + nweight * nloc
        attn = jnp.where(llane < width, numer / jnp.where(llane < width, denom, 1.0), 0.0).astype(jnp.bfloat16)
        pi = lax.broadcasted_iota(jnp.int32, (slab_rows, slab_rows), 0)
        pj = lax.broadcasted_iota(jnp.int32, (slab_rows, slab_rows), 1)
        perm = jnp.where(pj == (pi % rows) * heads + pi // rows, 1.0, 0.0).astype(jnp.bfloat16)
        attn = jnp.dot(perm, attn, preferred_element_type=jnp.float32)
        shifted = pltpu.roll(attn, width, 1)
        row = lax.broadcasted_iota(jnp.int32, attn.shape, 0)
        head_of = row // rows
        acc = jnp.zeros((slab_rows, d_model), jnp.float32)
        for pair in range(heads // 2):
            lhs = jnp.where(head_of == 2 * pair, attn, jnp.where(head_of == 2 * pair + 1, shifted, 0.0))
            acc = acc + jnp.dot(
                lhs.astype(jnp.bfloat16), w_ref[pl.ds(pair * 2 * width, 2 * width), :],
                preferred_element_type=jnp.float32,
            )
        acc_scr[...] = acc
        partial = acc_scr[pl.ds(0, rows), :]
        for h in range(1, heads):
            partial = partial + acc_scr[pl.ds(h * rows, rows), :]
        part_scr[...] = partial

        def kv_src(target):
            return part_scr.at[:, pl.ds(pl.multiple_of(target * cols, cols), cols)]

        kv_local = pltpu.make_async_copy(kv_src(mk), kv_recv.at[mk], loc_sems.at[1])
        kv_local.start()

        def kv_copy(j, target, slot):
            return pltpu.make_async_remote_copy(
                kv_src(target), kv_recv.at[slot], ksend.at[j], krecv.at[j],
                device_id=(me, target), device_id_type=mesh_id,
            )

        def send_kv(j, c):
            kv_copy(j, lax.rem(mk + j, n_kv), mk).start()
            return c

        lax.fori_loop(1, n_kv, send_kv, 0)

        def finish_kv(j, c):
            kv_copy(j, lax.rem(mk + j, n_kv), mk).wait_send()
            origin = lax.rem(mk + n_kv - j, n_kv)
            pltpu.make_async_remote_copy(
                kv_src(origin), kv_recv.at[origin], ksend.at[j], krecv.at[j],
                device_id=(me, origin), device_id_type=mesh_id,
            ).wait_recv()
            return c

        lax.fori_loop(1, n_kv, finish_kv, 0)
        kv_local.wait()
        out_ref[...] = jnp.sum(kv_recv[...], axis=0).astype(out_ref.dtype)

    return pl.pallas_call(
        kernel,
        out_shape=jax.ShapeDtypeStruct((rows, cols), jnp.bfloat16),
        in_specs=[pl.BlockSpec(memory_space=pltpu.VMEM)] * 2
        + [pl.BlockSpec(memory_space=pltpu.SMEM)] * 4
        + [pl.BlockSpec(memory_space=pltpu.VMEM)] * 3,
        out_specs=pl.BlockSpec(memory_space=pltpu.VMEM),
        scratch_shapes=[
            pltpu.VMEM((n_tok, slab_rows, 128), jnp.float32),
            pltpu.VMEM((slab_rows, d_model), jnp.float32),
            pltpu.VMEM((rows, d_model), jnp.float32),
            pltpu.VMEM((n_kv, rows, cols), jnp.float32),
            pltpu.VMEM((groups * (window // 8), 8, 128), jnp.float32),
            pltpu.VMEM((n_tok, slab_rows, 128), jnp.float32),
            pltpu.SemaphoreType.DMA((n_tok,)),
            pltpu.SemaphoreType.DMA((n_tok,)),
            pltpu.SemaphoreType.DMA((n_kv,)),
            pltpu.SemaphoreType.DMA((n_kv,)),
            pltpu.SemaphoreType.DMA((2,)),
        ],
        compiler_params=pltpu.CompilerParams(collective_id=1, has_side_effects=True),
    )(qrows, prefix, base, req_group, jrow, pre_len, own, new, w_out)


def block_stats(query, keyval, live):
    width = query.shape[-1]
    keys = keyval[..., :width]
    values = keyval[..., width:]
    scores = jnp.einsum("rhge,hrpe->rhgp", query, keys, preferred_element_type=jnp.float32) * SCALE
    mask = live[:, None, None, :]
    scores = jnp.where(mask, scores, NEG)
    top = jnp.max(scores, axis=-1)
    weights = jnp.where(mask, jnp.exp(scores - top[..., None]), 0.0)
    total = jnp.sum(weights, axis=-1)
    numer = jnp.einsum(
        "rhgp,hrpe->rhge", weights.astype(jnp.bfloat16), values, preferred_element_type=jnp.float32
    )
    return (top, total, numer)


def prompt_stats(all_query, prefix_cache, req_group, pre_len, block):
    all_rows, heads, per_kv, width = all_query.shape
    groups = prefix_cache.shape[1]
    pre_dev = prefix_cache.shape[2]
    group_ids = jnp.arange(groups, dtype=jnp.int32)
    starts = jnp.sum((req_group[None, :] < group_ids[:, None]).astype(jnp.int32), axis=1)
    slot_ids = jnp.arange(SHARE, dtype=jnp.int32)
    source = jnp.minimum(starts[:, None] + slot_ids[None, :], all_rows - 1).reshape(-1)
    slotted = jnp.take(all_query, source, axis=0).reshape(groups, SHARE, heads, per_kv, width)
    keys = prefix_cache[..., :width]
    values = prefix_cache[..., width:]
    scores = (
        jnp.einsum("gshqe,hgpe->hgsqp", slotted, keys, preferred_element_type=jnp.float32) * SCALE
    )
    pre_pos = block * pre_dev + jnp.arange(pre_dev, dtype=jnp.int32)
    live = pre_pos[None, :] < pre_len[:, None]
    mask = live[None, :, None, None, :]
    scores = jnp.where(mask, scores, NEG)
    top = jnp.max(scores, axis=-1)
    weights = jnp.where(mask, jnp.exp(scores - top[..., None]), 0.0)
    total = jnp.sum(weights, axis=-1)
    numer = jnp.einsum(
        "hgsqp,hgpe->hgsqe",
        weights.astype(jnp.bfloat16),
        values,
        preferred_element_type=jnp.float32,
    )
    match = req_group[:, None] == group_ids[None, :]
    start_req = jnp.sum(jnp.where(match, starts[None, :], 0), axis=1)
    place = req_group * SHARE + jnp.arange(all_rows, dtype=jnp.int32) - start_req
    alive = total > 0.0
    safe = jnp.where(alive, total, 1.0)
    level = jnp.where(alive, top + jnp.log(safe), NEG)
    packed = jnp.concatenate(
        [jnp.where(alive[..., None], numer / safe[..., None], 0.0),
         jnp.broadcast_to(level[..., None], top.shape + (128 - width,))],
        axis=-1,
    ).reshape(heads, groups * SHARE, per_kv, 128)
    packed = jnp.take(packed, place, axis=1)
    return jnp.transpose(packed, (1, 0, 2, 3)).reshape(all_rows * heads * per_kv, 128)


def body(hidden_in, w_query, w_keyval, w_out, own_cache, prefix_cache, own_len, req_group, pre_len):
    rows = hidden_in.shape[0]
    heads = w_keyval.shape[1]
    width = w_keyval.shape[2] // 2
    per_kv = w_query.shape[1] // (heads * width)
    columns = heads * per_kv
    inputs = hidden_in.astype(jnp.float32)
    normed = (inputs * lax.rsqrt(jnp.mean(inputs * inputs, axis=1, keepdims=True) + 1e-05)).astype(
        jnp.bfloat16
    )
    query = jnp.dot(normed, w_query, preferred_element_type=jnp.float32).astype(jnp.bfloat16)
    newkv = jnp.einsum("rd,dhe->rhe", normed, w_keyval, preferred_element_type=jnp.float32).astype(
        jnp.bfloat16
    )
    n_tok = lax.axis_size("tok")
    n_kv = lax.axis_size("kv")
    q_slab = query.astype(jnp.float32).reshape(-1, 128)
    q16 = jnp.concatenate(
        [query.reshape(rows * columns, width), jnp.zeros((rows * columns, width), query.dtype)], axis=1
    )
    _, own_block, qrows = broadcast_with_own(q_slab, q16, own_len, own_cache, n_tok, SCALE)
    all_rows = n_tok * rows
    qrows = qrows.reshape(all_rows, 8, 128)
    groups = prefix_cache.shape[1]
    group_ids = jnp.arange(groups, dtype=jnp.int32)
    starts = jnp.sum((req_group[None, :] < group_ids[:, None]).astype(jnp.int32), axis=1)
    base = jnp.minimum(starts, all_rows - SHARE)
    rg = jnp.clip(req_group, 0, groups - 1)
    own_start = jnp.sum((req_group[None, :] < req_group[:, None]).astype(jnp.int32), axis=1)
    own_base = jnp.minimum(own_start, all_rows - SHARE)
    jrow = jnp.clip(jnp.arange(all_rows, dtype=jnp.int32) - own_base, 0, SHARE - 1)
    local_query = query.reshape(rows, heads, per_kv, width)
    s_new = (
        jnp.einsum(
            "rhge,rhe->rhg", local_query, newkv[..., :width], preferred_element_type=jnp.float32
        )
        * SCALE
    )
    s_new = s_new.reshape(rows, columns)
    new_value = jnp.broadcast_to(
        newkv[:, :, None, width:].astype(jnp.float32), (rows, heads, per_kv, width)
    ).reshape(rows, columns, width)
    new_block = jnp.concatenate(
        [new_value, jnp.broadcast_to(s_new[..., None], (rows, columns, 128 - width))],
        axis=-1,
    ).reshape(rows * columns, 128)
    return finish_kernel_call(qrows, prefix_cache[0], base, rg, jrow, pre_len, own_block, new_block, w_out, n_tok, n_kv)


def solution(mesh):
    in_specs = (
        P("tok", None),
        P(None, "kv"),
        P(None, "kv", None),
        P("kv", None),
        P("kv", "tok", None, None),
        P("kv", None, "tok", None),
        P("tok"),
        P(),
        P(),
    )
    out_specs = P("tok", "kv")
    return jax.shard_map(body, mesh=mesh, in_specs=in_specs, out_specs=out_specs, check_vma=False)
```

```python
import jax
import jax.numpy as jnp
from jax import lax
from jax.sharding import PartitionSpec as P
from jax.experimental import pallas as pl
from jax.experimental.pallas import tpu as pltpu

SHARE = 16


SCALE = 0.015625
NEG = -1e30


def exchange(slabs, axis, other, n, broadcast, cid):
    slab_shape = slabs.shape[1:] if not broadcast else slabs.shape
    mesh_id = pl.DeviceIdType.MESH

    def kernel(x_ref, out_ref, send_sems, recv_sems, local_sem):
        me = lax.axis_index(axis)
        keep = lax.axis_index(other)

        def dev(peer):
            return (peer, keep) if axis == "tok" else (keep, peer)

        def src(peer):
            return x_ref if broadcast else x_ref.at[peer]

        barrier = pltpu.get_barrier_semaphore()

        def greet(i, c):
            peer = lax.rem(me + i, n)
            pl.semaphore_signal(barrier, inc=1, device_id=dev(peer), device_id_type=mesh_id)
            return c

        lax.fori_loop(1, n, greet, 0)
        pl.semaphore_wait(barrier, n - 1)
        local = pltpu.make_async_copy(src(me), out_ref.at[me], local_sem)
        local.start()

        def send(i, c):
            peer = lax.rem(me + i, n)
            pltpu.make_async_remote_copy(
                src(peer), out_ref.at[me], send_sems.at[i], recv_sems.at[i],
                device_id=dev(peer), device_id_type=mesh_id,
            ).start()
            return c

        lax.fori_loop(1, n, send, 0)

        def finish(i, c):
            peer = lax.rem(me + i, n)
            origin = lax.rem(me + n - i, n)
            pltpu.make_async_remote_copy(
                src(peer), out_ref.at[me], send_sems.at[i], recv_sems.at[i],
                device_id=dev(peer), device_id_type=mesh_id,
            ).wait_send()
            pltpu.make_async_remote_copy(
                src(peer), out_ref.at[origin], send_sems.at[i], recv_sems.at[i],
                device_id=dev(origin), device_id_type=mesh_id,
            ).wait_recv()
            return c

        lax.fori_loop(1, n, finish, 0)
        local.wait()

    return pl.pallas_call(
        kernel,
        out_shape=jax.ShapeDtypeStruct((n,) + tuple(slab_shape), slabs.dtype),
        in_specs=[pl.BlockSpec(memory_space=pltpu.VMEM)],
        out_specs=pl.BlockSpec(memory_space=pltpu.VMEM),
        scratch_shapes=[
            pltpu.SemaphoreType.DMA((n,)),
            pltpu.SemaphoreType.DMA((n,)),
            pltpu.SemaphoreType.DMA(()),
        ],
        compiler_params=pltpu.CompilerParams(collective_id=cid, has_side_effects=True),
    )(slabs)


def broadcast_with_own(q_slab, q16, lens16, own_cache, n, scale):
    mesh_id = pl.DeviceIdType.MESH
    reqs, cap, lanes = own_cache.shape[1:]
    half = lanes // 2
    per = q16.shape[0] // reqs

    def kernel(x_ref, q_ref, len_ref, own_hbm, out_ref, own_out, own_vmem,
               send_sems, recv_sems, local_sem, own_sem):
        me = lax.axis_index("tok")
        keep = lax.axis_index("kv")
        own_copy = pltpu.make_async_copy(own_hbm.at[0], own_vmem, own_sem)
        own_copy.start()
        barrier = pltpu.get_barrier_semaphore()

        def greet(i, c):
            pl.semaphore_signal(barrier, inc=1, device_id=(lax.rem(me + i, n), keep), device_id_type=mesh_id)
            return c

        lax.fori_loop(1, n, greet, 0)
        pl.semaphore_wait(barrier, n - 1)
        local = pltpu.make_async_copy(x_ref, out_ref.at[me], local_sem)
        local.start()

        def send(i, c):
            peer = lax.rem(me + i, n)
            pltpu.make_async_remote_copy(
                x_ref, out_ref.at[me], send_sems.at[i], recv_sems.at[i],
                device_id=(peer, keep), device_id_type=mesh_id,
            ).start()
            return c

        lax.fori_loop(1, n, send, 0)
        own_copy.wait()
        q = q_ref[...]
        row = lax.broadcasted_iota(jnp.int32, (q.shape[0], cap), 0)
        pos = lax.broadcasted_iota(jnp.int32, (q.shape[0], cap), 1)
        scores = jnp.zeros((q.shape[0], cap), jnp.float32)
        for r in range(reqs):
            part = lax.dot_general(q, own_vmem[r], (((1,), (1,)), ((), ())),
                                   preferred_element_type=jnp.float32)
            scores = jnp.where(row // per == r, part, scores)
        scores = scores * scale
        row_len = jnp.zeros((q.shape[0], cap), jnp.int32)
        for r in range(reqs):
            row_len = jnp.where(row // per == r, len_ref[r], row_len)
        live = pos < row_len
        scores = jnp.where(live, scores, NEG)
        top = jnp.max(scores, axis=1, keepdims=True)
        weights = jnp.where(live, jnp.exp(scores - top), 0.0)
        total = jnp.sum(weights, axis=1, keepdims=True)
        wb = weights.astype(jnp.bfloat16)
        acc = jnp.zeros((q.shape[0], lanes), jnp.float32)
        for r in range(reqs):
            acc = acc + jnp.dot(jnp.where(row // per == r, wb, jnp.zeros_like(wb)), own_vmem[r],
                                preferred_element_type=jnp.float32)
        numer = pltpu.roll(acc, half, 1)
        lane = lax.broadcasted_iota(jnp.int32, acc.shape, 1)
        alive = total > 0.0
        safe = jnp.where(alive, total, 1.0)
        level = jnp.where(alive, top + jnp.log(safe), NEG)
        own_out[...] = jnp.where(lane < half, jnp.where(alive, numer / safe, 0.0), level)

        def finish(i, c):
            peer = lax.rem(me + i, n)
            origin = lax.rem(me + n - i, n)
            pltpu.make_async_remote_copy(
                x_ref, out_ref.at[me], send_sems.at[i], recv_sems.at[i],
                device_id=(peer, keep), device_id_type=mesh_id,
            ).wait_send()
            pltpu.make_async_remote_copy(
                x_ref, out_ref.at[origin], send_sems.at[i], recv_sems.at[i],
                device_id=(origin, keep), device_id_type=mesh_id,
            ).wait_recv()
            return c

        lax.fori_loop(1, n, finish, 0)
        local.wait()

    return pl.pallas_call(
        kernel,
        out_shape=(
            jax.ShapeDtypeStruct((n,) + tuple(q_slab.shape), q_slab.dtype),
            jax.ShapeDtypeStruct((q16.shape[0], lanes), jnp.float32),
        ),
        in_specs=[pl.BlockSpec(memory_space=pltpu.VMEM)] * 2
        + [pl.BlockSpec(memory_space=pltpu.SMEM), pl.BlockSpec(memory_space=pl.ANY)],
        out_specs=(pl.BlockSpec(memory_space=pltpu.VMEM), pl.BlockSpec(memory_space=pltpu.VMEM)),
        scratch_shapes=[
            pltpu.VMEM((reqs, cap, lanes), own_cache.dtype),
            pltpu.SemaphoreType.DMA((n,)),
            pltpu.SemaphoreType.DMA((n,)),
            pltpu.SemaphoreType.DMA(()),
            pltpu.SemaphoreType.DMA(()),
        ],
        compiler_params=pltpu.CompilerParams(collective_id=0, has_side_effects=True),
    )(q_slab, q16, lens16, own_cache)


def finish_kernel_call(qrows, prefix, base, req_group, jrow, pre_len, own, new, w_out, n_tok, n_kv):
    slab_rows = 16
    rows = slab_rows // 4
    groups, pre_dev, kv_lanes = prefix.shape
    window = 16 * 8
    heads = 4
    width = 64
    d_model = w_out.shape[1]
    cols = d_model // n_kv
    mesh_id = pl.DeviceIdType.MESH

    def kernel(q_ref, pre_hbm, base_ref, rg_ref, j_ref, len_ref, own_ref, new_ref, w_hbm, out_ref,
               recv_scr, acc_scr, part_scr, kv_recv, res_scr, packed_ref, pre_ref, w_ref,
               tsend, trecv, ksend, krecv, loc_sems, in_sems):
        me = lax.axis_index("tok")
        mk = lax.axis_index("kv")
        barrier = pltpu.get_barrier_semaphore()

        def greet_tok(i, c):
            pl.semaphore_signal(barrier, inc=1, device_id=(lax.rem(me + i, n_tok), mk), device_id_type=mesh_id)
            return c

        def greet_kv(i, c):
            pl.semaphore_signal(barrier, inc=1, device_id=(me, lax.rem(mk + i, n_kv)), device_id_type=mesh_id)
            return c

        lax.fori_loop(1, n_tok, greet_tok, 0)
        lax.fori_loop(1, n_kv, greet_kv, 0)
        pre_copy = pltpu.make_async_copy(pre_hbm, pre_ref, in_sems.at[0])
        pre_copy.start()
        w_copy = pltpu.make_async_copy(w_hbm, w_ref, in_sems.at[1])
        w_copy.start()
        pre_copy.wait()

        glane = lax.broadcasted_iota(jnp.int32, (window, pre_dev), 1) + me * pre_dev
        olane = lax.broadcasted_iota(jnp.int32, (window, kv_lanes), 1)
        for g in range(groups):
            first = base_ref[g]
            qb = jnp.concatenate([q_ref[first + k] for k in range(window // 8)], axis=0)
            qb = qb.astype(jnp.bfloat16)
            kv = pre_ref[g]
            s = lax.dot_general(qb, kv, (((1,), (1,)), ((), ())), preferred_element_type=jnp.float32)
            s = s * SCALE
            live = glane < len_ref[g]
            s = jnp.where(live, s, NEG)
            top = jnp.max(s, axis=1, keepdims=True)
            e = jnp.where(live, jnp.exp(s - top), 0.0)
            total = jnp.sum(e, axis=1, keepdims=True)
            nm = jnp.dot(e.astype(jnp.bfloat16), kv, preferred_element_type=jnp.float32)
            nm = pltpu.roll(nm, width, 1)
            alive = total > 0.0
            safe = jnp.where(alive, total, 1.0)
            level = jnp.where(alive, top + jnp.log(safe), NEG)
            res_scr[pl.ds(g * (window // 8), window // 8)] = jnp.where(
                olane < width, jnp.where(alive, nm / safe, 0.0), level).reshape(window // 8, 8, kv_lanes)

        prow = lax.broadcasted_iota(jnp.int32, (8, kv_lanes), 0)

        def place(m, c):
            blocks = []
            for t in range(2):
                r = 2 * m + t
                blocks.append(res_scr[rg_ref[r] * (window // 8) + j_ref[r]])
            both = jnp.where(prow < 4, blocks[0], pltpu.roll(blocks[1], 4, 0))
            packed_ref[m // 2, pl.ds(pl.multiple_of((m % 2) * 8, 8), 8), :] = both
            return c

        lax.fori_loop(0, n_tok * 2, place, 0)
        pl.semaphore_wait(barrier, n_tok - 1 + n_kv - 1)

        local_copy = pltpu.make_async_copy(packed_ref.at[me], recv_scr.at[me], loc_sems.at[0])
        local_copy.start()

        def tok_copy(i, target, slot):
            return pltpu.make_async_remote_copy(
                packed_ref.at[target], recv_scr.at[slot], tsend.at[i], trecv.at[i],
                device_id=(target, mk), device_id_type=mesh_id,
            )

        def send_tok(i, c):
            tok_copy(i, lax.rem(me + i, n_tok), me).start()
            return c

        lax.fori_loop(1, n_tok, send_tok, 0)

        def finish_tok(i, c):
            tok_copy(i, lax.rem(me + i, n_tok), me).wait_send()
            origin = lax.rem(me + n_tok - i, n_tok)
            pltpu.make_async_remote_copy(
                packed_ref.at[origin], recv_scr.at[origin], tsend.at[i], trecv.at[i],
                device_id=(origin, mk), device_id_type=mesh_id,
            ).wait_recv()
            return c

        lax.fori_loop(1, n_tok, finish_tok, 0)
        local_copy.wait()

        x = recv_scr[...]
        loc = own_ref[...]
        nloc = new_ref[...]
        llane = lax.broadcasted_iota(jnp.int32, loc.shape, 1)
        big = jnp.maximum(jnp.maximum(jnp.max(x, axis=0), loc), nloc)
        keep_hi = llane >= width
        weight = jnp.where(keep_hi[None], jnp.exp(x - big[None]), 0.0)
        lweight = jnp.where(keep_hi, jnp.exp(loc - big), 0.0)
        nweight = jnp.where(keep_hi, jnp.exp(nloc - big), 0.0)
        weight = pltpu.roll(weight.reshape(-1, 128), width, 1).reshape(x.shape)
        lweight = pltpu.roll(lweight, width, 1)
        nweight = pltpu.roll(nweight, width, 1)
        denom = jnp.sum(weight, axis=0) + lweight + nweight
        numer = jnp.sum(weight * x, axis=0) + lweight * loc + nweight * nloc
        attn = jnp.where(llane < width, numer / jnp.where(llane < width, denom, 1.0), 0.0).astype(jnp.bfloat16)
        pi = lax.broadcasted_iota(jnp.int32, (slab_rows, slab_rows), 0)
        pj = lax.broadcasted_iota(jnp.int32, (slab_rows, slab_rows), 1)
        perm = jnp.where(pj == (pi % rows) * heads + pi // rows, 1.0, 0.0).astype(jnp.bfloat16)
        attn = jnp.dot(perm, attn, preferred_element_type=jnp.float32)
        shifted = pltpu.roll(attn, width, 1)
        row = lax.broadcasted_iota(jnp.int32, attn.shape, 0)
        head_of = row // rows
        w_copy.wait()
        acc = jnp.zeros((slab_rows, d_model), jnp.float32)
        for pair in range(heads // 2):
            lhs = jnp.where(head_of == 2 * pair, attn, jnp.where(head_of == 2 * pair + 1, shifted, 0.0))
            acc = acc + jnp.dot(
                lhs.astype(jnp.bfloat16), w_ref[pl.ds(pair * 2 * width, 2 * width), :],
                preferred_element_type=jnp.float32,
            )
        acc_scr[...] = acc
        partial = acc_scr[pl.ds(0, rows), :]
        for h in range(1, heads):
            partial = partial + acc_scr[pl.ds(h * rows, rows), :]
        part_scr[...] = partial

        def kv_src(target):
            return part_scr.at[:, pl.ds(pl.multiple_of(target * cols, cols), cols)]

        kv_local = pltpu.make_async_copy(kv_src(mk), kv_recv.at[mk], loc_sems.at[1])
        kv_local.start()

        def kv_copy(j, target, slot):
            return pltpu.make_async_remote_copy(
                kv_src(target), kv_recv.at[slot], ksend.at[j], krecv.at[j],
                device_id=(me, target), device_id_type=mesh_id,
            )

        def send_kv(j, c):
            kv_copy(j, lax.rem(mk + j, n_kv), mk).start()
            return c

        lax.fori_loop(1, n_kv, send_kv, 0)

        def finish_kv(j, c):
            kv_copy(j, lax.rem(mk + j, n_kv), mk).wait_send()
            origin = lax.rem(mk + n_kv - j, n_kv)
            pltpu.make_async_remote_copy(
                kv_src(origin), kv_recv.at[origin], ksend.at[j], krecv.at[j],
                device_id=(me, origin), device_id_type=mesh_id,
            ).wait_recv()
            return c

        lax.fori_loop(1, n_kv, finish_kv, 0)
        kv_local.wait()
        out_ref[...] = jnp.sum(kv_recv[...], axis=0).astype(out_ref.dtype)

    return pl.pallas_call(
        kernel,
        out_shape=jax.ShapeDtypeStruct((rows, cols), jnp.bfloat16),
        in_specs=[pl.BlockSpec(memory_space=pltpu.VMEM), pl.BlockSpec(memory_space=pl.ANY)]
        + [pl.BlockSpec(memory_space=pltpu.SMEM)] * 4
        + [pl.BlockSpec(memory_space=pltpu.VMEM)] * 2 + [pl.BlockSpec(memory_space=pl.ANY)],
        out_specs=pl.BlockSpec(memory_space=pltpu.VMEM),
        scratch_shapes=[
            pltpu.VMEM((n_tok, slab_rows, 128), jnp.float32),
            pltpu.VMEM((slab_rows, d_model), jnp.float32),
            pltpu.VMEM((rows, d_model), jnp.float32),
            pltpu.VMEM((n_kv, rows, cols), jnp.float32),
            pltpu.VMEM((groups * (window // 8), 8, 128), jnp.float32),
            pltpu.VMEM((n_tok, slab_rows, 128), jnp.float32),
            pltpu.VMEM(prefix.shape, prefix.dtype),
            pltpu.VMEM(w_out.shape, w_out.dtype),
            pltpu.SemaphoreType.DMA((n_tok,)),
            pltpu.SemaphoreType.DMA((n_tok,)),
            pltpu.SemaphoreType.DMA((n_kv,)),
            pltpu.SemaphoreType.DMA((n_kv,)),
            pltpu.SemaphoreType.DMA((2,)),
            pltpu.SemaphoreType.DMA((2,)),
        ],
        compiler_params=pltpu.CompilerParams(collective_id=1, has_side_effects=True),
    )(qrows, prefix, base, req_group, jrow, pre_len, own, new, w_out)


def block_stats(query, keyval, live):
    width = query.shape[-1]
    keys = keyval[..., :width]
    values = keyval[..., width:]
    scores = jnp.einsum("rhge,hrpe->rhgp", query, keys, preferred_element_type=jnp.float32) * SCALE
    mask = live[:, None, None, :]
    scores = jnp.where(mask, scores, NEG)
    top = jnp.max(scores, axis=-1)
    weights = jnp.where(mask, jnp.exp(scores - top[..., None]), 0.0)
    total = jnp.sum(weights, axis=-1)
    numer = jnp.einsum(
        "rhgp,hrpe->rhge", weights.astype(jnp.bfloat16), values, preferred_element_type=jnp.float32
    )
    return (top, total, numer)


def prompt_stats(all_query, prefix_cache, req_group, pre_len, block):
    all_rows, heads, per_kv, width = all_query.shape
    groups = prefix_cache.shape[1]
    pre_dev = prefix_cache.shape[2]
    group_ids = jnp.arange(groups, dtype=jnp.int32)
    starts = jnp.sum((req_group[None, :] < group_ids[:, None]).astype(jnp.int32), axis=1)
    slot_ids = jnp.arange(SHARE, dtype=jnp.int32)
    source = jnp.minimum(starts[:, None] + slot_ids[None, :], all_rows - 1).reshape(-1)
    slotted = jnp.take(all_query, source, axis=0).reshape(groups, SHARE, heads, per_kv, width)
    keys = prefix_cache[..., :width]
    values = prefix_cache[..., width:]
    scores = (
        jnp.einsum("gshqe,hgpe->hgsqp", slotted, keys, preferred_element_type=jnp.float32) * SCALE
    )
    pre_pos = block * pre_dev + jnp.arange(pre_dev, dtype=jnp.int32)
    live = pre_pos[None, :] < pre_len[:, None]
    mask = live[None, :, None, None, :]
    scores = jnp.where(mask, scores, NEG)
    top = jnp.max(scores, axis=-1)
    weights = jnp.where(mask, jnp.exp(scores - top[..., None]), 0.0)
    total = jnp.sum(weights, axis=-1)
    numer = jnp.einsum(
        "hgsqp,hgpe->hgsqe",
        weights.astype(jnp.bfloat16),
        values,
        preferred_element_type=jnp.float32,
    )
    match = req_group[:, None] == group_ids[None, :]
    start_req = jnp.sum(jnp.where(match, starts[None, :], 0), axis=1)
    place = req_group * SHARE + jnp.arange(all_rows, dtype=jnp.int32) - start_req
    alive = total > 0.0
    safe = jnp.where(alive, total, 1.0)
    level = jnp.where(alive, top + jnp.log(safe), NEG)
    packed = jnp.concatenate(
        [jnp.where(alive[..., None], numer / safe[..., None], 0.0),
         jnp.broadcast_to(level[..., None], top.shape + (128 - width,))],
        axis=-1,
    ).reshape(heads, groups * SHARE, per_kv, 128)
    packed = jnp.take(packed, place, axis=1)
    return jnp.transpose(packed, (1, 0, 2, 3)).reshape(all_rows * heads * per_kv, 128)


def body(hidden_in, w_query, w_keyval, w_out, own_cache, prefix_cache, own_len, req_group, pre_len):
    rows = hidden_in.shape[0]
    heads = w_keyval.shape[1]
    width = w_keyval.shape[2] // 2
    per_kv = w_query.shape[1] // (heads * width)
    columns = heads * per_kv
    inputs = hidden_in.astype(jnp.float32)
    normed = (inputs * lax.rsqrt(jnp.mean(inputs * inputs, axis=1, keepdims=True) + 1e-05)).astype(
        jnp.bfloat16
    )
    query = jnp.dot(normed, w_query, preferred_element_type=jnp.float32).astype(jnp.bfloat16)
    newkv = jnp.einsum("rd,dhe->rhe", normed, w_keyval, preferred_element_type=jnp.float32).astype(
        jnp.bfloat16
    )
    n_tok = lax.axis_size("tok")
    n_kv = lax.axis_size("kv")
    q_slab = query.reshape(-1, 128)
    q16 = jnp.concatenate(
        [query.reshape(rows * columns, width), jnp.zeros((rows * columns, width), query.dtype)], axis=1
    )
    gathered, own_block = broadcast_with_own(q_slab, q16, own_len, own_cache, n_tok, SCALE)
    gathered = gathered.reshape(n_tok * rows, -1)
    all_rows = gathered.shape[0]
    qrows = jnp.concatenate(
        [gathered.reshape(all_rows, columns, width).astype(jnp.float32),
         jnp.zeros((all_rows, columns, 128 - width), jnp.float32)], axis=2)
    qrows = jnp.concatenate([qrows, jnp.zeros((all_rows, 8 - columns, 128), jnp.float32)], axis=1)
    groups = prefix_cache.shape[1]
    group_ids = jnp.arange(groups, dtype=jnp.int32)
    starts = jnp.sum((req_group[None, :] < group_ids[:, None]).astype(jnp.int32), axis=1)
    base = jnp.minimum(starts, all_rows - SHARE)
    rg = jnp.clip(req_group, 0, groups - 1)
    own_start = jnp.sum((req_group[None, :] < req_group[:, None]).astype(jnp.int32), axis=1)
    own_base = jnp.minimum(own_start, all_rows - SHARE)
    jrow = jnp.clip(jnp.arange(all_rows, dtype=jnp.int32) - own_base, 0, SHARE - 1)
    local_query = query.reshape(rows, heads, per_kv, width)
    s_new = (
        jnp.einsum(
            "rhge,rhe->rhg", local_query, newkv[..., :width], preferred_element_type=jnp.float32
        )
        * SCALE
    )
    s_new = s_new.reshape(rows, columns)
    new_value = jnp.broadcast_to(
        newkv[:, :, None, width:].astype(jnp.float32), (rows, heads, per_kv, width)
    ).reshape(rows, columns, width)
    new_block = jnp.concatenate(
        [new_value, jnp.broadcast_to(s_new[..., None], (rows, columns, 128 - width))],
        axis=-1,
    ).reshape(rows * columns, 128)
    return finish_kernel_call(qrows, prefix_cache[0], base, rg, jrow, pre_len, own_block, new_block, w_out, n_tok, n_kv)


def solution(mesh):
    in_specs = (
        P("tok", None),
        P(None, "kv"),
        P(None, "kv", None),
        P("kv", None),
        P("kv", "tok", None, None),
        P("kv", None, "tok", None),
        P("tok"),
        P(),
        P(),
    )
    out_specs = P("tok", "kv")
    return jax.shard_map(body, mesh=mesh, in_specs=in_specs, out_specs=out_specs, check_vma=False)
```

```python
import jax
import jax.numpy as jnp
from jax import lax
from jax.sharding import PartitionSpec as P
from jax.experimental import pallas as pl
from jax.experimental.pallas import tpu as pltpu

SHARE = 16


SCALE = 0.015625
NEG = -1e30


def exchange(slabs, axis, other, n, broadcast, cid):
    slab_shape = slabs.shape[1:] if not broadcast else slabs.shape
    mesh_id = pl.DeviceIdType.MESH

    def kernel(x_ref, out_ref, send_sems, recv_sems, local_sem):
        me = lax.axis_index(axis)
        keep = lax.axis_index(other)

        def dev(peer):
            return (peer, keep) if axis == "tok" else (keep, peer)

        def src(peer):
            return x_ref if broadcast else x_ref.at[peer]

        barrier = pltpu.get_barrier_semaphore()

        def greet(i, c):
            peer = lax.rem(me + i, n)
            pl.semaphore_signal(barrier, inc=1, device_id=dev(peer), device_id_type=mesh_id)
            return c

        lax.fori_loop(1, n, greet, 0)
        pl.semaphore_wait(barrier, n - 1)
        local = pltpu.make_async_copy(src(me), out_ref.at[me], local_sem)
        local.start()

        def send(i, c):
            peer = lax.rem(me + i, n)
            pltpu.make_async_remote_copy(
                src(peer), out_ref.at[me], send_sems.at[i], recv_sems.at[i],
                device_id=dev(peer), device_id_type=mesh_id,
            ).start()
            return c

        lax.fori_loop(1, n, send, 0)

        def finish(i, c):
            peer = lax.rem(me + i, n)
            origin = lax.rem(me + n - i, n)
            pltpu.make_async_remote_copy(
                src(peer), out_ref.at[me], send_sems.at[i], recv_sems.at[i],
                device_id=dev(peer), device_id_type=mesh_id,
            ).wait_send()
            pltpu.make_async_remote_copy(
                src(peer), out_ref.at[origin], send_sems.at[i], recv_sems.at[i],
                device_id=dev(origin), device_id_type=mesh_id,
            ).wait_recv()
            return c

        lax.fori_loop(1, n, finish, 0)
        local.wait()

    return pl.pallas_call(
        kernel,
        out_shape=jax.ShapeDtypeStruct((n,) + tuple(slab_shape), slabs.dtype),
        in_specs=[pl.BlockSpec(memory_space=pltpu.VMEM)],
        out_specs=pl.BlockSpec(memory_space=pltpu.VMEM),
        scratch_shapes=[
            pltpu.SemaphoreType.DMA((n,)),
            pltpu.SemaphoreType.DMA((n,)),
            pltpu.SemaphoreType.DMA(()),
        ],
        compiler_params=pltpu.CompilerParams(collective_id=cid, has_side_effects=True),
    )(slabs)


def broadcast_with_own(q_slab, q16, lens16, own_cache, n, scale):
    mesh_id = pl.DeviceIdType.MESH
    reqs, cap, lanes = own_cache.shape[1:]
    half = lanes // 2
    per = q16.shape[0] // reqs

    def kernel(x_ref, q_ref, len_ref, own_hbm, out_ref, own_out, own_vmem,
               send_sems, recv_sems, local_sem, own_sem):
        me = lax.axis_index("tok")
        keep = lax.axis_index("kv")
        own_copy = pltpu.make_async_copy(own_hbm.at[0], own_vmem, own_sem)
        own_copy.start()
        barrier = pltpu.get_barrier_semaphore()

        def greet(i, c):
            pl.semaphore_signal(barrier, inc=1, device_id=(lax.rem(me + i, n), keep), device_id_type=mesh_id)
            return c

        lax.fori_loop(1, n, greet, 0)
        pl.semaphore_wait(barrier, n - 1)
        local = pltpu.make_async_copy(x_ref, out_ref.at[me], local_sem)
        local.start()

        def send(i, c):
            peer = lax.rem(me + i, n)
            pltpu.make_async_remote_copy(
                x_ref, out_ref.at[me], send_sems.at[i], recv_sems.at[i],
                device_id=(peer, keep), device_id_type=mesh_id,
            ).start()
            return c

        lax.fori_loop(1, n, send, 0)
        own_copy.wait()
        q = q_ref[...]
        row = lax.broadcasted_iota(jnp.int32, (q.shape[0], cap), 0)
        pos = lax.broadcasted_iota(jnp.int32, (q.shape[0], cap), 1)
        scores = jnp.zeros((q.shape[0], cap), jnp.float32)
        for r in range(reqs):
            part = lax.dot_general(q, own_vmem[r], (((1,), (1,)), ((), ())),
                                   preferred_element_type=jnp.float32)
            scores = jnp.where(row // per == r, part, scores)
        scores = scores * scale
        row_len = jnp.zeros((q.shape[0], cap), jnp.int32)
        for r in range(reqs):
            row_len = jnp.where(row // per == r, len_ref[r], row_len)
        live = pos < row_len
        scores = jnp.where(live, scores, NEG)
        top = jnp.max(scores, axis=1, keepdims=True)
        weights = jnp.where(live, jnp.exp(scores - top), 0.0)
        total = jnp.sum(weights, axis=1, keepdims=True)
        wb = weights.astype(jnp.bfloat16)
        acc = jnp.zeros((q.shape[0], lanes), jnp.float32)
        for r in range(reqs):
            acc = acc + jnp.dot(jnp.where(row // per == r, wb, jnp.zeros_like(wb)), own_vmem[r],
                                preferred_element_type=jnp.float32)
        numer = pltpu.roll(acc, half, 1)
        lane = lax.broadcasted_iota(jnp.int32, acc.shape, 1)
        alive = total > 0.0
        safe = jnp.where(alive, total, 1.0)
        level = jnp.where(alive, top + jnp.log(safe), NEG)
        own_out[...] = jnp.where(lane < half, jnp.where(alive, numer / safe, 0.0), level)

        def finish(i, c):
            peer = lax.rem(me + i, n)
            origin = lax.rem(me + n - i, n)
            pltpu.make_async_remote_copy(
                x_ref, out_ref.at[me], send_sems.at[i], recv_sems.at[i],
                device_id=(peer, keep), device_id_type=mesh_id,
            ).wait_send()
            pltpu.make_async_remote_copy(
                x_ref, out_ref.at[origin], send_sems.at[i], recv_sems.at[i],
                device_id=(origin, keep), device_id_type=mesh_id,
            ).wait_recv()
            return c

        lax.fori_loop(1, n, finish, 0)
        local.wait()

    return pl.pallas_call(
        kernel,
        out_shape=(
            jax.ShapeDtypeStruct((n,) + tuple(q_slab.shape), q_slab.dtype),
            jax.ShapeDtypeStruct((q16.shape[0], lanes), jnp.float32),
        ),
        in_specs=[pl.BlockSpec(memory_space=pltpu.VMEM)] * 2
        + [pl.BlockSpec(memory_space=pltpu.SMEM), pl.BlockSpec(memory_space=pl.ANY)],
        out_specs=(pl.BlockSpec(memory_space=pltpu.VMEM), pl.BlockSpec(memory_space=pltpu.VMEM)),
        scratch_shapes=[
            pltpu.VMEM((reqs, cap, lanes), own_cache.dtype),
            pltpu.SemaphoreType.DMA((n,)),
            pltpu.SemaphoreType.DMA((n,)),
            pltpu.SemaphoreType.DMA(()),
            pltpu.SemaphoreType.DMA(()),
        ],
        compiler_params=pltpu.CompilerParams(collective_id=0, has_side_effects=True),
    )(q_slab, q16, lens16, own_cache)


def finish_kernel_call(q_slab, q16, own_len, own_cache, prefix, base, req_group, jrow, pre_len, new, w_out, n_tok, n_kv):
    slab_rows = 16
    rows = slab_rows // 4
    groups, pre_dev, kv_lanes = prefix.shape
    window = 16 * 8
    heads = 4
    width = 64
    d_model = w_out.shape[1]
    cols = d_model // n_kv
    mesh_id = pl.DeviceIdType.MESH

    reqs, cap, lanes = own_cache.shape[1:]
    per = q16.shape[0] // reqs

    def kernel(x_ref, q16_ref, olen_ref, own_hbm, pre_ref, base_ref, rg_ref, j_ref, len_ref, new_ref, w_ref,
               out_ref, recv_scr, acc_scr, part_scr, kv_recv, res_scr, packed_ref,
               qrecv, qrows_scr, own_vmem, own_ref,
               tsend, trecv, ksend, krecv, loc_sems, qsend, qrsem, extra_sems):
        me = lax.axis_index("tok")
        mk = lax.axis_index("kv")
        barrier = pltpu.get_barrier_semaphore()

        def greet_tok(i, c):
            pl.semaphore_signal(barrier, inc=1, device_id=(lax.rem(me + i, n_tok), mk), device_id_type=mesh_id)
            return c

        def greet_kv(i, c):
            pl.semaphore_signal(barrier, inc=1, device_id=(me, lax.rem(mk + i, n_kv)), device_id_type=mesh_id)
            return c

        own_copy = pltpu.make_async_copy(own_hbm.at[0], own_vmem, extra_sems.at[0])
        own_copy.start()
        lax.fori_loop(1, n_tok, greet_tok, 0)
        lax.fori_loop(1, n_kv, greet_kv, 0)
        pl.semaphore_wait(barrier, n_tok - 1 + n_kv - 1)
        qlocal = pltpu.make_async_copy(x_ref, qrecv.at[me], extra_sems.at[1])
        qlocal.start()

        def q_copy(i, target, slot):
            return pltpu.make_async_remote_copy(
                x_ref, qrecv.at[slot], qsend.at[i], qrsem.at[i],
                device_id=(target, mk), device_id_type=mesh_id,
            )

        def send_q(i, c):
            q_copy(i, lax.rem(me + i, n_tok), me).start()
            return c

        lax.fori_loop(1, n_tok, send_q, 0)
        own_copy.wait()
        q = q16_ref[...]
        orow = lax.broadcasted_iota(jnp.int32, (q.shape[0], cap), 0)
        opos = lax.broadcasted_iota(jnp.int32, (q.shape[0], cap), 1)
        scores = jnp.zeros((q.shape[0], cap), jnp.float32)
        for r in range(reqs):
            part = lax.dot_general(q, own_vmem[r], (((1,), (1,)), ((), ())),
                                   preferred_element_type=jnp.float32)
            scores = jnp.where(orow // per == r, part, scores)
        scores = scores * SCALE
        row_len = jnp.zeros((q.shape[0], cap), jnp.int32)
        for r in range(reqs):
            row_len = jnp.where(orow // per == r, olen_ref[r], row_len)
        olive = opos < row_len
        scores = jnp.where(olive, scores, NEG)
        otop = jnp.max(scores, axis=1, keepdims=True)
        oweights = jnp.where(olive, jnp.exp(scores - otop), 0.0)
        ototal = jnp.sum(oweights, axis=1, keepdims=True)
        owb = oweights.astype(jnp.bfloat16)
        oacc = jnp.zeros((q.shape[0], lanes), jnp.float32)
        for r in range(reqs):
            oacc = oacc + jnp.dot(jnp.where(orow // per == r, owb, jnp.zeros_like(owb)), own_vmem[r],
                                  preferred_element_type=jnp.float32)
        onumer = pltpu.roll(oacc, width, 1)
        olane2 = lax.broadcasted_iota(jnp.int32, oacc.shape, 1)
        oalive = ototal > 0.0
        osafe = jnp.where(oalive, ototal, 1.0)
        olevel = jnp.where(oalive, otop + jnp.log(osafe), NEG)
        own_ref[...] = jnp.where(olane2 < width, jnp.where(oalive, onumer / osafe, 0.0), olevel)

        def finish_q(i, c):
            q_copy(i, lax.rem(me + i, n_tok), me).wait_send()
            q_copy(i, lax.rem(me + n_tok - i, n_tok), lax.rem(me + n_tok - i, n_tok)).wait_recv()
            return c

        lax.fori_loop(1, n_tok, finish_q, 0)
        qlocal.wait()
        qrows_scr[...] = jnp.zeros(qrows_scr.shape, jnp.float32)
        got = qrecv[...]
        qlane = lax.broadcasted_iota(jnp.int32, (n_tok, 128), 1)
        for r in range(reqs):
            for h in range(per):
                line = got[:, r * 2 + h // 2, :]
                if h % 2:
                    line = pltpu.roll(line, width, 1)
                qrows_scr[:, r, h, :] = jnp.where(qlane < width, line, 0.0)
        q_ref = qrows_scr.reshape(n_tok * reqs, 8, 128)

        glane = lax.broadcasted_iota(jnp.int32, (window, pre_dev), 1) + me * pre_dev
        olane = lax.broadcasted_iota(jnp.int32, (window, kv_lanes), 1)
        for g in range(groups):
            first = base_ref[g]
            qb = jnp.concatenate([q_ref[first + k] for k in range(window // 8)], axis=0)
            qb = qb.astype(jnp.bfloat16)
            kv = pre_ref[g]
            s = lax.dot_general(qb, kv, (((1,), (1,)), ((), ())), preferred_element_type=jnp.float32)
            s = s * SCALE
            live = glane < len_ref[g]
            s = jnp.where(live, s, NEG)
            top = jnp.max(s, axis=1, keepdims=True)
            e = jnp.where(live, jnp.exp(s - top), 0.0)
            total = jnp.sum(e, axis=1, keepdims=True)
            nm = jnp.dot(e.astype(jnp.bfloat16), kv, preferred_element_type=jnp.float32)
            nm = pltpu.roll(nm, width, 1)
            alive = total > 0.0
            safe = jnp.where(alive, total, 1.0)
            level = jnp.where(alive, top + jnp.log(safe), NEG)
            res_scr[pl.ds(g * (window // 8), window // 8)] = jnp.where(
                olane < width, jnp.where(alive, nm / safe, 0.0), level).reshape(window // 8, 8, kv_lanes)

        prow = lax.broadcasted_iota(jnp.int32, (8, kv_lanes), 0)

        def place(m, c):
            blocks = []
            for t in range(2):
                r = 2 * m + t
                blocks.append(res_scr[rg_ref[r] * (window // 8) + j_ref[r]])
            both = jnp.where(prow < 4, blocks[0], pltpu.roll(blocks[1], 4, 0))
            packed_ref[m // 2, pl.ds(pl.multiple_of((m % 2) * 8, 8), 8), :] = both
            return c

        lax.fori_loop(0, n_tok * 2, place, 0)

        local_copy = pltpu.make_async_copy(packed_ref.at[me], recv_scr.at[me], loc_sems.at[0])
        local_copy.start()

        def tok_copy(i, target, slot):
            return pltpu.make_async_remote_copy(
                packed_ref.at[target], recv_scr.at[slot], tsend.at[i], trecv.at[i],
                device_id=(target, mk), device_id_type=mesh_id,
            )

        def send_tok(i, c):
            tok_copy(i, lax.rem(me + i, n_tok), me).start()
            return c

        lax.fori_loop(1, n_tok, send_tok, 0)

        def finish_tok(i, c):
            tok_copy(i, lax.rem(me + i, n_tok), me).wait_send()
            origin = lax.rem(me + n_tok - i, n_tok)
            pltpu.make_async_remote_copy(
                packed_ref.at[origin], recv_scr.at[origin], tsend.at[i], trecv.at[i],
                device_id=(origin, mk), device_id_type=mesh_id,
            ).wait_recv()
            return c

        lax.fori_loop(1, n_tok, finish_tok, 0)
        local_copy.wait()

        x = recv_scr[...]
        loc = own_ref[...]
        nloc = new_ref[...]
        llane = lax.broadcasted_iota(jnp.int32, loc.shape, 1)
        big = jnp.maximum(jnp.maximum(jnp.max(x, axis=0), loc), nloc)
        keep_hi = llane >= width
        weight = jnp.where(keep_hi[None], jnp.exp(x - big[None]), 0.0)
        lweight = jnp.where(keep_hi, jnp.exp(loc - big), 0.0)
        nweight = jnp.where(keep_hi, jnp.exp(nloc - big), 0.0)
        weight = pltpu.roll(weight.reshape(-1, 128), width, 1).reshape(x.shape)
        lweight = pltpu.roll(lweight, width, 1)
        nweight = pltpu.roll(nweight, width, 1)
        denom = jnp.sum(weight, axis=0) + lweight + nweight
        numer = jnp.sum(weight * x, axis=0) + lweight * loc + nweight * nloc
        attn = jnp.where(llane < width, numer / jnp.where(llane < width, denom, 1.0), 0.0).astype(jnp.bfloat16)
        pi = lax.broadcasted_iota(jnp.int32, (slab_rows, slab_rows), 0)
        pj = lax.broadcasted_iota(jnp.int32, (slab_rows, slab_rows), 1)
        perm = jnp.where(pj == (pi % rows) * heads + pi // rows, 1.0, 0.0).astype(jnp.bfloat16)
        attn = jnp.dot(perm, attn, preferred_element_type=jnp.float32)
        shifted = pltpu.roll(attn, width, 1)
        row = lax.broadcasted_iota(jnp.int32, attn.shape, 0)
        head_of = row // rows
        acc = jnp.zeros((slab_rows, d_model), jnp.float32)
        for pair in range(heads // 2):
            lhs = jnp.where(head_of == 2 * pair, attn, jnp.where(head_of == 2 * pair + 1, shifted, 0.0))
            acc = acc + jnp.dot(
                lhs.astype(jnp.bfloat16), w_ref[pl.ds(pair * 2 * width, 2 * width), :],
                preferred_element_type=jnp.float32,
            )
        acc_scr[...] = acc
        partial = acc_scr[pl.ds(0, rows), :]
        for h in range(1, heads):
            partial = partial + acc_scr[pl.ds(h * rows, rows), :]
        part_scr[...] = partial

        def kv_src(target):
            return part_scr.at[:, pl.ds(pl.multiple_of(target * cols, cols), cols)]

        kv_local = pltpu.make_async_copy(kv_src(mk), kv_recv.at[mk], loc_sems.at[1])
        kv_local.start()

        def kv_copy(j, target, slot):
            return pltpu.make_async_remote_copy(
                kv_src(target), kv_recv.at[slot], ksend.at[j], krecv.at[j],
                device_id=(me, target), device_id_type=mesh_id,
            )

        def send_kv(j, c):
            kv_copy(j, lax.rem(mk + j, n_kv), mk).start()
            return c

        lax.fori_loop(1, n_kv, send_kv, 0)

        def finish_kv(j, c):
            kv_copy(j, lax.rem(mk + j, n_kv), mk).wait_send()
            origin = lax.rem(mk + n_kv - j, n_kv)
            pltpu.make_async_remote_copy(
                kv_src(origin), kv_recv.at[origin], ksend.at[j], krecv.at[j],
                device_id=(me, origin), device_id_type=mesh_id,
            ).wait_recv()
            return c

        lax.fori_loop(1, n_kv, finish_kv, 0)
        kv_local.wait()
        out_ref[...] = jnp.sum(kv_recv[...], axis=0).astype(out_ref.dtype)

    return pl.pallas_call(
        kernel,
        out_shape=jax.ShapeDtypeStruct((rows, cols), jnp.bfloat16),
        in_specs=[pl.BlockSpec(memory_space=pltpu.VMEM)] * 2
        + [pl.BlockSpec(memory_space=pltpu.SMEM), pl.BlockSpec(memory_space=pl.ANY),
           pl.BlockSpec(memory_space=pltpu.VMEM)]
        + [pl.BlockSpec(memory_space=pltpu.SMEM)] * 4
        + [pl.BlockSpec(memory_space=pltpu.VMEM)] * 2,
        out_specs=pl.BlockSpec(memory_space=pltpu.VMEM),
        scratch_shapes=[
            pltpu.VMEM((n_tok, slab_rows, 128), jnp.float32),
            pltpu.VMEM((slab_rows, d_model), jnp.float32),
            pltpu.VMEM((rows, d_model), jnp.float32),
            pltpu.VMEM((n_kv, rows, cols), jnp.float32),
            pltpu.VMEM((groups * (window // 8), 8, 128), jnp.float32),
            pltpu.VMEM((n_tok, slab_rows, 128), jnp.float32),
            pltpu.VMEM((n_tok,) + tuple(q_slab.shape), jnp.float32),
            pltpu.VMEM((n_tok, reqs, 8, 128), jnp.float32),
            pltpu.VMEM((reqs, cap, lanes), own_cache.dtype),
            pltpu.VMEM((slab_rows, 128), jnp.float32),
            pltpu.SemaphoreType.DMA((n_tok,)),
            pltpu.SemaphoreType.DMA((n_tok,)),
            pltpu.SemaphoreType.DMA((n_kv,)),
            pltpu.SemaphoreType.DMA((n_kv,)),
            pltpu.SemaphoreType.DMA((2,)),
            pltpu.SemaphoreType.DMA((n_tok,)),
            pltpu.SemaphoreType.DMA((n_tok,)),
            pltpu.SemaphoreType.DMA((2,)),
        ],
        compiler_params=pltpu.CompilerParams(collective_id=1, has_side_effects=True),
    )(q_slab, q16, own_len, own_cache, prefix, base, req_group, jrow, pre_len, new, w_out)


def block_stats(query, keyval, live):
    width = query.shape[-1]
    keys = keyval[..., :width]
    values = keyval[..., width:]
    scores = jnp.einsum("rhge,hrpe->rhgp", query, keys, preferred_element_type=jnp.float32) * SCALE
    mask = live[:, None, None, :]
    scores = jnp.where(mask, scores, NEG)
    top = jnp.max(scores, axis=-1)
    weights = jnp.where(mask, jnp.exp(scores - top[..., None]), 0.0)
    total = jnp.sum(weights, axis=-1)
    numer = jnp.einsum(
        "rhgp,hrpe->rhge", weights.astype(jnp.bfloat16), values, preferred_element_type=jnp.float32
    )
    return (top, total, numer)


def prompt_stats(all_query, prefix_cache, req_group, pre_len, block):
    all_rows, heads, per_kv, width = all_query.shape
    groups = prefix_cache.shape[1]
    pre_dev = prefix_cache.shape[2]
    group_ids = jnp.arange(groups, dtype=jnp.int32)
    starts = jnp.sum((req_group[None, :] < group_ids[:, None]).astype(jnp.int32), axis=1)
    slot_ids = jnp.arange(SHARE, dtype=jnp.int32)
    source = jnp.minimum(starts[:, None] + slot_ids[None, :], all_rows - 1).reshape(-1)
    slotted = jnp.take(all_query, source, axis=0).reshape(groups, SHARE, heads, per_kv, width)
    keys = prefix_cache[..., :width]
    values = prefix_cache[..., width:]
    scores = (
        jnp.einsum("gshqe,hgpe->hgsqp", slotted, keys, preferred_element_type=jnp.float32) * SCALE
    )
    pre_pos = block * pre_dev + jnp.arange(pre_dev, dtype=jnp.int32)
    live = pre_pos[None, :] < pre_len[:, None]
    mask = live[None, :, None, None, :]
    scores = jnp.where(mask, scores, NEG)
    top = jnp.max(scores, axis=-1)
    weights = jnp.where(mask, jnp.exp(scores - top[..., None]), 0.0)
    total = jnp.sum(weights, axis=-1)
    numer = jnp.einsum(
        "hgsqp,hgpe->hgsqe",
        weights.astype(jnp.bfloat16),
        values,
        preferred_element_type=jnp.float32,
    )
    match = req_group[:, None] == group_ids[None, :]
    start_req = jnp.sum(jnp.where(match, starts[None, :], 0), axis=1)
    place = req_group * SHARE + jnp.arange(all_rows, dtype=jnp.int32) - start_req
    alive = total > 0.0
    safe = jnp.where(alive, total, 1.0)
    level = jnp.where(alive, top + jnp.log(safe), NEG)
    packed = jnp.concatenate(
        [jnp.where(alive[..., None], numer / safe[..., None], 0.0),
         jnp.broadcast_to(level[..., None], top.shape + (128 - width,))],
        axis=-1,
    ).reshape(heads, groups * SHARE, per_kv, 128)
    packed = jnp.take(packed, place, axis=1)
    return jnp.transpose(packed, (1, 0, 2, 3)).reshape(all_rows * heads * per_kv, 128)


def body(hidden_in, w_query, w_keyval, w_out, own_cache, prefix_cache, own_len, req_group, pre_len):
    rows = hidden_in.shape[0]
    heads = w_keyval.shape[1]
    width = w_keyval.shape[2] // 2
    per_kv = w_query.shape[1] // (heads * width)
    columns = heads * per_kv
    inputs = hidden_in.astype(jnp.float32)
    normed = (inputs * lax.rsqrt(jnp.mean(inputs * inputs, axis=1, keepdims=True) + 1e-05)).astype(
        jnp.bfloat16
    )
    query = jnp.dot(normed, w_query, preferred_element_type=jnp.float32).astype(jnp.bfloat16)
    newkv = jnp.einsum("rd,dhe->rhe", normed, w_keyval, preferred_element_type=jnp.float32).astype(
        jnp.bfloat16
    )
    n_tok = lax.axis_size("tok")
    n_kv = lax.axis_size("kv")
    q_slab = query.astype(jnp.float32).reshape(-1, 128)
    q16 = jnp.concatenate(
        [query.reshape(rows * columns, width), jnp.zeros((rows * columns, width), query.dtype)], axis=1
    )
    all_rows = n_tok * rows
    groups = prefix_cache.shape[1]
    group_ids = jnp.arange(groups, dtype=jnp.int32)
    starts = jnp.sum((req_group[None, :] < group_ids[:, None]).astype(jnp.int32), axis=1)
    base = jnp.minimum(starts, all_rows - SHARE)
    rg = jnp.clip(req_group, 0, groups - 1)
    own_start = jnp.sum((req_group[None, :] < req_group[:, None]).astype(jnp.int32), axis=1)
    own_base = jnp.minimum(own_start, all_rows - SHARE)
    jrow = jnp.clip(jnp.arange(all_rows, dtype=jnp.int32) - own_base, 0, SHARE - 1)
    local_query = query.reshape(rows, heads, per_kv, width)
    s_new = (
        jnp.einsum(
            "rhge,rhe->rhg", local_query, newkv[..., :width], preferred_element_type=jnp.float32
        )
        * SCALE
    )
    s_new = s_new.reshape(rows, columns)
    new_value = jnp.broadcast_to(
        newkv[:, :, None, width:].astype(jnp.float32), (rows, heads, per_kv, width)
    ).reshape(rows, columns, width)
    new_block = jnp.concatenate(
        [new_value, jnp.broadcast_to(s_new[..., None], (rows, columns, 128 - width))],
        axis=-1,
    ).reshape(rows * columns, 128)
    return finish_kernel_call(q_slab, q16, own_len, own_cache, prefix_cache[0], base, rg, jrow, pre_len, new_block, w_out, n_tok, n_kv)


def solution(mesh):
    in_specs = (
        P("tok", None),
        P(None, "kv"),
        P(None, "kv", None),
        P("kv", None),
        P("kv", "tok", None, None),
        P("kv", None, "tok", None),
        P("tok"),
        P(),
        P(),
    )
    out_specs = P("tok", "kv")
    return jax.shard_map(body, mesh=mesh, in_specs=in_specs, out_specs=out_specs, check_vma=False)
```

```python
import jax
import jax.numpy as jnp
from jax import lax
from jax.sharding import PartitionSpec as P
from jax.experimental import pallas as pl
from jax.experimental.pallas import tpu as pltpu

SHARE = 16


SCALE = 0.015625
NEG = -1e30


def exchange(slabs, axis, other, n, broadcast, cid):
    slab_shape = slabs.shape[1:] if not broadcast else slabs.shape
    mesh_id = pl.DeviceIdType.MESH

    def kernel(x_ref, out_ref, send_sems, recv_sems, local_sem):
        me = lax.axis_index(axis)
        keep = lax.axis_index(other)

        def dev(peer):
            return (peer, keep) if axis == "tok" else (keep, peer)

        def src(peer):
            return x_ref if broadcast else x_ref.at[peer]

        barrier = pltpu.get_barrier_semaphore()

        def greet(i, c):
            peer = lax.rem(me + i, n)
            pl.semaphore_signal(barrier, inc=1, device_id=dev(peer), device_id_type=mesh_id)
            return c

        lax.fori_loop(1, n, greet, 0)
        pl.semaphore_wait(barrier, n - 1)
        local = pltpu.make_async_copy(src(me), out_ref.at[me], local_sem)
        local.start()

        def send(i, c):
            peer = lax.rem(me + i, n)
            pltpu.make_async_remote_copy(
                src(peer), out_ref.at[me], send_sems.at[i], recv_sems.at[i],
                device_id=dev(peer), device_id_type=mesh_id,
            ).start()
            return c

        lax.fori_loop(1, n, send, 0)

        def finish(i, c):
            peer = lax.rem(me + i, n)
            origin = lax.rem(me + n - i, n)
            pltpu.make_async_remote_copy(
                src(peer), out_ref.at[me], send_sems.at[i], recv_sems.at[i],
                device_id=dev(peer), device_id_type=mesh_id,
            ).wait_send()
            pltpu.make_async_remote_copy(
                src(peer), out_ref.at[origin], send_sems.at[i], recv_sems.at[i],
                device_id=dev(origin), device_id_type=mesh_id,
            ).wait_recv()
            return c

        lax.fori_loop(1, n, finish, 0)
        local.wait()

    return pl.pallas_call(
        kernel,
        out_shape=jax.ShapeDtypeStruct((n,) + tuple(slab_shape), slabs.dtype),
        in_specs=[pl.BlockSpec(memory_space=pltpu.VMEM)],
        out_specs=pl.BlockSpec(memory_space=pltpu.VMEM),
        scratch_shapes=[
            pltpu.SemaphoreType.DMA((n,)),
            pltpu.SemaphoreType.DMA((n,)),
            pltpu.SemaphoreType.DMA(()),
        ],
        compiler_params=pltpu.CompilerParams(collective_id=cid, has_side_effects=True),
    )(slabs)


def broadcast_with_own(q_slab, q16, lens16, own_cache, n, scale):
    mesh_id = pl.DeviceIdType.MESH
    reqs, cap, lanes = own_cache.shape[1:]
    half = lanes // 2
    per = q16.shape[0] // reqs

    def kernel(x_ref, q_ref, len_ref, own_hbm, out_ref, own_out, own_vmem,
               send_sems, recv_sems, local_sem, own_sem):
        me = lax.axis_index("tok")
        keep = lax.axis_index("kv")
        own_copy = pltpu.make_async_copy(own_hbm.at[0], own_vmem, own_sem)
        own_copy.start()
        barrier = pltpu.get_barrier_semaphore()

        def greet(i, c):
            pl.semaphore_signal(barrier, inc=1, device_id=(lax.rem(me + i, n), keep), device_id_type=mesh_id)
            return c

        lax.fori_loop(1, n, greet, 0)
        pl.semaphore_wait(barrier, n - 1)
        local = pltpu.make_async_copy(x_ref, out_ref.at[me], local_sem)
        local.start()

        def send(i, c):
            peer = lax.rem(me + i, n)
            pltpu.make_async_remote_copy(
                x_ref, out_ref.at[me], send_sems.at[i], recv_sems.at[i],
                device_id=(peer, keep), device_id_type=mesh_id,
            ).start()
            return c

        lax.fori_loop(1, n, send, 0)
        own_copy.wait()
        q = q_ref[...]
        row = lax.broadcasted_iota(jnp.int32, (q.shape[0], cap), 0)
        pos = lax.broadcasted_iota(jnp.int32, (q.shape[0], cap), 1)
        scores = jnp.zeros((q.shape[0], cap), jnp.float32)
        for r in range(reqs):
            part = lax.dot_general(q, own_vmem[r], (((1,), (1,)), ((), ())),
                                   preferred_element_type=jnp.float32)
            scores = jnp.where(row // per == r, part, scores)
        scores = scores * scale
        row_len = jnp.zeros((q.shape[0], cap), jnp.int32)
        for r in range(reqs):
            row_len = jnp.where(row // per == r, len_ref[r], row_len)
        live = pos < row_len
        scores = jnp.where(live, scores, NEG)
        top = jnp.max(scores, axis=1, keepdims=True)
        weights = jnp.where(live, jnp.exp(scores - top), 0.0)
        total = jnp.sum(weights, axis=1, keepdims=True)
        wb = weights.astype(jnp.bfloat16)
        acc = jnp.zeros((q.shape[0], lanes), jnp.float32)
        for r in range(reqs):
            acc = acc + jnp.dot(jnp.where(row // per == r, wb, jnp.zeros_like(wb)), own_vmem[r],
                                preferred_element_type=jnp.float32)
        numer = pltpu.roll(acc, half, 1)
        lane = lax.broadcasted_iota(jnp.int32, acc.shape, 1)
        alive = total > 0.0
        safe = jnp.where(alive, total, 1.0)
        level = jnp.where(alive, top + jnp.log(safe), NEG)
        own_out[...] = jnp.where(lane < half, jnp.where(alive, numer / safe, 0.0), level)

        def finish(i, c):
            peer = lax.rem(me + i, n)
            origin = lax.rem(me + n - i, n)
            pltpu.make_async_remote_copy(
                x_ref, out_ref.at[me], send_sems.at[i], recv_sems.at[i],
                device_id=(peer, keep), device_id_type=mesh_id,
            ).wait_send()
            pltpu.make_async_remote_copy(
                x_ref, out_ref.at[origin], send_sems.at[i], recv_sems.at[i],
                device_id=(origin, keep), device_id_type=mesh_id,
            ).wait_recv()
            return c

        lax.fori_loop(1, n, finish, 0)
        local.wait()

    return pl.pallas_call(
        kernel,
        out_shape=(
            jax.ShapeDtypeStruct((n,) + tuple(q_slab.shape), q_slab.dtype),
            jax.ShapeDtypeStruct((q16.shape[0], lanes), jnp.float32),
        ),
        in_specs=[pl.BlockSpec(memory_space=pltpu.VMEM)] * 2
        + [pl.BlockSpec(memory_space=pltpu.SMEM), pl.BlockSpec(memory_space=pl.ANY)],
        out_specs=(pl.BlockSpec(memory_space=pltpu.VMEM), pl.BlockSpec(memory_space=pltpu.VMEM)),
        scratch_shapes=[
            pltpu.VMEM((reqs, cap, lanes), own_cache.dtype),
            pltpu.SemaphoreType.DMA((n,)),
            pltpu.SemaphoreType.DMA((n,)),
            pltpu.SemaphoreType.DMA(()),
            pltpu.SemaphoreType.DMA(()),
        ],
        compiler_params=pltpu.CompilerParams(collective_id=0, has_side_effects=True),
    )(q_slab, q16, lens16, own_cache)


def finish_kernel_call(q_slab, q16_rows, own_len, own_cache, prefix, base, req_group, jrow, pre_len, new, w_out, n_tok, n_kv):
    slab_rows = 16
    rows = slab_rows // 4
    groups, pre_dev, kv_lanes = prefix.shape
    window = 16 * 8
    heads = 4
    width = 64
    d_model = w_out.shape[1]
    cols = d_model // n_kv
    mesh_id = pl.DeviceIdType.MESH

    reqs, cap, lanes = own_cache.shape[1:]
    per = q16_rows // reqs

    def kernel(x_ref, olen_ref, own_hbm, pre_ref, idx_ref, rg_ref, len_ref, new_ref, w_ref,
               out_ref, recv_scr, acc_scr, part_scr, kv_recv, res_scr, packed_ref,
               qrecv, qrows_scr, own_vmem, own_ref,
               tsend, trecv, ksend, krecv, loc_sems, qsend, qrsem, extra_sems):
        me = lax.axis_index("tok")
        mk = lax.axis_index("kv")
        barrier = pltpu.get_barrier_semaphore()

        def greet_tok(i, c):
            pl.semaphore_signal(barrier, inc=1, device_id=(lax.rem(me + i, n_tok), mk), device_id_type=mesh_id)
            return c

        def greet_kv(i, c):
            pl.semaphore_signal(barrier, inc=1, device_id=(me, lax.rem(mk + i, n_kv)), device_id_type=mesh_id)
            return c

        own_copy = pltpu.make_async_copy(own_hbm.at[0], own_vmem, extra_sems.at[0])
        own_copy.start()
        lax.fori_loop(1, n_tok, greet_tok, 0)
        lax.fori_loop(1, n_kv, greet_kv, 0)
        pl.semaphore_wait(barrier, n_tok - 1 + n_kv - 1)
        qlocal = pltpu.make_async_copy(x_ref, qrecv.at[me], extra_sems.at[1])
        qlocal.start()

        def q_copy(i, target, slot):
            return pltpu.make_async_remote_copy(
                x_ref, qrecv.at[slot], qsend.at[i], qrsem.at[i],
                device_id=(target, mk), device_id_type=mesh_id,
            )

        def send_q(i, c):
            q_copy(i, lax.rem(me + i, n_tok), me).start()
            return c

        lax.fori_loop(1, n_tok, send_q, 0)
        own_copy.wait()
        xs = x_ref[...]
        xlane = lax.broadcasted_iota(jnp.int32, (1, 128), 1)
        pieces = []
        for r in range(reqs):
            for h in range(per):
                line = xs[r * 2 + h // 2 : r * 2 + h // 2 + 1, :]
                if h % 2:
                    line = pltpu.roll(line, width, 1)
                pieces.append(jnp.where(xlane < width, line, 0.0))
        q = jnp.concatenate(pieces, axis=0).astype(jnp.bfloat16)
        orow = lax.broadcasted_iota(jnp.int32, (q.shape[0], cap), 0)
        opos = lax.broadcasted_iota(jnp.int32, (q.shape[0], cap), 1)
        scores = jnp.zeros((q.shape[0], cap), jnp.float32)
        for r in range(reqs):
            part = lax.dot_general(q, own_vmem[r], (((1,), (1,)), ((), ())),
                                   preferred_element_type=jnp.float32)
            scores = jnp.where(orow // per == r, part, scores)
        scores = scores * SCALE
        row_len = jnp.zeros((q.shape[0], cap), jnp.int32)
        for r in range(reqs):
            row_len = jnp.where(orow // per == r, olen_ref[r], row_len)
        olive = opos < row_len
        scores = jnp.where(olive, scores, NEG)
        otop = jnp.max(scores, axis=1, keepdims=True)
        oweights = jnp.where(olive, jnp.exp(scores - otop), 0.0)
        ototal = jnp.sum(oweights, axis=1, keepdims=True)
        owb = oweights.astype(jnp.bfloat16)
        oacc = jnp.zeros((q.shape[0], lanes), jnp.float32)
        for r in range(reqs):
            oacc = oacc + jnp.dot(jnp.where(orow // per == r, owb, jnp.zeros_like(owb)), own_vmem[r],
                                  preferred_element_type=jnp.float32)
        onumer = pltpu.roll(oacc, width, 1)
        olane2 = lax.broadcasted_iota(jnp.int32, oacc.shape, 1)
        oalive = ototal > 0.0
        osafe = jnp.where(oalive, ototal, 1.0)
        olevel = jnp.where(oalive, otop + jnp.log(osafe), NEG)
        own_ref[...] = jnp.where(olane2 < width, jnp.where(oalive, onumer / osafe, 0.0), olevel)

        def finish_q(i, c):
            q_copy(i, lax.rem(me + i, n_tok), me).wait_send()
            q_copy(i, lax.rem(me + n_tok - i, n_tok), lax.rem(me + n_tok - i, n_tok)).wait_recv()
            return c

        lax.fori_loop(1, n_tok, finish_q, 0)
        qlocal.wait()
        qrows_scr[...] = jnp.zeros(qrows_scr.shape, jnp.float32)
        got = qrecv[...]
        qlane = lax.broadcasted_iota(jnp.int32, (n_tok, 128), 1)
        for r in range(reqs):
            for h in range(per):
                line = got[:, r * 2 + h // 2, :]
                if h % 2:
                    line = pltpu.roll(line, width, 1)
                qrows_scr[:, r, h, :] = jnp.where(qlane < width, line, 0.0)
        q_ref = qrows_scr.reshape(n_tok * reqs, 8, 128)

        glane = lax.broadcasted_iota(jnp.int32, (window, pre_dev), 1) + me * pre_dev
        olane = lax.broadcasted_iota(jnp.int32, (window, kv_lanes), 1)
        for g in range(groups):
            first = idx_ref[g]
            qb = jnp.concatenate([q_ref[first + k] for k in range(window // 8)], axis=0)
            qb = qb.astype(jnp.bfloat16)
            kv = pre_ref[g]
            s = lax.dot_general(qb, kv, (((1,), (1,)), ((), ())), preferred_element_type=jnp.float32)
            s = s * SCALE
            live = glane < len_ref[g]
            s = jnp.where(live, s, NEG)
            top = jnp.max(s, axis=1, keepdims=True)
            e = jnp.where(live, jnp.exp(s - top), 0.0)
            total = jnp.sum(e, axis=1, keepdims=True)
            nm = jnp.dot(e.astype(jnp.bfloat16), kv, preferred_element_type=jnp.float32)
            nm = pltpu.roll(nm, width, 1)
            alive = total > 0.0
            safe = jnp.where(alive, total, 1.0)
            level = jnp.where(alive, top + jnp.log(safe), NEG)
            res_scr[pl.ds(g * (window // 8), window // 8)] = jnp.where(
                olane < width, jnp.where(alive, nm / safe, 0.0), level).reshape(window // 8, 8, kv_lanes)

        prow = lax.broadcasted_iota(jnp.int32, (8, kv_lanes), 0)

        def place(m, c):
            blocks = []
            for t in range(2):
                r = 2 * m + t
                blocks.append(res_scr[rg_ref[r] * (window // 8) + idx_ref[groups + r]])
            both = jnp.where(prow < 4, blocks[0], pltpu.roll(blocks[1], 4, 0))
            packed_ref[m // 2, pl.ds(pl.multiple_of((m % 2) * 8, 8), 8), :] = both
            return c

        lax.fori_loop(0, n_tok * 2, place, 0)

        local_copy = pltpu.make_async_copy(packed_ref.at[me], recv_scr.at[me], loc_sems.at[0])
        local_copy.start()

        def tok_copy(i, target, slot):
            return pltpu.make_async_remote_copy(
                packed_ref.at[target], recv_scr.at[slot], tsend.at[i], trecv.at[i],
                device_id=(target, mk), device_id_type=mesh_id,
            )

        def send_tok(i, c):
            tok_copy(i, lax.rem(me + i, n_tok), me).start()
            return c

        lax.fori_loop(1, n_tok, send_tok, 0)

        def finish_tok(i, c):
            tok_copy(i, lax.rem(me + i, n_tok), me).wait_send()
            origin = lax.rem(me + n_tok - i, n_tok)
            pltpu.make_async_remote_copy(
                packed_ref.at[origin], recv_scr.at[origin], tsend.at[i], trecv.at[i],
                device_id=(origin, mk), device_id_type=mesh_id,
            ).wait_recv()
            return c

        lax.fori_loop(1, n_tok, finish_tok, 0)
        local_copy.wait()

        x = recv_scr[...]
        loc = own_ref[...]
        nloc = new_ref[...]
        llane = lax.broadcasted_iota(jnp.int32, loc.shape, 1)
        big = jnp.maximum(jnp.maximum(jnp.max(x, axis=0), loc), nloc)
        keep_hi = llane >= width
        weight = jnp.where(keep_hi[None], jnp.exp(x - big[None]), 0.0)
        lweight = jnp.where(keep_hi, jnp.exp(loc - big), 0.0)
        nweight = jnp.where(keep_hi, jnp.exp(nloc - big), 0.0)
        weight = pltpu.roll(weight.reshape(-1, 128), width, 1).reshape(x.shape)
        lweight = pltpu.roll(lweight, width, 1)
        nweight = pltpu.roll(nweight, width, 1)
        denom = jnp.sum(weight, axis=0) + lweight + nweight
        numer = jnp.sum(weight * x, axis=0) + lweight * loc + nweight * nloc
        attn = jnp.where(llane < width, numer / jnp.where(llane < width, denom, 1.0), 0.0).astype(jnp.bfloat16)
        pi = lax.broadcasted_iota(jnp.int32, (slab_rows, slab_rows), 0)
        pj = lax.broadcasted_iota(jnp.int32, (slab_rows, slab_rows), 1)
        perm = jnp.where(pj == (pi % rows) * heads + pi // rows, 1.0, 0.0).astype(jnp.bfloat16)
        attn = jnp.dot(perm, attn, preferred_element_type=jnp.float32)
        shifted = pltpu.roll(attn, width, 1)
        row = lax.broadcasted_iota(jnp.int32, attn.shape, 0)
        head_of = row // rows
        acc = jnp.zeros((slab_rows, d_model), jnp.float32)
        for pair in range(heads // 2):
            lhs = jnp.where(head_of == 2 * pair, attn, jnp.where(head_of == 2 * pair + 1, shifted, 0.0))
            acc = acc + jnp.dot(
                lhs.astype(jnp.bfloat16), w_ref[pl.ds(pair * 2 * width, 2 * width), :],
                preferred_element_type=jnp.float32,
            )
        acc_scr[...] = acc
        partial = acc_scr[pl.ds(0, rows), :]
        for h in range(1, heads):
            partial = partial + acc_scr[pl.ds(h * rows, rows), :]
        part_scr[...] = partial

        def kv_src(target):
            return part_scr.at[:, pl.ds(pl.multiple_of(target * cols, cols), cols)]

        kv_local = pltpu.make_async_copy(kv_src(mk), kv_recv.at[mk], loc_sems.at[1])
        kv_local.start()

        def kv_copy(j, target, slot):
            return pltpu.make_async_remote_copy(
                kv_src(target), kv_recv.at[slot], ksend.at[j], krecv.at[j],
                device_id=(me, target), device_id_type=mesh_id,
            )

        def send_kv(j, c):
            kv_copy(j, lax.rem(mk + j, n_kv), mk).start()
            return c

        lax.fori_loop(1, n_kv, send_kv, 0)

        def finish_kv(j, c):
            kv_copy(j, lax.rem(mk + j, n_kv), mk).wait_send()
            origin = lax.rem(mk + n_kv - j, n_kv)
            pltpu.make_async_remote_copy(
                kv_src(origin), kv_recv.at[origin], ksend.at[j], krecv.at[j],
                device_id=(me, origin), device_id_type=mesh_id,
            ).wait_recv()
            return c

        lax.fori_loop(1, n_kv, finish_kv, 0)
        kv_local.wait()
        out_ref[...] = jnp.sum(kv_recv[...], axis=0).astype(out_ref.dtype)

    return pl.pallas_call(
        kernel,
        out_shape=jax.ShapeDtypeStruct((rows, cols), jnp.bfloat16),
        in_specs=[pl.BlockSpec(memory_space=pltpu.VMEM)]
        + [pl.BlockSpec(memory_space=pltpu.SMEM), pl.BlockSpec(memory_space=pl.ANY),
           pl.BlockSpec(memory_space=pltpu.VMEM)]
        + [pl.BlockSpec(memory_space=pltpu.SMEM)] * 3
        + [pl.BlockSpec(memory_space=pltpu.VMEM)] * 2,
        out_specs=pl.BlockSpec(memory_space=pltpu.VMEM),
        scratch_shapes=[
            pltpu.VMEM((n_tok, slab_rows, 128), jnp.float32),
            pltpu.VMEM((slab_rows, d_model), jnp.float32),
            pltpu.VMEM((rows, d_model), jnp.float32),
            pltpu.VMEM((n_kv, rows, cols), jnp.float32),
            pltpu.VMEM((groups * (window // 8), 8, 128), jnp.float32),
            pltpu.VMEM((n_tok, slab_rows, 128), jnp.float32),
            pltpu.VMEM((n_tok,) + tuple(q_slab.shape), jnp.float32),
            pltpu.VMEM((n_tok, reqs, 8, 128), jnp.float32),
            pltpu.VMEM((reqs, cap, lanes), own_cache.dtype),
            pltpu.VMEM((slab_rows, 128), jnp.float32),
            pltpu.SemaphoreType.DMA((n_tok,)),
            pltpu.SemaphoreType.DMA((n_tok,)),
            pltpu.SemaphoreType.DMA((n_kv,)),
            pltpu.SemaphoreType.DMA((n_kv,)),
            pltpu.SemaphoreType.DMA((2,)),
            pltpu.SemaphoreType.DMA((n_tok,)),
            pltpu.SemaphoreType.DMA((n_tok,)),
            pltpu.SemaphoreType.DMA((2,)),
        ],
        compiler_params=pltpu.CompilerParams(collective_id=1, has_side_effects=True),
    )(q_slab, own_len, own_cache, prefix, jnp.concatenate([base, jrow]), req_group, pre_len, new, w_out)


def block_stats(query, keyval, live):
    width = query.shape[-1]
    keys = keyval[..., :width]
    values = keyval[..., width:]
    scores = jnp.einsum("rhge,hrpe->rhgp", query, keys, preferred_element_type=jnp.float32) * SCALE
    mask = live[:, None, None, :]
    scores = jnp.where(mask, scores, NEG)
    top = jnp.max(scores, axis=-1)
    weights = jnp.where(mask, jnp.exp(scores - top[..., None]), 0.0)
    total = jnp.sum(weights, axis=-1)
    numer = jnp.einsum(
        "rhgp,hrpe->rhge", weights.astype(jnp.bfloat16), values, preferred_element_type=jnp.float32
    )
    return (top, total, numer)


def prompt_stats(all_query, prefix_cache, req_group, pre_len, block):
    all_rows, heads, per_kv, width = all_query.shape
    groups = prefix_cache.shape[1]
    pre_dev = prefix_cache.shape[2]
    group_ids = jnp.arange(groups, dtype=jnp.int32)
    starts = jnp.sum((req_group[None, :] < group_ids[:, None]).astype(jnp.int32), axis=1)
    slot_ids = jnp.arange(SHARE, dtype=jnp.int32)
    source = jnp.minimum(starts[:, None] + slot_ids[None, :], all_rows - 1).reshape(-1)
    slotted = jnp.take(all_query, source, axis=0).reshape(groups, SHARE, heads, per_kv, width)
    keys = prefix_cache[..., :width]
    values = prefix_cache[..., width:]
    scores = (
        jnp.einsum("gshqe,hgpe->hgsqp", slotted, keys, preferred_element_type=jnp.float32) * SCALE
    )
    pre_pos = block * pre_dev + jnp.arange(pre_dev, dtype=jnp.int32)
    live = pre_pos[None, :] < pre_len[:, None]
    mask = live[None, :, None, None, :]
    scores = jnp.where(mask, scores, NEG)
    top = jnp.max(scores, axis=-1)
    weights = jnp.where(mask, jnp.exp(scores - top[..., None]), 0.0)
    total = jnp.sum(weights, axis=-1)
    numer = jnp.einsum(
        "hgsqp,hgpe->hgsqe",
        weights.astype(jnp.bfloat16),
        values,
        preferred_element_type=jnp.float32,
    )
    match = req_group[:, None] == group_ids[None, :]
    start_req = jnp.sum(jnp.where(match, starts[None, :], 0), axis=1)
    place = req_group * SHARE + jnp.arange(all_rows, dtype=jnp.int32) - start_req
    alive = total > 0.0
    safe = jnp.where(alive, total, 1.0)
    level = jnp.where(alive, top + jnp.log(safe), NEG)
    packed = jnp.concatenate(
        [jnp.where(alive[..., None], numer / safe[..., None], 0.0),
         jnp.broadcast_to(level[..., None], top.shape + (128 - width,))],
        axis=-1,
    ).reshape(heads, groups * SHARE, per_kv, 128)
    packed = jnp.take(packed, place, axis=1)
    return jnp.transpose(packed, (1, 0, 2, 3)).reshape(all_rows * heads * per_kv, 128)


def body(hidden_in, w_query, w_keyval, w_out, own_cache, prefix_cache, own_len, req_group, pre_len):
    rows = hidden_in.shape[0]
    heads = w_keyval.shape[1]
    width = w_keyval.shape[2] // 2
    per_kv = w_query.shape[1] // (heads * width)
    columns = heads * per_kv
    inputs = hidden_in.astype(jnp.float32)
    normed = (inputs * lax.rsqrt(jnp.mean(inputs * inputs, axis=1, keepdims=True) + 1e-05)).astype(
        jnp.bfloat16
    )
    query = jnp.dot(normed, w_query, preferred_element_type=jnp.float32).astype(jnp.bfloat16)
    newkv = jnp.einsum("rd,dhe->rhe", normed, w_keyval, preferred_element_type=jnp.float32).astype(
        jnp.bfloat16
    )
    n_tok = lax.axis_size("tok")
    n_kv = lax.axis_size("kv")
    q_slab = query.astype(jnp.float32).reshape(-1, 128)
    q16 = jnp.concatenate(
        [query.reshape(rows * columns, width), jnp.zeros((rows * columns, width), query.dtype)], axis=1
    )
    all_rows = n_tok * rows
    groups = prefix_cache.shape[1]
    group_ids = jnp.arange(groups, dtype=jnp.int32)
    starts = jnp.sum((req_group[None, :] < group_ids[:, None]).astype(jnp.int32), axis=1)
    base = jnp.minimum(starts, all_rows - SHARE)
    rg = jnp.clip(req_group, 0, groups - 1)
    own_start = jnp.sum((req_group[None, :] < req_group[:, None]).astype(jnp.int32), axis=1)
    own_base = jnp.minimum(own_start, all_rows - SHARE)
    jrow = jnp.clip(jnp.arange(all_rows, dtype=jnp.int32) - own_base, 0, SHARE - 1)
    local_query = query.reshape(rows, heads, per_kv, width)
    s_new = (
        jnp.einsum(
            "rhge,rhe->rhg", local_query, newkv[..., :width], preferred_element_type=jnp.float32
        )
        * SCALE
    )
    s_new = s_new.reshape(rows, columns)
    new_value = jnp.broadcast_to(
        newkv[:, :, None, width:].astype(jnp.float32), (rows, heads, per_kv, width)
    ).reshape(rows, columns, width)
    new_block = jnp.concatenate(
        [new_value, jnp.broadcast_to(s_new[..., None], (rows, columns, 128 - width))],
        axis=-1,
    ).reshape(rows * columns, 128)
    return finish_kernel_call(q_slab, rows * columns, own_len, own_cache, prefix_cache[0], base, rg, jrow, pre_len, new_block, w_out, n_tok, n_kv)


def solution(mesh):
    in_specs = (
        P("tok", None),
        P(None, "kv"),
        P(None, "kv", None),
        P("kv", None),
        P("kv", "tok", None, None),
        P("kv", None, "tok", None),
        P("tok"),
        P(),
        P(),
    )
    out_specs = P("tok", "kv")
    return jax.shard_map(body, mesh=mesh, in_specs=in_specs, out_specs=out_specs, check_vma=False)
```

```python
import jax
import jax.numpy as jnp
from jax import lax
from jax.sharding import PartitionSpec as P
from jax.experimental import pallas as pl
from jax.experimental.pallas import tpu as pltpu

SHARE = 16


SCALE = 0.015625
NEG = -1e30


def exchange(slabs, axis, other, n, broadcast, cid):
    slab_shape = slabs.shape[1:] if not broadcast else slabs.shape
    mesh_id = pl.DeviceIdType.MESH

    def kernel(x_ref, out_ref, send_sems, recv_sems, local_sem):
        me = lax.axis_index(axis)
        keep = lax.axis_index(other)

        def dev(peer):
            return (peer, keep) if axis == "tok" else (keep, peer)

        def src(peer):
            return x_ref if broadcast else x_ref.at[peer]

        barrier = pltpu.get_barrier_semaphore()

        def greet(i, c):
            peer = lax.rem(me + i, n)
            pl.semaphore_signal(barrier, inc=1, device_id=dev(peer), device_id_type=mesh_id)
            return c

        lax.fori_loop(1, n, greet, 0)
        pl.semaphore_wait(barrier, n - 1)
        local = pltpu.make_async_copy(src(me), out_ref.at[me], local_sem)
        local.start()

        def send(i, c):
            peer = lax.rem(me + i, n)
            pltpu.make_async_remote_copy(
                src(peer), out_ref.at[me], send_sems.at[i], recv_sems.at[i],
                device_id=dev(peer), device_id_type=mesh_id,
            ).start()
            return c

        lax.fori_loop(1, n, send, 0)

        def finish(i, c):
            peer = lax.rem(me + i, n)
            origin = lax.rem(me + n - i, n)
            pltpu.make_async_remote_copy(
                src(peer), out_ref.at[me], send_sems.at[i], recv_sems.at[i],
                device_id=dev(peer), device_id_type=mesh_id,
            ).wait_send()
            pltpu.make_async_remote_copy(
                src(peer), out_ref.at[origin], send_sems.at[i], recv_sems.at[i],
                device_id=dev(origin), device_id_type=mesh_id,
            ).wait_recv()
            return c

        lax.fori_loop(1, n, finish, 0)
        local.wait()

    return pl.pallas_call(
        kernel,
        out_shape=jax.ShapeDtypeStruct((n,) + tuple(slab_shape), slabs.dtype),
        in_specs=[pl.BlockSpec(memory_space=pltpu.VMEM)],
        out_specs=pl.BlockSpec(memory_space=pltpu.VMEM),
        scratch_shapes=[
            pltpu.SemaphoreType.DMA((n,)),
            pltpu.SemaphoreType.DMA((n,)),
            pltpu.SemaphoreType.DMA(()),
        ],
        compiler_params=pltpu.CompilerParams(collective_id=cid, has_side_effects=True),
    )(slabs)


def broadcast_with_own(q_slab, q16, lens16, own_cache, n, scale):
    mesh_id = pl.DeviceIdType.MESH
    reqs, cap, lanes = own_cache.shape[1:]
    half = lanes // 2
    per = q16.shape[0] // reqs

    def kernel(x_ref, q_ref, len_ref, own_hbm, out_ref, own_out, own_vmem,
               send_sems, recv_sems, local_sem, own_sem):
        me = lax.axis_index("tok")
        keep = lax.axis_index("kv")
        own_copy = pltpu.make_async_copy(own_hbm.at[0], own_vmem, own_sem)
        own_copy.start()
        barrier = pltpu.get_barrier_semaphore()

        def greet(i, c):
            pl.semaphore_signal(barrier, inc=1, device_id=(lax.rem(me + i, n), keep), device_id_type=mesh_id)
            return c

        lax.fori_loop(1, n, greet, 0)
        pl.semaphore_wait(barrier, n - 1)
        local = pltpu.make_async_copy(x_ref, out_ref.at[me], local_sem)
        local.start()

        def send(i, c):
            peer = lax.rem(me + i, n)
            pltpu.make_async_remote_copy(
                x_ref, out_ref.at[me], send_sems.at[i], recv_sems.at[i],
                device_id=(peer, keep), device_id_type=mesh_id,
            ).start()
            return c

        lax.fori_loop(1, n, send, 0)
        own_copy.wait()
        q = q_ref[...]
        row = lax.broadcasted_iota(jnp.int32, (q.shape[0], cap), 0)
        pos = lax.broadcasted_iota(jnp.int32, (q.shape[0], cap), 1)
        scores = jnp.zeros((q.shape[0], cap), jnp.float32)
        for r in range(reqs):
            part = lax.dot_general(q, own_vmem[r], (((1,), (1,)), ((), ())),
                                   preferred_element_type=jnp.float32)
            scores = jnp.where(row // per == r, part, scores)
        scores = scores * scale
        row_len = jnp.zeros((q.shape[0], cap), jnp.int32)
        for r in range(reqs):
            row_len = jnp.where(row // per == r, len_ref[r], row_len)
        live = pos < row_len
        scores = jnp.where(live, scores, NEG)
        top = jnp.max(scores, axis=1, keepdims=True)
        weights = jnp.where(live, jnp.exp(scores - top), 0.0)
        total = jnp.sum(weights, axis=1, keepdims=True)
        wb = weights.astype(jnp.bfloat16)
        acc = jnp.zeros((q.shape[0], lanes), jnp.float32)
        for r in range(reqs):
            acc = acc + jnp.dot(jnp.where(row // per == r, wb, jnp.zeros_like(wb)), own_vmem[r],
                                preferred_element_type=jnp.float32)
        numer = pltpu.roll(acc, half, 1)
        lane = lax.broadcasted_iota(jnp.int32, acc.shape, 1)
        alive = total > 0.0
        safe = jnp.where(alive, total, 1.0)
        level = jnp.where(alive, top + jnp.log(safe), NEG)
        own_out[...] = jnp.where(lane < half, jnp.where(alive, numer / safe, 0.0), level)

        def finish(i, c):
            peer = lax.rem(me + i, n)
            origin = lax.rem(me + n - i, n)
            pltpu.make_async_remote_copy(
                x_ref, out_ref.at[me], send_sems.at[i], recv_sems.at[i],
                device_id=(peer, keep), device_id_type=mesh_id,
            ).wait_send()
            pltpu.make_async_remote_copy(
                x_ref, out_ref.at[origin], send_sems.at[i], recv_sems.at[i],
                device_id=(origin, keep), device_id_type=mesh_id,
            ).wait_recv()
            return c

        lax.fori_loop(1, n, finish, 0)
        local.wait()

    return pl.pallas_call(
        kernel,
        out_shape=(
            jax.ShapeDtypeStruct((n,) + tuple(q_slab.shape), q_slab.dtype),
            jax.ShapeDtypeStruct((q16.shape[0], lanes), jnp.float32),
        ),
        in_specs=[pl.BlockSpec(memory_space=pltpu.VMEM)] * 2
        + [pl.BlockSpec(memory_space=pltpu.SMEM), pl.BlockSpec(memory_space=pl.ANY)],
        out_specs=(pl.BlockSpec(memory_space=pltpu.VMEM), pl.BlockSpec(memory_space=pltpu.VMEM)),
        scratch_shapes=[
            pltpu.VMEM((reqs, cap, lanes), own_cache.dtype),
            pltpu.SemaphoreType.DMA((n,)),
            pltpu.SemaphoreType.DMA((n,)),
            pltpu.SemaphoreType.DMA(()),
            pltpu.SemaphoreType.DMA(()),
        ],
        compiler_params=pltpu.CompilerParams(collective_id=0, has_side_effects=True),
    )(q_slab, q16, lens16, own_cache)


def finish_kernel_call(q_slab, q16_rows, own_len, own_cache, prefix, base, req_group, jrow, pre_len, new, w_out, n_tok, n_kv):
    slab_rows = 16
    rows = slab_rows // 4
    groups, pre_dev, kv_lanes = prefix.shape
    window = 16 * 8
    heads = 4
    width = 64
    d_model = w_out.shape[1]
    cols = d_model // n_kv
    mesh_id = pl.DeviceIdType.MESH

    reqs, cap, lanes = own_cache.shape[1:]
    per = q16_rows // reqs

    def kernel(x_ref, olen_ref, own_hbm, pre_ref, idx_ref, rg_ref, len_ref, new_ref, w_ref,
               out_ref, recv_scr, acc_scr, part_scr, kv_recv, res_scr, packed_ref,
               qrecv, qrows_scr, own_vmem, own_ref, new_scr,
               tsend, trecv, ksend, krecv, loc_sems, qsend, qrsem, extra_sems):
        me = lax.axis_index("tok")
        mk = lax.axis_index("kv")
        barrier = pltpu.get_barrier_semaphore()

        def greet_tok(i, c):
            pl.semaphore_signal(barrier, inc=1, device_id=(lax.rem(me + i, n_tok), mk), device_id_type=mesh_id)
            return c

        def greet_kv(i, c):
            pl.semaphore_signal(barrier, inc=1, device_id=(me, lax.rem(mk + i, n_kv)), device_id_type=mesh_id)
            return c

        own_copy = pltpu.make_async_copy(own_hbm.at[0], own_vmem, extra_sems.at[0])
        own_copy.start()
        lax.fori_loop(1, n_tok, greet_tok, 0)
        lax.fori_loop(1, n_kv, greet_kv, 0)
        pl.semaphore_wait(barrier, n_tok - 1 + n_kv - 1)
        qlocal = pltpu.make_async_copy(x_ref, qrecv.at[me], extra_sems.at[1])
        qlocal.start()

        def q_copy(i, target, slot):
            return pltpu.make_async_remote_copy(
                x_ref, qrecv.at[slot], qsend.at[i], qrsem.at[i],
                device_id=(target, mk), device_id_type=mesh_id,
            )

        def send_q(i, c):
            q_copy(i, lax.rem(me + i, n_tok), me).start()
            return c

        lax.fori_loop(1, n_tok, send_q, 0)
        own_copy.wait()
        xs = x_ref[...]
        xlane = lax.broadcasted_iota(jnp.int32, (1, 128), 1)
        pieces = []
        for r in range(reqs):
            for h in range(per):
                line = xs[r * 2 + h // 2 : r * 2 + h // 2 + 1, :]
                if h % 2:
                    line = pltpu.roll(line, width, 1)
                pieces.append(jnp.where(xlane < width, line, 0.0))
        qf = jnp.concatenate(pieces, axis=0)
        q = qf.astype(jnp.bfloat16)
        nkv = new_ref[...].astype(jnp.float32)
        knew = jnp.concatenate([nkv[r : r + 1] for r in range(reqs) for _ in range(per)], axis=0)
        nlane = lax.broadcasted_iota(jnp.int32, knew.shape, 1)
        s_new = jnp.sum(jnp.where(nlane < width, qf * knew, 0.0), axis=1, keepdims=True) * SCALE
        new_scr[...] = jnp.where(nlane < width, pltpu.roll(knew, width, 1), s_new)
        orow = lax.broadcasted_iota(jnp.int32, (q.shape[0], cap), 0)
        opos = lax.broadcasted_iota(jnp.int32, (q.shape[0], cap), 1)
        scores = jnp.zeros((q.shape[0], cap), jnp.float32)
        for r in range(reqs):
            part = lax.dot_general(q, own_vmem[r], (((1,), (1,)), ((), ())),
                                   preferred_element_type=jnp.float32)
            scores = jnp.where(orow // per == r, part, scores)
        scores = scores * SCALE
        row_len = jnp.zeros((q.shape[0], cap), jnp.int32)
        for r in range(reqs):
            row_len = jnp.where(orow // per == r, olen_ref[r], row_len)
        olive = opos < row_len
        scores = jnp.where(olive, scores, NEG)
        otop = jnp.max(scores, axis=1, keepdims=True)
        oweights = jnp.where(olive, jnp.exp(scores - otop), 0.0)
        ototal = jnp.sum(oweights, axis=1, keepdims=True)
        owb = oweights.astype(jnp.bfloat16)
        oacc = jnp.zeros((q.shape[0], lanes), jnp.float32)
        for r in range(reqs):
            oacc = oacc + jnp.dot(jnp.where(orow // per == r, owb, jnp.zeros_like(owb)), own_vmem[r],
                                  preferred_element_type=jnp.float32)
        onumer = pltpu.roll(oacc, width, 1)
        olane2 = lax.broadcasted_iota(jnp.int32, oacc.shape, 1)
        oalive = ototal > 0.0
        osafe = jnp.where(oalive, ototal, 1.0)
        olevel = jnp.where(oalive, otop + jnp.log(osafe), NEG)
        own_ref[...] = jnp.where(olane2 < width, jnp.where(oalive, onumer / osafe, 0.0), olevel)

        def finish_q(i, c):
            q_copy(i, lax.rem(me + i, n_tok), me).wait_send()
            q_copy(i, lax.rem(me + n_tok - i, n_tok), lax.rem(me + n_tok - i, n_tok)).wait_recv()
            return c

        lax.fori_loop(1, n_tok, finish_q, 0)
        qlocal.wait()
        qrows_scr[...] = jnp.zeros(qrows_scr.shape, jnp.float32)
        got = qrecv[...]
        qlane = lax.broadcasted_iota(jnp.int32, (n_tok, 128), 1)
        for r in range(reqs):
            for h in range(per):
                line = got[:, r * 2 + h // 2, :]
                if h % 2:
                    line = pltpu.roll(line, width, 1)
                qrows_scr[:, r, h, :] = jnp.where(qlane < width, line, 0.0)
        q_ref = qrows_scr.reshape(n_tok * reqs, 8, 128)

        glane = lax.broadcasted_iota(jnp.int32, (window, pre_dev), 1) + me * pre_dev
        olane = lax.broadcasted_iota(jnp.int32, (window, kv_lanes), 1)
        for g in range(groups):
            first = idx_ref[g]
            qb = jnp.concatenate([q_ref[first + k] for k in range(window // 8)], axis=0)
            qb = qb.astype(jnp.bfloat16)
            kv = pre_ref[g]
            s = lax.dot_general(qb, kv, (((1,), (1,)), ((), ())), preferred_element_type=jnp.float32)
            s = s * SCALE
            live = glane < len_ref[g]
            s = jnp.where(live, s, NEG)
            top = jnp.max(s, axis=1, keepdims=True)
            e = jnp.where(live, jnp.exp(s - top), 0.0)
            total = jnp.sum(e, axis=1, keepdims=True)
            nm = jnp.dot(e.astype(jnp.bfloat16), kv, preferred_element_type=jnp.float32)
            nm = pltpu.roll(nm, width, 1)
            alive = total > 0.0
            safe = jnp.where(alive, total, 1.0)
            level = jnp.where(alive, top + jnp.log(safe), NEG)
            res_scr[pl.ds(g * (window // 8), window // 8)] = jnp.where(
                olane < width, jnp.where(alive, nm / safe, 0.0), level).reshape(window // 8, 8, kv_lanes)

        prow = lax.broadcasted_iota(jnp.int32, (8, kv_lanes), 0)

        def place(m, c):
            blocks = []
            for t in range(2):
                r = 2 * m + t
                blocks.append(res_scr[rg_ref[r] * (window // 8) + idx_ref[groups + r]])
            both = jnp.where(prow < 4, blocks[0], pltpu.roll(blocks[1], 4, 0))
            packed_ref[m // 2, pl.ds(pl.multiple_of((m % 2) * 8, 8), 8), :] = both
            return c

        lax.fori_loop(0, n_tok * 2, place, 0)

        local_copy = pltpu.make_async_copy(packed_ref.at[me], recv_scr.at[me], loc_sems.at[0])
        local_copy.start()

        def tok_copy(i, target, slot):
            return pltpu.make_async_remote_copy(
                packed_ref.at[target], recv_scr.at[slot], tsend.at[i], trecv.at[i],
                device_id=(target, mk), device_id_type=mesh_id,
            )

        def send_tok(i, c):
            tok_copy(i, lax.rem(me + i, n_tok), me).start()
            return c

        lax.fori_loop(1, n_tok, send_tok, 0)

        def finish_tok(i, c):
            tok_copy(i, lax.rem(me + i, n_tok), me).wait_send()
            origin = lax.rem(me + n_tok - i, n_tok)
            pltpu.make_async_remote_copy(
                packed_ref.at[origin], recv_scr.at[origin], tsend.at[i], trecv.at[i],
                device_id=(origin, mk), device_id_type=mesh_id,
            ).wait_recv()
            return c

        lax.fori_loop(1, n_tok, finish_tok, 0)
        local_copy.wait()

        x = recv_scr[...]
        loc = own_ref[...]
        nloc = new_scr[...]
        llane = lax.broadcasted_iota(jnp.int32, loc.shape, 1)
        big = jnp.maximum(jnp.maximum(jnp.max(x, axis=0), loc), nloc)
        keep_hi = llane >= width
        weight = jnp.where(keep_hi[None], jnp.exp(x - big[None]), 0.0)
        lweight = jnp.where(keep_hi, jnp.exp(loc - big), 0.0)
        nweight = jnp.where(keep_hi, jnp.exp(nloc - big), 0.0)
        weight = pltpu.roll(weight.reshape(-1, 128), width, 1).reshape(x.shape)
        lweight = pltpu.roll(lweight, width, 1)
        nweight = pltpu.roll(nweight, width, 1)
        denom = jnp.sum(weight, axis=0) + lweight + nweight
        numer = jnp.sum(weight * x, axis=0) + lweight * loc + nweight * nloc
        attn = jnp.where(llane < width, numer / jnp.where(llane < width, denom, 1.0), 0.0).astype(jnp.bfloat16)
        pi = lax.broadcasted_iota(jnp.int32, (slab_rows, slab_rows), 0)
        pj = lax.broadcasted_iota(jnp.int32, (slab_rows, slab_rows), 1)
        perm = jnp.where(pj == (pi % rows) * heads + pi // rows, 1.0, 0.0).astype(jnp.bfloat16)
        attn = jnp.dot(perm, attn, preferred_element_type=jnp.float32)
        shifted = pltpu.roll(attn, width, 1)
        row = lax.broadcasted_iota(jnp.int32, attn.shape, 0)
        head_of = row // rows
        acc = jnp.zeros((slab_rows, d_model), jnp.float32)
        for pair in range(heads // 2):
            lhs = jnp.where(head_of == 2 * pair, attn, jnp.where(head_of == 2 * pair + 1, shifted, 0.0))
            acc = acc + jnp.dot(
                lhs.astype(jnp.bfloat16), w_ref[pl.ds(pair * 2 * width, 2 * width), :],
                preferred_element_type=jnp.float32,
            )
        acc_scr[...] = acc
        partial = acc_scr[pl.ds(0, rows), :]
        for h in range(1, heads):
            partial = partial + acc_scr[pl.ds(h * rows, rows), :]
        part_scr[...] = partial

        def kv_src(target):
            return part_scr.at[:, pl.ds(pl.multiple_of(target * cols, cols), cols)]

        kv_local = pltpu.make_async_copy(kv_src(mk), kv_recv.at[mk], loc_sems.at[1])
        kv_local.start()

        def kv_copy(j, target, slot):
            return pltpu.make_async_remote_copy(
                kv_src(target), kv_recv.at[slot], ksend.at[j], krecv.at[j],
                device_id=(me, target), device_id_type=mesh_id,
            )

        def send_kv(j, c):
            kv_copy(j, lax.rem(mk + j, n_kv), mk).start()
            return c

        lax.fori_loop(1, n_kv, send_kv, 0)

        def finish_kv(j, c):
            kv_copy(j, lax.rem(mk + j, n_kv), mk).wait_send()
            origin = lax.rem(mk + n_kv - j, n_kv)
            pltpu.make_async_remote_copy(
                kv_src(origin), kv_recv.at[origin], ksend.at[j], krecv.at[j],
                device_id=(me, origin), device_id_type=mesh_id,
            ).wait_recv()
            return c

        lax.fori_loop(1, n_kv, finish_kv, 0)
        kv_local.wait()
        out_ref[...] = jnp.sum(kv_recv[...], axis=0).astype(out_ref.dtype)

    return pl.pallas_call(
        kernel,
        out_shape=jax.ShapeDtypeStruct((rows, cols), jnp.bfloat16),
        in_specs=[pl.BlockSpec(memory_space=pltpu.VMEM)]
        + [pl.BlockSpec(memory_space=pltpu.SMEM), pl.BlockSpec(memory_space=pl.ANY),
           pl.BlockSpec(memory_space=pltpu.VMEM)]
        + [pl.BlockSpec(memory_space=pltpu.SMEM)] * 3
        + [pl.BlockSpec(memory_space=pltpu.VMEM)] * 2,
        out_specs=pl.BlockSpec(memory_space=pltpu.VMEM),
        scratch_shapes=[
            pltpu.VMEM((n_tok, slab_rows, 128), jnp.float32),
            pltpu.VMEM((slab_rows, d_model), jnp.float32),
            pltpu.VMEM((rows, d_model), jnp.float32),
            pltpu.VMEM((n_kv, rows, cols), jnp.float32),
            pltpu.VMEM((groups * (window // 8), 8, 128), jnp.float32),
            pltpu.VMEM((n_tok, slab_rows, 128), jnp.float32),
            pltpu.VMEM((n_tok,) + tuple(q_slab.shape), jnp.float32),
            pltpu.VMEM((n_tok, reqs, 8, 128), jnp.float32),
            pltpu.VMEM((reqs, cap, lanes), own_cache.dtype),
            pltpu.VMEM((slab_rows, 128), jnp.float32),
            pltpu.VMEM((slab_rows, 128), jnp.float32),
            pltpu.SemaphoreType.DMA((n_tok,)),
            pltpu.SemaphoreType.DMA((n_tok,)),
            pltpu.SemaphoreType.DMA((n_kv,)),
            pltpu.SemaphoreType.DMA((n_kv,)),
            pltpu.SemaphoreType.DMA((2,)),
            pltpu.SemaphoreType.DMA((n_tok,)),
            pltpu.SemaphoreType.DMA((n_tok,)),
            pltpu.SemaphoreType.DMA((2,)),
        ],
        compiler_params=pltpu.CompilerParams(collective_id=1, has_side_effects=True),
    )(q_slab, own_len, own_cache, prefix, jnp.concatenate([base, jrow]), req_group, pre_len, new, w_out)


def block_stats(query, keyval, live):
    width = query.shape[-1]
    keys = keyval[..., :width]
    values = keyval[..., width:]
    scores = jnp.einsum("rhge,hrpe->rhgp", query, keys, preferred_element_type=jnp.float32) * SCALE
    mask = live[:, None, None, :]
    scores = jnp.where(mask, scores, NEG)
    top = jnp.max(scores, axis=-1)
    weights = jnp.where(mask, jnp.exp(scores - top[..., None]), 0.0)
    total = jnp.sum(weights, axis=-1)
    numer = jnp.einsum(
        "rhgp,hrpe->rhge", weights.astype(jnp.bfloat16), values, preferred_element_type=jnp.float32
    )
    return (top, total, numer)


def prompt_stats(all_query, prefix_cache, req_group, pre_len, block):
    all_rows, heads, per_kv, width = all_query.shape
    groups = prefix_cache.shape[1]
    pre_dev = prefix_cache.shape[2]
    group_ids = jnp.arange(groups, dtype=jnp.int32)
    starts = jnp.sum((req_group[None, :] < group_ids[:, None]).astype(jnp.int32), axis=1)
    slot_ids = jnp.arange(SHARE, dtype=jnp.int32)
    source = jnp.minimum(starts[:, None] + slot_ids[None, :], all_rows - 1).reshape(-1)
    slotted = jnp.take(all_query, source, axis=0).reshape(groups, SHARE, heads, per_kv, width)
    keys = prefix_cache[..., :width]
    values = prefix_cache[..., width:]
    scores = (
        jnp.einsum("gshqe,hgpe->hgsqp", slotted, keys, preferred_element_type=jnp.float32) * SCALE
    )
    pre_pos = block * pre_dev + jnp.arange(pre_dev, dtype=jnp.int32)
    live = pre_pos[None, :] < pre_len[:, None]
    mask = live[None, :, None, None, :]
    scores = jnp.where(mask, scores, NEG)
    top = jnp.max(scores, axis=-1)
    weights = jnp.where(mask, jnp.exp(scores - top[..., None]), 0.0)
    total = jnp.sum(weights, axis=-1)
    numer = jnp.einsum(
        "hgsqp,hgpe->hgsqe",
        weights.astype(jnp.bfloat16),
        values,
        preferred_element_type=jnp.float32,
    )
    match = req_group[:, None] == group_ids[None, :]
    start_req = jnp.sum(jnp.where(match, starts[None, :], 0), axis=1)
    place = req_group * SHARE + jnp.arange(all_rows, dtype=jnp.int32) - start_req
    alive = total > 0.0
    safe = jnp.where(alive, total, 1.0)
    level = jnp.where(alive, top + jnp.log(safe), NEG)
    packed = jnp.concatenate(
        [jnp.where(alive[..., None], numer / safe[..., None], 0.0),
         jnp.broadcast_to(level[..., None], top.shape + (128 - width,))],
        axis=-1,
    ).reshape(heads, groups * SHARE, per_kv, 128)
    packed = jnp.take(packed, place, axis=1)
    return jnp.transpose(packed, (1, 0, 2, 3)).reshape(all_rows * heads * per_kv, 128)


def body(hidden_in, w_query, w_keyval, w_out, own_cache, prefix_cache, own_len, req_group, pre_len):
    rows = hidden_in.shape[0]
    heads = w_keyval.shape[1]
    width = w_keyval.shape[2] // 2
    per_kv = w_query.shape[1] // (heads * width)
    columns = heads * per_kv
    inputs = hidden_in.astype(jnp.float32)
    normed = (inputs * lax.rsqrt(jnp.mean(inputs * inputs, axis=1, keepdims=True) + 1e-05)).astype(
        jnp.bfloat16
    )
    query = jnp.dot(normed, w_query, preferred_element_type=jnp.float32).astype(jnp.bfloat16)
    newkv = jnp.einsum("rd,dhe->rhe", normed, w_keyval, preferred_element_type=jnp.float32).astype(
        jnp.bfloat16
    )
    n_tok = lax.axis_size("tok")
    n_kv = lax.axis_size("kv")
    q_slab = query.astype(jnp.float32).reshape(-1, 128)
    q16 = jnp.concatenate(
        [query.reshape(rows * columns, width), jnp.zeros((rows * columns, width), query.dtype)], axis=1
    )
    all_rows = n_tok * rows
    groups = prefix_cache.shape[1]
    group_ids = jnp.arange(groups, dtype=jnp.int32)
    starts = jnp.sum((req_group[None, :] < group_ids[:, None]).astype(jnp.int32), axis=1)
    base = jnp.minimum(starts, all_rows - SHARE)
    rg = jnp.clip(req_group, 0, groups - 1)
    own_start = jnp.sum((req_group[None, :] < req_group[:, None]).astype(jnp.int32), axis=1)
    own_base = jnp.minimum(own_start, all_rows - SHARE)
    jrow = jnp.clip(jnp.arange(all_rows, dtype=jnp.int32) - own_base, 0, SHARE - 1)
    local_query = query.reshape(rows, heads, per_kv, width)
    s_new = (
        jnp.einsum(
            "rhge,rhe->rhg", local_query, newkv[..., :width], preferred_element_type=jnp.float32
        )
        * SCALE
    )
    s_new = s_new.reshape(rows, columns)
    new_value = jnp.broadcast_to(
        newkv[:, :, None, width:].astype(jnp.float32), (rows, heads, per_kv, width)
    ).reshape(rows, columns, width)
    new_block = jnp.concatenate(
        [new_value, jnp.broadcast_to(s_new[..., None], (rows, columns, 128 - width))],
        axis=-1,
    ).reshape(rows * columns, 128)
    return finish_kernel_call(q_slab, rows * columns, own_len, own_cache, prefix_cache[0], base, rg, jrow, pre_len, newkv.reshape(rows, -1), w_out, n_tok, n_kv)


def solution(mesh):
    in_specs = (
        P("tok", None),
        P(None, "kv"),
        P(None, "kv", None),
        P("kv", None),
        P("kv", "tok", None, None),
        P("kv", None, "tok", None),
        P("tok"),
        P(),
        P(),
    )
    out_specs = P("tok", "kv")
    return jax.shard_map(body, mesh=mesh, in_specs=in_specs, out_specs=out_specs, check_vma=False)
```

```python
import jax
import jax.numpy as jnp
from jax import lax
from jax.sharding import PartitionSpec as P
from jax.experimental import pallas as pl
from jax.experimental.pallas import tpu as pltpu

SHARE = 16


SCALE = 0.015625
NEG = -1e30


def exchange(slabs, axis, other, n, broadcast, cid):
    slab_shape = slabs.shape[1:] if not broadcast else slabs.shape
    mesh_id = pl.DeviceIdType.MESH

    def kernel(x_ref, out_ref, send_sems, recv_sems, local_sem):
        me = lax.axis_index(axis)
        keep = lax.axis_index(other)

        def dev(peer):
            return (peer, keep) if axis == "tok" else (keep, peer)

        def src(peer):
            return x_ref if broadcast else x_ref.at[peer]

        barrier = pltpu.get_barrier_semaphore()

        def greet(i, c):
            peer = lax.rem(me + i, n)
            pl.semaphore_signal(barrier, inc=1, device_id=dev(peer), device_id_type=mesh_id)
            return c

        lax.fori_loop(1, n, greet, 0)
        pl.semaphore_wait(barrier, n - 1)
        local = pltpu.make_async_copy(src(me), out_ref.at[me], local_sem)
        local.start()

        def send(i, c):
            peer = lax.rem(me + i, n)
            pltpu.make_async_remote_copy(
                src(peer), out_ref.at[me], send_sems.at[i], recv_sems.at[i],
                device_id=dev(peer), device_id_type=mesh_id,
            ).start()
            return c

        lax.fori_loop(1, n, send, 0)

        def finish(i, c):
            peer = lax.rem(me + i, n)
            origin = lax.rem(me + n - i, n)
            pltpu.make_async_remote_copy(
                src(peer), out_ref.at[me], send_sems.at[i], recv_sems.at[i],
                device_id=dev(peer), device_id_type=mesh_id,
            ).wait_send()
            pltpu.make_async_remote_copy(
                src(peer), out_ref.at[origin], send_sems.at[i], recv_sems.at[i],
                device_id=dev(origin), device_id_type=mesh_id,
            ).wait_recv()
            return c

        lax.fori_loop(1, n, finish, 0)
        local.wait()

    return pl.pallas_call(
        kernel,
        out_shape=jax.ShapeDtypeStruct((n,) + tuple(slab_shape), slabs.dtype),
        in_specs=[pl.BlockSpec(memory_space=pltpu.VMEM)],
        out_specs=pl.BlockSpec(memory_space=pltpu.VMEM),
        scratch_shapes=[
            pltpu.SemaphoreType.DMA((n,)),
            pltpu.SemaphoreType.DMA((n,)),
            pltpu.SemaphoreType.DMA(()),
        ],
        compiler_params=pltpu.CompilerParams(collective_id=cid, has_side_effects=True),
    )(slabs)


def broadcast_with_own(q_slab, q16, lens16, own_cache, n, scale):
    mesh_id = pl.DeviceIdType.MESH
    reqs, cap, lanes = own_cache.shape[1:]
    half = lanes // 2
    per = q16.shape[0] // reqs

    def kernel(x_ref, q_ref, len_ref, own_hbm, out_ref, own_out, own_vmem,
               send_sems, recv_sems, local_sem, own_sem):
        me = lax.axis_index("tok")
        keep = lax.axis_index("kv")
        own_copy = pltpu.make_async_copy(own_hbm.at[0], own_vmem, own_sem)
        own_copy.start()
        barrier = pltpu.get_barrier_semaphore()

        def greet(i, c):
            pl.semaphore_signal(barrier, inc=1, device_id=(lax.rem(me + i, n), keep), device_id_type=mesh_id)
            return c

        lax.fori_loop(1, n, greet, 0)
        pl.semaphore_wait(barrier, n - 1)
        local = pltpu.make_async_copy(x_ref, out_ref.at[me], local_sem)
        local.start()

        def send(i, c):
            peer = lax.rem(me + i, n)
            pltpu.make_async_remote_copy(
                x_ref, out_ref.at[me], send_sems.at[i], recv_sems.at[i],
                device_id=(peer, keep), device_id_type=mesh_id,
            ).start()
            return c

        lax.fori_loop(1, n, send, 0)
        own_copy.wait()
        q = q_ref[...]
        row = lax.broadcasted_iota(jnp.int32, (q.shape[0], cap), 0)
        pos = lax.broadcasted_iota(jnp.int32, (q.shape[0], cap), 1)
        scores = jnp.zeros((q.shape[0], cap), jnp.float32)
        for r in range(reqs):
            part = lax.dot_general(q, own_vmem[r], (((1,), (1,)), ((), ())),
                                   preferred_element_type=jnp.float32)
            scores = jnp.where(row // per == r, part, scores)
        scores = scores * scale
        row_len = jnp.zeros((q.shape[0], cap), jnp.int32)
        for r in range(reqs):
            row_len = jnp.where(row // per == r, len_ref[r], row_len)
        live = pos < row_len
        scores = jnp.where(live, scores, NEG)
        top = jnp.max(scores, axis=1, keepdims=True)
        weights = jnp.where(live, jnp.exp(scores - top), 0.0)
        total = jnp.sum(weights, axis=1, keepdims=True)
        wb = weights.astype(jnp.bfloat16)
        acc = jnp.zeros((q.shape[0], lanes), jnp.float32)
        for r in range(reqs):
            acc = acc + jnp.dot(jnp.where(row // per == r, wb, jnp.zeros_like(wb)), own_vmem[r],
                                preferred_element_type=jnp.float32)
        numer = pltpu.roll(acc, half, 1)
        lane = lax.broadcasted_iota(jnp.int32, acc.shape, 1)
        alive = total > 0.0
        safe = jnp.where(alive, total, 1.0)
        level = jnp.where(alive, top + jnp.log(safe), NEG)
        own_out[...] = jnp.where(lane < half, jnp.where(alive, numer / safe, 0.0), level)

        def finish(i, c):
            peer = lax.rem(me + i, n)
            origin = lax.rem(me + n - i, n)
            pltpu.make_async_remote_copy(
                x_ref, out_ref.at[me], send_sems.at[i], recv_sems.at[i],
                device_id=(peer, keep), device_id_type=mesh_id,
            ).wait_send()
            pltpu.make_async_remote_copy(
                x_ref, out_ref.at[origin], send_sems.at[i], recv_sems.at[i],
                device_id=(origin, keep), device_id_type=mesh_id,
            ).wait_recv()
            return c

        lax.fori_loop(1, n, finish, 0)
        local.wait()

    return pl.pallas_call(
        kernel,
        out_shape=(
            jax.ShapeDtypeStruct((n,) + tuple(q_slab.shape), q_slab.dtype),
            jax.ShapeDtypeStruct((q16.shape[0], lanes), jnp.float32),
        ),
        in_specs=[pl.BlockSpec(memory_space=pltpu.VMEM)] * 2
        + [pl.BlockSpec(memory_space=pltpu.SMEM), pl.BlockSpec(memory_space=pl.ANY)],
        out_specs=(pl.BlockSpec(memory_space=pltpu.VMEM), pl.BlockSpec(memory_space=pltpu.VMEM)),
        scratch_shapes=[
            pltpu.VMEM((reqs, cap, lanes), own_cache.dtype),
            pltpu.SemaphoreType.DMA((n,)),
            pltpu.SemaphoreType.DMA((n,)),
            pltpu.SemaphoreType.DMA(()),
            pltpu.SemaphoreType.DMA(()),
        ],
        compiler_params=pltpu.CompilerParams(collective_id=0, has_side_effects=True),
    )(q_slab, q16, lens16, own_cache)


def finish_kernel_call(q_slab, q16_rows, own_len, own_cache, prefix, base, req_group, jrow, pre_len, new, w_out, n_tok, n_kv):
    slab_rows = 16
    rows = slab_rows // 4
    groups, pre_dev, kv_lanes = prefix.shape
    window = 16 * 8
    heads = 4
    width = 64
    d_model = w_out.shape[1]
    cols = d_model // n_kv
    mesh_id = pl.DeviceIdType.MESH

    reqs, cap, lanes = own_cache.shape[1:]
    per = q16_rows // reqs

    def kernel(x_ref, olen_ref, own_hbm, pre_ref, idx_ref, len_ref, new_ref, w_ref,
               out_ref, recv_scr, acc_scr, part_scr, kv_recv, res_scr, packed_ref,
               qrecv, qrows_scr, own_vmem, own_ref, new_scr,
               tsend, trecv, ksend, krecv, loc_sems, qsend, qrsem, extra_sems):
        me = lax.axis_index("tok")
        mk = lax.axis_index("kv")
        barrier = pltpu.get_barrier_semaphore()

        def greet_tok(i, c):
            pl.semaphore_signal(barrier, inc=1, device_id=(lax.rem(me + i, n_tok), mk), device_id_type=mesh_id)
            return c

        def greet_kv(i, c):
            pl.semaphore_signal(barrier, inc=1, device_id=(me, lax.rem(mk + i, n_kv)), device_id_type=mesh_id)
            return c

        own_copy = pltpu.make_async_copy(own_hbm.at[0], own_vmem, extra_sems.at[0])
        own_copy.start()
        lax.fori_loop(1, n_tok, greet_tok, 0)
        lax.fori_loop(1, n_kv, greet_kv, 0)
        pl.semaphore_wait(barrier, n_tok - 1 + n_kv - 1)
        qlocal = pltpu.make_async_copy(x_ref, qrecv.at[me], extra_sems.at[1])
        qlocal.start()

        def q_copy(i, target, slot):
            return pltpu.make_async_remote_copy(
                x_ref, qrecv.at[slot], qsend.at[i], qrsem.at[i],
                device_id=(target, mk), device_id_type=mesh_id,
            )

        def send_q(i, c):
            q_copy(i, lax.rem(me + i, n_tok), me).start()
            return c

        lax.fori_loop(1, n_tok, send_q, 0)
        own_copy.wait()
        xs = x_ref[...]
        xlane = lax.broadcasted_iota(jnp.int32, (1, 128), 1)
        pieces = []
        for r in range(reqs):
            for h in range(per):
                line = xs[r * 2 + h // 2 : r * 2 + h // 2 + 1, :]
                if h % 2:
                    line = pltpu.roll(line, width, 1)
                pieces.append(jnp.where(xlane < width, line, 0.0))
        qf = jnp.concatenate(pieces, axis=0)
        q = qf.astype(jnp.bfloat16)
        nkv = new_ref[...].astype(jnp.float32)
        knew = jnp.concatenate([nkv[r : r + 1] for r in range(reqs) for _ in range(per)], axis=0)
        nlane = lax.broadcasted_iota(jnp.int32, knew.shape, 1)
        s_new = jnp.sum(jnp.where(nlane < width, qf * knew, 0.0), axis=1, keepdims=True) * SCALE
        new_scr[...] = jnp.where(nlane < width, pltpu.roll(knew, width, 1), s_new)
        orow = lax.broadcasted_iota(jnp.int32, (q.shape[0], cap), 0)
        opos = lax.broadcasted_iota(jnp.int32, (q.shape[0], cap), 1)
        scores = jnp.zeros((q.shape[0], cap), jnp.float32)
        for r in range(reqs):
            part = lax.dot_general(q, own_vmem[r], (((1,), (1,)), ((), ())),
                                   preferred_element_type=jnp.float32)
            scores = jnp.where(orow // per == r, part, scores)
        scores = scores * SCALE
        row_len = jnp.zeros((q.shape[0], cap), jnp.int32)
        for r in range(reqs):
            row_len = jnp.where(orow // per == r, olen_ref[r], row_len)
        olive = opos < row_len
        scores = jnp.where(olive, scores, NEG)
        otop = jnp.max(scores, axis=1, keepdims=True)
        oweights = jnp.where(olive, jnp.exp(scores - otop), 0.0)
        ototal = jnp.sum(oweights, axis=1, keepdims=True)
        owb = oweights.astype(jnp.bfloat16)
        oacc = jnp.zeros((q.shape[0], lanes), jnp.float32)
        for r in range(reqs):
            oacc = oacc + jnp.dot(jnp.where(orow // per == r, owb, jnp.zeros_like(owb)), own_vmem[r],
                                  preferred_element_type=jnp.float32)
        onumer = pltpu.roll(oacc, width, 1)
        olane2 = lax.broadcasted_iota(jnp.int32, oacc.shape, 1)
        oalive = ototal > 0.0
        osafe = jnp.where(oalive, ototal, 1.0)
        olevel = jnp.where(oalive, otop + jnp.log(osafe), NEG)
        own_ref[...] = jnp.where(olane2 < width, jnp.where(oalive, onumer / osafe, 0.0), olevel)

        def finish_q(i, c):
            q_copy(i, lax.rem(me + i, n_tok), me).wait_send()
            q_copy(i, lax.rem(me + n_tok - i, n_tok), lax.rem(me + n_tok - i, n_tok)).wait_recv()
            return c

        lax.fori_loop(1, n_tok, finish_q, 0)
        qlocal.wait()
        qrows_scr[...] = jnp.zeros(qrows_scr.shape, jnp.float32)
        got = qrecv[...]
        qlane = lax.broadcasted_iota(jnp.int32, (n_tok, 128), 1)
        for r in range(reqs):
            for h in range(per):
                line = got[:, r * 2 + h // 2, :]
                if h % 2:
                    line = pltpu.roll(line, width, 1)
                qrows_scr[:, r, h, :] = jnp.where(qlane < width, line, 0.0)
        q_ref = qrows_scr.reshape(n_tok * reqs, 8, 128)

        glane = lax.broadcasted_iota(jnp.int32, (window, pre_dev), 1) + me * pre_dev
        olane = lax.broadcasted_iota(jnp.int32, (window, kv_lanes), 1)
        for g in range(groups):
            first = idx_ref[g]
            qb = jnp.concatenate([q_ref[first + k] for k in range(window // 8)], axis=0)
            qb = qb.astype(jnp.bfloat16)
            kv = pre_ref[g]
            s = lax.dot_general(qb, kv, (((1,), (1,)), ((), ())), preferred_element_type=jnp.float32)
            s = s * SCALE
            live = glane < len_ref[g]
            s = jnp.where(live, s, NEG)
            top = jnp.max(s, axis=1, keepdims=True)
            e = jnp.where(live, jnp.exp(s - top), 0.0)
            total = jnp.sum(e, axis=1, keepdims=True)
            nm = jnp.dot(e.astype(jnp.bfloat16), kv, preferred_element_type=jnp.float32)
            nm = pltpu.roll(nm, width, 1)
            alive = total > 0.0
            safe = jnp.where(alive, total, 1.0)
            level = jnp.where(alive, top + jnp.log(safe), NEG)
            res_scr[pl.ds(g * (window // 8), window // 8)] = jnp.where(
                olane < width, jnp.where(alive, nm / safe, 0.0), level).reshape(window // 8, 8, kv_lanes)

        prow = lax.broadcasted_iota(jnp.int32, (8, kv_lanes), 0)

        def place(m, c):
            blocks = []
            for t in range(2):
                r = 2 * m + t
                blocks.append(res_scr[idx_ref[groups + n_tok * rows + r] * (window // 8) + idx_ref[groups + r]])
            both = jnp.where(prow < 4, blocks[0], pltpu.roll(blocks[1], 4, 0))
            packed_ref[m // 2, pl.ds(pl.multiple_of((m % 2) * 8, 8), 8), :] = both
            return c

        lax.fori_loop(0, n_tok * 2, place, 0)

        local_copy = pltpu.make_async_copy(packed_ref.at[me], recv_scr.at[me], loc_sems.at[0])
        local_copy.start()

        def tok_copy(i, target, slot):
            return pltpu.make_async_remote_copy(
                packed_ref.at[target], recv_scr.at[slot], tsend.at[i], trecv.at[i],
                device_id=(target, mk), device_id_type=mesh_id,
            )

        def send_tok(i, c):
            tok_copy(i, lax.rem(me + i, n_tok), me).start()
            return c

        lax.fori_loop(1, n_tok, send_tok, 0)

        def finish_tok(i, c):
            tok_copy(i, lax.rem(me + i, n_tok), me).wait_send()
            origin = lax.rem(me + n_tok - i, n_tok)
            pltpu.make_async_remote_copy(
                packed_ref.at[origin], recv_scr.at[origin], tsend.at[i], trecv.at[i],
                device_id=(origin, mk), device_id_type=mesh_id,
            ).wait_recv()
            return c

        lax.fori_loop(1, n_tok, finish_tok, 0)
        local_copy.wait()

        x = recv_scr[...]
        loc = own_ref[...]
        nloc = new_scr[...]
        llane = lax.broadcasted_iota(jnp.int32, loc.shape, 1)
        big = jnp.maximum(jnp.maximum(jnp.max(x, axis=0), loc), nloc)
        keep_hi = llane >= width
        weight = jnp.where(keep_hi[None], jnp.exp(x - big[None]), 0.0)
        lweight = jnp.where(keep_hi, jnp.exp(loc - big), 0.0)
        nweight = jnp.where(keep_hi, jnp.exp(nloc - big), 0.0)
        weight = pltpu.roll(weight.reshape(-1, 128), width, 1).reshape(x.shape)
        lweight = pltpu.roll(lweight, width, 1)
        nweight = pltpu.roll(nweight, width, 1)
        denom = jnp.sum(weight, axis=0) + lweight + nweight
        numer = jnp.sum(weight * x, axis=0) + lweight * loc + nweight * nloc
        attn = jnp.where(llane < width, numer / jnp.where(llane < width, denom, 1.0), 0.0).astype(jnp.bfloat16)
        pi = lax.broadcasted_iota(jnp.int32, (slab_rows, slab_rows), 0)
        pj = lax.broadcasted_iota(jnp.int32, (slab_rows, slab_rows), 1)
        perm = jnp.where(pj == (pi % rows) * heads + pi // rows, 1.0, 0.0).astype(jnp.bfloat16)
        attn = jnp.dot(perm, attn, preferred_element_type=jnp.float32)
        shifted = pltpu.roll(attn, width, 1)
        row = lax.broadcasted_iota(jnp.int32, attn.shape, 0)
        head_of = row // rows
        acc = jnp.zeros((slab_rows, d_model), jnp.float32)
        for pair in range(heads // 2):
            lhs = jnp.where(head_of == 2 * pair, attn, jnp.where(head_of == 2 * pair + 1, shifted, 0.0))
            acc = acc + jnp.dot(
                lhs.astype(jnp.bfloat16), w_ref[pl.ds(pair * 2 * width, 2 * width), :],
                preferred_element_type=jnp.float32,
            )
        acc_scr[...] = acc
        partial = acc_scr[pl.ds(0, rows), :]
        for h in range(1, heads):
            partial = partial + acc_scr[pl.ds(h * rows, rows), :]
        part_scr[...] = partial

        def kv_src(target):
            return part_scr.at[:, pl.ds(pl.multiple_of(target * cols, cols), cols)]

        kv_local = pltpu.make_async_copy(kv_src(mk), kv_recv.at[mk], loc_sems.at[1])
        kv_local.start()

        def kv_copy(j, target, slot):
            return pltpu.make_async_remote_copy(
                kv_src(target), kv_recv.at[slot], ksend.at[j], krecv.at[j],
                device_id=(me, target), device_id_type=mesh_id,
            )

        def send_kv(j, c):
            kv_copy(j, lax.rem(mk + j, n_kv), mk).start()
            return c

        lax.fori_loop(1, n_kv, send_kv, 0)

        def finish_kv(j, c):
            kv_copy(j, lax.rem(mk + j, n_kv), mk).wait_send()
            origin = lax.rem(mk + n_kv - j, n_kv)
            pltpu.make_async_remote_copy(
                kv_src(origin), kv_recv.at[origin], ksend.at[j], krecv.at[j],
                device_id=(me, origin), device_id_type=mesh_id,
            ).wait_recv()
            return c

        lax.fori_loop(1, n_kv, finish_kv, 0)
        kv_local.wait()
        out_ref[...] = jnp.sum(kv_recv[...], axis=0).astype(out_ref.dtype)

    return pl.pallas_call(
        kernel,
        out_shape=jax.ShapeDtypeStruct((rows, cols), jnp.bfloat16),
        in_specs=[pl.BlockSpec(memory_space=pltpu.VMEM)]
        + [pl.BlockSpec(memory_space=pltpu.SMEM), pl.BlockSpec(memory_space=pl.ANY),
           pl.BlockSpec(memory_space=pltpu.VMEM)]
        + [pl.BlockSpec(memory_space=pltpu.SMEM)] * 2
        + [pl.BlockSpec(memory_space=pltpu.VMEM)] * 2,
        out_specs=pl.BlockSpec(memory_space=pltpu.VMEM),
        scratch_shapes=[
            pltpu.VMEM((n_tok, slab_rows, 128), jnp.float32),
            pltpu.VMEM((slab_rows, d_model), jnp.float32),
            pltpu.VMEM((rows, d_model), jnp.float32),
            pltpu.VMEM((n_kv, rows, cols), jnp.float32),
            pltpu.VMEM((groups * (window // 8), 8, 128), jnp.float32),
            pltpu.VMEM((n_tok, slab_rows, 128), jnp.float32),
            pltpu.VMEM((n_tok,) + tuple(q_slab.shape), jnp.float32),
            pltpu.VMEM((n_tok, reqs, 8, 128), jnp.float32),
            pltpu.VMEM((reqs, cap, lanes), own_cache.dtype),
            pltpu.VMEM((slab_rows, 128), jnp.float32),
            pltpu.VMEM((slab_rows, 128), jnp.float32),
            pltpu.SemaphoreType.DMA((n_tok,)),
            pltpu.SemaphoreType.DMA((n_tok,)),
            pltpu.SemaphoreType.DMA((n_kv,)),
            pltpu.SemaphoreType.DMA((n_kv,)),
            pltpu.SemaphoreType.DMA((2,)),
            pltpu.SemaphoreType.DMA((n_tok,)),
            pltpu.SemaphoreType.DMA((n_tok,)),
            pltpu.SemaphoreType.DMA((2,)),
        ],
        compiler_params=pltpu.CompilerParams(collective_id=1, has_side_effects=True),
    )(q_slab, own_len, own_cache, prefix, jnp.concatenate([base, jrow, req_group]), pre_len, new, w_out)


def block_stats(query, keyval, live):
    width = query.shape[-1]
    keys = keyval[..., :width]
    values = keyval[..., width:]
    scores = jnp.einsum("rhge,hrpe->rhgp", query, keys, preferred_element_type=jnp.float32) * SCALE
    mask = live[:, None, None, :]
    scores = jnp.where(mask, scores, NEG)
    top = jnp.max(scores, axis=-1)
    weights = jnp.where(mask, jnp.exp(scores - top[..., None]), 0.0)
    total = jnp.sum(weights, axis=-1)
    numer = jnp.einsum(
        "rhgp,hrpe->rhge", weights.astype(jnp.bfloat16), values, preferred_element_type=jnp.float32
    )
    return (top, total, numer)


def prompt_stats(all_query, prefix_cache, req_group, pre_len, block):
    all_rows, heads, per_kv, width = all_query.shape
    groups = prefix_cache.shape[1]
    pre_dev = prefix_cache.shape[2]
    group_ids = jnp.arange(groups, dtype=jnp.int32)
    starts = jnp.sum((req_group[None, :] < group_ids[:, None]).astype(jnp.int32), axis=1)
    slot_ids = jnp.arange(SHARE, dtype=jnp.int32)
    source = jnp.minimum(starts[:, None] + slot_ids[None, :], all_rows - 1).reshape(-1)
    slotted = jnp.take(all_query, source, axis=0).reshape(groups, SHARE, heads, per_kv, width)
    keys = prefix_cache[..., :width]
    values = prefix_cache[..., width:]
    scores = (
        jnp.einsum("gshqe,hgpe->hgsqp", slotted, keys, preferred_element_type=jnp.float32) * SCALE
    )
    pre_pos = block * pre_dev + jnp.arange(pre_dev, dtype=jnp.int32)
    live = pre_pos[None, :] < pre_len[:, None]
    mask = live[None, :, None, None, :]
    scores = jnp.where(mask, scores, NEG)
    top = jnp.max(scores, axis=-1)
    weights = jnp.where(mask, jnp.exp(scores - top[..., None]), 0.0)
    total = jnp.sum(weights, axis=-1)
    numer = jnp.einsum(
        "hgsqp,hgpe->hgsqe",
        weights.astype(jnp.bfloat16),
        values,
        preferred_element_type=jnp.float32,
    )
    match = req_group[:, None] == group_ids[None, :]
    start_req = jnp.sum(jnp.where(match, starts[None, :], 0), axis=1)
    place = req_group * SHARE + jnp.arange(all_rows, dtype=jnp.int32) - start_req
    alive = total > 0.0
    safe = jnp.where(alive, total, 1.0)
    level = jnp.where(alive, top + jnp.log(safe), NEG)
    packed = jnp.concatenate(
        [jnp.where(alive[..., None], numer / safe[..., None], 0.0),
         jnp.broadcast_to(level[..., None], top.shape + (128 - width,))],
        axis=-1,
    ).reshape(heads, groups * SHARE, per_kv, 128)
    packed = jnp.take(packed, place, axis=1)
    return jnp.transpose(packed, (1, 0, 2, 3)).reshape(all_rows * heads * per_kv, 128)


def body(hidden_in, w_query, w_keyval, w_out, own_cache, prefix_cache, own_len, req_group, pre_len):
    rows = hidden_in.shape[0]
    heads = w_keyval.shape[1]
    width = w_keyval.shape[2] // 2
    per_kv = w_query.shape[1] // (heads * width)
    columns = heads * per_kv
    inputs = hidden_in.astype(jnp.float32)
    normed = (inputs * lax.rsqrt(jnp.mean(inputs * inputs, axis=1, keepdims=True) + 1e-05)).astype(
        jnp.bfloat16
    )
    query = jnp.dot(normed, w_query, preferred_element_type=jnp.float32).astype(jnp.bfloat16)
    newkv = jnp.einsum("rd,dhe->rhe", normed, w_keyval, preferred_element_type=jnp.float32).astype(
        jnp.bfloat16
    )
    n_tok = lax.axis_size("tok")
    n_kv = lax.axis_size("kv")
    q_slab = query.astype(jnp.float32).reshape(-1, 128)
    q16 = jnp.concatenate(
        [query.reshape(rows * columns, width), jnp.zeros((rows * columns, width), query.dtype)], axis=1
    )
    all_rows = n_tok * rows
    groups = prefix_cache.shape[1]
    group_ids = jnp.arange(groups, dtype=jnp.int32)
    starts = jnp.sum((req_group[None, :] < group_ids[:, None]).astype(jnp.int32), axis=1)
    base = jnp.minimum(starts, all_rows - SHARE)
    rg = jnp.clip(req_group, 0, groups - 1)
    own_start = jnp.sum((req_group[None, :] < req_group[:, None]).astype(jnp.int32), axis=1)
    own_base = jnp.minimum(own_start, all_rows - SHARE)
    jrow = jnp.clip(jnp.arange(all_rows, dtype=jnp.int32) - own_base, 0, SHARE - 1)
    local_query = query.reshape(rows, heads, per_kv, width)
    s_new = (
        jnp.einsum(
            "rhge,rhe->rhg", local_query, newkv[..., :width], preferred_element_type=jnp.float32
        )
        * SCALE
    )
    s_new = s_new.reshape(rows, columns)
    new_value = jnp.broadcast_to(
        newkv[:, :, None, width:].astype(jnp.float32), (rows, heads, per_kv, width)
    ).reshape(rows, columns, width)
    new_block = jnp.concatenate(
        [new_value, jnp.broadcast_to(s_new[..., None], (rows, columns, 128 - width))],
        axis=-1,
    ).reshape(rows * columns, 128)
    return finish_kernel_call(q_slab, rows * columns, own_len, own_cache, prefix_cache[0], base, rg, jrow, pre_len, newkv.reshape(rows, -1), w_out, n_tok, n_kv)


def solution(mesh):
    in_specs = (
        P("tok", None),
        P(None, "kv"),
        P(None, "kv", None),
        P("kv", None),
        P("kv", "tok", None, None),
        P("kv", None, "tok", None),
        P("tok"),
        P(),
        P(),
    )
    out_specs = P("tok", "kv")
    return jax.shard_map(body, mesh=mesh, in_specs=in_specs, out_specs=out_specs, check_vma=False)
```

```python
import jax
import jax.numpy as jnp
from jax import lax
from jax.sharding import PartitionSpec as P
from jax.experimental import pallas as pl
from jax.experimental.pallas import tpu as pltpu

SHARE = 16


SCALE = 0.015625
NEG = -1e30


def exchange(slabs, axis, other, n, broadcast, cid):
    slab_shape = slabs.shape[1:] if not broadcast else slabs.shape
    mesh_id = pl.DeviceIdType.MESH

    def kernel(x_ref, out_ref, send_sems, recv_sems, local_sem):
        me = lax.axis_index(axis)
        keep = lax.axis_index(other)

        def dev(peer):
            return (peer, keep) if axis == "tok" else (keep, peer)

        def src(peer):
            return x_ref if broadcast else x_ref.at[peer]

        barrier = pltpu.get_barrier_semaphore()

        def greet(i, c):
            peer = lax.rem(me + i, n)
            pl.semaphore_signal(barrier, inc=1, device_id=dev(peer), device_id_type=mesh_id)
            return c

        lax.fori_loop(1, n, greet, 0)
        pl.semaphore_wait(barrier, n - 1)
        local = pltpu.make_async_copy(src(me), out_ref.at[me], local_sem)
        local.start()

        def send(i, c):
            peer = lax.rem(me + i, n)
            pltpu.make_async_remote_copy(
                src(peer), out_ref.at[me], send_sems.at[i], recv_sems.at[i],
                device_id=dev(peer), device_id_type=mesh_id,
            ).start()
            return c

        lax.fori_loop(1, n, send, 0)

        def finish(i, c):
            peer = lax.rem(me + i, n)
            origin = lax.rem(me + n - i, n)
            pltpu.make_async_remote_copy(
                src(peer), out_ref.at[me], send_sems.at[i], recv_sems.at[i],
                device_id=dev(peer), device_id_type=mesh_id,
            ).wait_send()
            pltpu.make_async_remote_copy(
                src(peer), out_ref.at[origin], send_sems.at[i], recv_sems.at[i],
                device_id=dev(origin), device_id_type=mesh_id,
            ).wait_recv()
            return c

        lax.fori_loop(1, n, finish, 0)
        local.wait()

    return pl.pallas_call(
        kernel,
        out_shape=jax.ShapeDtypeStruct((n,) + tuple(slab_shape), slabs.dtype),
        in_specs=[pl.BlockSpec(memory_space=pltpu.VMEM)],
        out_specs=pl.BlockSpec(memory_space=pltpu.VMEM),
        scratch_shapes=[
            pltpu.SemaphoreType.DMA((n,)),
            pltpu.SemaphoreType.DMA((n,)),
            pltpu.SemaphoreType.DMA(()),
        ],
        compiler_params=pltpu.CompilerParams(collective_id=cid, has_side_effects=True),
    )(slabs)


def broadcast_with_own(q_slab, q16, lens16, own_cache, n, scale):
    mesh_id = pl.DeviceIdType.MESH
    reqs, cap, lanes = own_cache.shape[1:]
    half = lanes // 2
    per = q16.shape[0] // reqs

    def kernel(x_ref, q_ref, len_ref, own_hbm, out_ref, own_out, own_vmem,
               send_sems, recv_sems, local_sem, own_sem):
        me = lax.axis_index("tok")
        keep = lax.axis_index("kv")
        own_copy = pltpu.make_async_copy(own_hbm.at[0], own_vmem, own_sem)
        own_copy.start()
        barrier = pltpu.get_barrier_semaphore()

        def greet(i, c):
            pl.semaphore_signal(barrier, inc=1, device_id=(lax.rem(me + i, n), keep), device_id_type=mesh_id)
            return c

        lax.fori_loop(1, n, greet, 0)
        pl.semaphore_wait(barrier, n - 1)
        local = pltpu.make_async_copy(x_ref, out_ref.at[me], local_sem)
        local.start()

        def send(i, c):
            peer = lax.rem(me + i, n)
            pltpu.make_async_remote_copy(
                x_ref, out_ref.at[me], send_sems.at[i], recv_sems.at[i],
                device_id=(peer, keep), device_id_type=mesh_id,
            ).start()
            return c

        lax.fori_loop(1, n, send, 0)
        own_copy.wait()
        q = q_ref[...]
        row = lax.broadcasted_iota(jnp.int32, (q.shape[0], cap), 0)
        pos = lax.broadcasted_iota(jnp.int32, (q.shape[0], cap), 1)
        scores = jnp.zeros((q.shape[0], cap), jnp.float32)
        for r in range(reqs):
            part = lax.dot_general(q, own_vmem[r], (((1,), (1,)), ((), ())),
                                   preferred_element_type=jnp.float32)
            scores = jnp.where(row // per == r, part, scores)
        scores = scores * scale
        row_len = jnp.zeros((q.shape[0], cap), jnp.int32)
        for r in range(reqs):
            row_len = jnp.where(row // per == r, len_ref[r], row_len)
        live = pos < row_len
        scores = jnp.where(live, scores, NEG)
        top = jnp.max(scores, axis=1, keepdims=True)
        weights = jnp.where(live, jnp.exp(scores - top), 0.0)
        total = jnp.sum(weights, axis=1, keepdims=True)
        wb = weights.astype(jnp.bfloat16)
        acc = jnp.zeros((q.shape[0], lanes), jnp.float32)
        for r in range(reqs):
            acc = acc + jnp.dot(jnp.where(row // per == r, wb, jnp.zeros_like(wb)), own_vmem[r],
                                preferred_element_type=jnp.float32)
        numer = pltpu.roll(acc, half, 1)
        lane = lax.broadcasted_iota(jnp.int32, acc.shape, 1)
        alive = total > 0.0
        safe = jnp.where(alive, total, 1.0)
        level = jnp.where(alive, top + jnp.log(safe), NEG)
        own_out[...] = jnp.where(lane < half, jnp.where(alive, numer / safe, 0.0), level)

        def finish(i, c):
            peer = lax.rem(me + i, n)
            origin = lax.rem(me + n - i, n)
            pltpu.make_async_remote_copy(
                x_ref, out_ref.at[me], send_sems.at[i], recv_sems.at[i],
                device_id=(peer, keep), device_id_type=mesh_id,
            ).wait_send()
            pltpu.make_async_remote_copy(
                x_ref, out_ref.at[origin], send_sems.at[i], recv_sems.at[i],
                device_id=(origin, keep), device_id_type=mesh_id,
            ).wait_recv()
            return c

        lax.fori_loop(1, n, finish, 0)
        local.wait()

    return pl.pallas_call(
        kernel,
        out_shape=(
            jax.ShapeDtypeStruct((n,) + tuple(q_slab.shape), q_slab.dtype),
            jax.ShapeDtypeStruct((q16.shape[0], lanes), jnp.float32),
        ),
        in_specs=[pl.BlockSpec(memory_space=pltpu.VMEM)] * 2
        + [pl.BlockSpec(memory_space=pltpu.SMEM), pl.BlockSpec(memory_space=pl.ANY)],
        out_specs=(pl.BlockSpec(memory_space=pltpu.VMEM), pl.BlockSpec(memory_space=pltpu.VMEM)),
        scratch_shapes=[
            pltpu.VMEM((reqs, cap, lanes), own_cache.dtype),
            pltpu.SemaphoreType.DMA((n,)),
            pltpu.SemaphoreType.DMA((n,)),
            pltpu.SemaphoreType.DMA(()),
            pltpu.SemaphoreType.DMA(()),
        ],
        compiler_params=pltpu.CompilerParams(collective_id=0, has_side_effects=True),
    )(q_slab, q16, lens16, own_cache)


def finish_kernel_call(q_slab, q16_rows, own_len, own_cache, prefix, base, req_group, jrow, pre_len, new, w_kv, w_out, n_tok, n_kv):
    slab_rows = 16
    rows = slab_rows // 4
    groups, pre_dev, kv_lanes = prefix.shape
    window = 16 * 8
    heads = 4
    width = 64
    d_model = w_out.shape[1]
    cols = d_model // n_kv
    mesh_id = pl.DeviceIdType.MESH

    reqs, cap, lanes = own_cache.shape[1:]
    per = q16_rows // reqs

    def kernel(x_ref, olen_ref, own_hbm, pre_ref, idx_ref, rg_ref, len_ref, new_ref, wkv_ref, w_ref,
               out_ref, recv_scr, acc_scr, part_scr, kv_recv, res_scr, packed_ref,
               qrecv, qrows_scr, own_vmem, own_ref, new_scr,
               tsend, trecv, ksend, krecv, loc_sems, qsend, qrsem, extra_sems):
        me = lax.axis_index("tok")
        mk = lax.axis_index("kv")
        barrier = pltpu.get_barrier_semaphore()

        def greet_tok(i, c):
            pl.semaphore_signal(barrier, inc=1, device_id=(lax.rem(me + i, n_tok), mk), device_id_type=mesh_id)
            return c

        def greet_kv(i, c):
            pl.semaphore_signal(barrier, inc=1, device_id=(me, lax.rem(mk + i, n_kv)), device_id_type=mesh_id)
            return c

        own_copy = pltpu.make_async_copy(own_hbm.at[0], own_vmem, extra_sems.at[0])
        own_copy.start()
        lax.fori_loop(1, n_tok, greet_tok, 0)
        lax.fori_loop(1, n_kv, greet_kv, 0)
        pl.semaphore_wait(barrier, n_tok - 1 + n_kv - 1)
        qlocal = pltpu.make_async_copy(x_ref, qrecv.at[me], extra_sems.at[1])
        qlocal.start()

        def q_copy(i, target, slot):
            return pltpu.make_async_remote_copy(
                x_ref, qrecv.at[slot], qsend.at[i], qrsem.at[i],
                device_id=(target, mk), device_id_type=mesh_id,
            )

        def send_q(i, c):
            q_copy(i, lax.rem(me + i, n_tok), me).start()
            return c

        lax.fori_loop(1, n_tok, send_q, 0)
        own_copy.wait()
        xs = x_ref[...]
        xlane = lax.broadcasted_iota(jnp.int32, (1, 128), 1)
        pieces = []
        for r in range(reqs):
            for h in range(per):
                line = xs[r * 2 + h // 2 : r * 2 + h // 2 + 1, :]
                if h % 2:
                    line = pltpu.roll(line, width, 1)
                pieces.append(jnp.where(xlane < width, line, 0.0))
        qf = jnp.concatenate(pieces, axis=0)
        q = qf.astype(jnp.bfloat16)
        nkv = jnp.dot(new_ref[...], wkv_ref[...], preferred_element_type=jnp.float32)
        nkv = nkv.astype(jnp.bfloat16).astype(jnp.float32)
        knew = jnp.concatenate([nkv[r : r + 1] for r in range(reqs) for _ in range(per)], axis=0)
        nlane = lax.broadcasted_iota(jnp.int32, knew.shape, 1)
        s_new = jnp.sum(jnp.where(nlane < width, qf * knew, 0.0), axis=1, keepdims=True) * SCALE
        new_scr[...] = jnp.where(nlane < width, pltpu.roll(knew, width, 1), s_new)
        orow = lax.broadcasted_iota(jnp.int32, (q.shape[0], cap), 0)
        opos = lax.broadcasted_iota(jnp.int32, (q.shape[0], cap), 1)
        scores = jnp.zeros((q.shape[0], cap), jnp.float32)
        for r in range(reqs):
            part = lax.dot_general(q, own_vmem[r], (((1,), (1,)), ((), ())),
                                   preferred_element_type=jnp.float32)
            scores = jnp.where(orow // per == r, part, scores)
        scores = scores * SCALE
        row_len = jnp.zeros((q.shape[0], cap), jnp.int32)
        for r in range(reqs):
            row_len = jnp.where(orow // per == r, olen_ref[r], row_len)
        olive = opos < row_len
        scores = jnp.where(olive, scores, NEG)
        otop = jnp.max(scores, axis=1, keepdims=True)
        oweights = jnp.where(olive, jnp.exp(scores - otop), 0.0)
        ototal = jnp.sum(oweights, axis=1, keepdims=True)
        owb = oweights.astype(jnp.bfloat16)
        oacc = jnp.zeros((q.shape[0], lanes), jnp.float32)
        for r in range(reqs):
            oacc = oacc + jnp.dot(jnp.where(orow // per == r, owb, jnp.zeros_like(owb)), own_vmem[r],
                                  preferred_element_type=jnp.float32)
        onumer = pltpu.roll(oacc, width, 1)
        olane2 = lax.broadcasted_iota(jnp.int32, oacc.shape, 1)
        oalive = ototal > 0.0
        osafe = jnp.where(oalive, ototal, 1.0)
        olevel = jnp.where(oalive, otop + jnp.log(osafe), NEG)
        own_ref[...] = jnp.where(olane2 < width, jnp.where(oalive, onumer / osafe, 0.0), olevel)

        def finish_q(i, c):
            q_copy(i, lax.rem(me + i, n_tok), me).wait_send()
            q_copy(i, lax.rem(me + n_tok - i, n_tok), lax.rem(me + n_tok - i, n_tok)).wait_recv()
            return c

        lax.fori_loop(1, n_tok, finish_q, 0)
        qlocal.wait()
        qrows_scr[...] = jnp.zeros(qrows_scr.shape, jnp.float32)
        got = qrecv[...]
        qlane = lax.broadcasted_iota(jnp.int32, (n_tok, 128), 1)
        for r in range(reqs):
            for h in range(per):
                line = got[:, r * 2 + h // 2, :]
                if h % 2:
                    line = pltpu.roll(line, width, 1)
                qrows_scr[:, r, h, :] = jnp.where(qlane < width, line, 0.0)
        q_ref = qrows_scr.reshape(n_tok * reqs, 8, 128)

        glane = lax.broadcasted_iota(jnp.int32, (window, pre_dev), 1) + me * pre_dev
        olane = lax.broadcasted_iota(jnp.int32, (window, kv_lanes), 1)
        for g in range(groups):
            first = idx_ref[g]
            qb = jnp.concatenate([q_ref[first + k] for k in range(window // 8)], axis=0)
            qb = qb.astype(jnp.bfloat16)
            kv = pre_ref[g]
            s = lax.dot_general(qb, kv, (((1,), (1,)), ((), ())), preferred_element_type=jnp.float32)
            s = s * SCALE
            live = glane < len_ref[g]
            s = jnp.where(live, s, NEG)
            top = jnp.max(s, axis=1, keepdims=True)
            e = jnp.where(live, jnp.exp(s - top), 0.0)
            total = jnp.sum(e, axis=1, keepdims=True)
            nm = jnp.dot(e.astype(jnp.bfloat16), kv, preferred_element_type=jnp.float32)
            nm = pltpu.roll(nm, width, 1)
            alive = total > 0.0
            safe = jnp.where(alive, total, 1.0)
            level = jnp.where(alive, top + jnp.log(safe), NEG)
            res_scr[pl.ds(g * (window // 8), window // 8)] = jnp.where(
                olane < width, jnp.where(alive, nm / safe, 0.0), level).reshape(window // 8, 8, kv_lanes)

        prow = lax.broadcasted_iota(jnp.int32, (8, kv_lanes), 0)

        def place(m, c):
            blocks = []
            for t in range(2):
                r = 2 * m + t
                blocks.append(res_scr[rg_ref[r] * (window // 8) + idx_ref[groups + r]])
            both = jnp.where(prow < 4, blocks[0], pltpu.roll(blocks[1], 4, 0))
            packed_ref[m // 2, pl.ds(pl.multiple_of((m % 2) * 8, 8), 8), :] = both
            return c

        lax.fori_loop(0, n_tok * 2, place, 0)

        local_copy = pltpu.make_async_copy(packed_ref.at[me], recv_scr.at[me], loc_sems.at[0])
        local_copy.start()

        def tok_copy(i, target, slot):
            return pltpu.make_async_remote_copy(
                packed_ref.at[target], recv_scr.at[slot], tsend.at[i], trecv.at[i],
                device_id=(target, mk), device_id_type=mesh_id,
            )

        def send_tok(i, c):
            tok_copy(i, lax.rem(me + i, n_tok), me).start()
            return c

        lax.fori_loop(1, n_tok, send_tok, 0)

        def finish_tok(i, c):
            tok_copy(i, lax.rem(me + i, n_tok), me).wait_send()
            origin = lax.rem(me + n_tok - i, n_tok)
            pltpu.make_async_remote_copy(
                packed_ref.at[origin], recv_scr.at[origin], tsend.at[i], trecv.at[i],
                device_id=(origin, mk), device_id_type=mesh_id,
            ).wait_recv()
            return c

        lax.fori_loop(1, n_tok, finish_tok, 0)
        local_copy.wait()

        x = recv_scr[...]
        loc = own_ref[...]
        nloc = new_scr[...]
        llane = lax.broadcasted_iota(jnp.int32, loc.shape, 1)
        big = jnp.maximum(jnp.maximum(jnp.max(x, axis=0), loc), nloc)
        keep_hi = llane >= width
        weight = jnp.where(keep_hi[None], jnp.exp(x - big[None]), 0.0)
        lweight = jnp.where(keep_hi, jnp.exp(loc - big), 0.0)
        nweight = jnp.where(keep_hi, jnp.exp(nloc - big), 0.0)
        weight = pltpu.roll(weight.reshape(-1, 128), width, 1).reshape(x.shape)
        lweight = pltpu.roll(lweight, width, 1)
        nweight = pltpu.roll(nweight, width, 1)
        denom = jnp.sum(weight, axis=0) + lweight + nweight
        numer = jnp.sum(weight * x, axis=0) + lweight * loc + nweight * nloc
        attn = jnp.where(llane < width, numer / jnp.where(llane < width, denom, 1.0), 0.0).astype(jnp.bfloat16)
        pi = lax.broadcasted_iota(jnp.int32, (slab_rows, slab_rows), 0)
        pj = lax.broadcasted_iota(jnp.int32, (slab_rows, slab_rows), 1)
        perm = jnp.where(pj == (pi % rows) * heads + pi // rows, 1.0, 0.0).astype(jnp.bfloat16)
        attn = jnp.dot(perm, attn, preferred_element_type=jnp.float32)
        shifted = pltpu.roll(attn, width, 1)
        row = lax.broadcasted_iota(jnp.int32, attn.shape, 0)
        head_of = row // rows
        acc = jnp.zeros((slab_rows, d_model), jnp.float32)
        for pair in range(heads // 2):
            lhs = jnp.where(head_of == 2 * pair, attn, jnp.where(head_of == 2 * pair + 1, shifted, 0.0))
            acc = acc + jnp.dot(
                lhs.astype(jnp.bfloat16), w_ref[pl.ds(pair * 2 * width, 2 * width), :],
                preferred_element_type=jnp.float32,
            )
        acc_scr[...] = acc
        partial = acc_scr[pl.ds(0, rows), :]
        for h in range(1, heads):
            partial = partial + acc_scr[pl.ds(h * rows, rows), :]
        part_scr[...] = partial

        def kv_src(target):
            return part_scr.at[:, pl.ds(pl.multiple_of(target * cols, cols), cols)]

        kv_local = pltpu.make_async_copy(kv_src(mk), kv_recv.at[mk], loc_sems.at[1])
        kv_local.start()

        def kv_copy(j, target, slot):
            return pltpu.make_async_remote_copy(
                kv_src(target), kv_recv.at[slot], ksend.at[j], krecv.at[j],
                device_id=(me, target), device_id_type=mesh_id,
            )

        def send_kv(j, c):
            kv_copy(j, lax.rem(mk + j, n_kv), mk).start()
            return c

        lax.fori_loop(1, n_kv, send_kv, 0)

        def finish_kv(j, c):
            kv_copy(j, lax.rem(mk + j, n_kv), mk).wait_send()
            origin = lax.rem(mk + n_kv - j, n_kv)
            pltpu.make_async_remote_copy(
                kv_src(origin), kv_recv.at[origin], ksend.at[j], krecv.at[j],
                device_id=(me, origin), device_id_type=mesh_id,
            ).wait_recv()
            return c

        lax.fori_loop(1, n_kv, finish_kv, 0)
        kv_local.wait()
        out_ref[...] = jnp.sum(kv_recv[...], axis=0).astype(out_ref.dtype)

    return pl.pallas_call(
        kernel,
        out_shape=jax.ShapeDtypeStruct((rows, cols), jnp.bfloat16),
        in_specs=[pl.BlockSpec(memory_space=pltpu.VMEM)]
        + [pl.BlockSpec(memory_space=pltpu.SMEM), pl.BlockSpec(memory_space=pl.ANY),
           pl.BlockSpec(memory_space=pltpu.VMEM)]
        + [pl.BlockSpec(memory_space=pltpu.SMEM)] * 3
        + [pl.BlockSpec(memory_space=pltpu.VMEM)] * 3,
        out_specs=pl.BlockSpec(memory_space=pltpu.VMEM),
        scratch_shapes=[
            pltpu.VMEM((n_tok, slab_rows, 128), jnp.float32),
            pltpu.VMEM((slab_rows, d_model), jnp.float32),
            pltpu.VMEM((rows, d_model), jnp.float32),
            pltpu.VMEM((n_kv, rows, cols), jnp.float32),
            pltpu.VMEM((groups * (window // 8), 8, 128), jnp.float32),
            pltpu.VMEM((n_tok, slab_rows, 128), jnp.float32),
            pltpu.VMEM((n_tok,) + tuple(q_slab.shape), jnp.float32),
            pltpu.VMEM((n_tok, reqs, 8, 128), jnp.float32),
            pltpu.VMEM((reqs, cap, lanes), own_cache.dtype),
            pltpu.VMEM((slab_rows, 128), jnp.float32),
            pltpu.VMEM((slab_rows, 128), jnp.float32),
            pltpu.SemaphoreType.DMA((n_tok,)),
            pltpu.SemaphoreType.DMA((n_tok,)),
            pltpu.SemaphoreType.DMA((n_kv,)),
            pltpu.SemaphoreType.DMA((n_kv,)),
            pltpu.SemaphoreType.DMA((2,)),
            pltpu.SemaphoreType.DMA((n_tok,)),
            pltpu.SemaphoreType.DMA((n_tok,)),
            pltpu.SemaphoreType.DMA((2,)),
        ],
        compiler_params=pltpu.CompilerParams(collective_id=1, has_side_effects=True),
    )(q_slab, own_len, own_cache, prefix, jnp.concatenate([base, jrow]), req_group, pre_len, new, w_kv, w_out)


def block_stats(query, keyval, live):
    width = query.shape[-1]
    keys = keyval[..., :width]
    values = keyval[..., width:]
    scores = jnp.einsum("rhge,hrpe->rhgp", query, keys, preferred_element_type=jnp.float32) * SCALE
    mask = live[:, None, None, :]
    scores = jnp.where(mask, scores, NEG)
    top = jnp.max(scores, axis=-1)
    weights = jnp.where(mask, jnp.exp(scores - top[..., None]), 0.0)
    total = jnp.sum(weights, axis=-1)
    numer = jnp.einsum(
        "rhgp,hrpe->rhge", weights.astype(jnp.bfloat16), values, preferred_element_type=jnp.float32
    )
    return (top, total, numer)


def prompt_stats(all_query, prefix_cache, req_group, pre_len, block):
    all_rows, heads, per_kv, width = all_query.shape
    groups = prefix_cache.shape[1]
    pre_dev = prefix_cache.shape[2]
    group_ids = jnp.arange(groups, dtype=jnp.int32)
    starts = jnp.sum((req_group[None, :] < group_ids[:, None]).astype(jnp.int32), axis=1)
    slot_ids = jnp.arange(SHARE, dtype=jnp.int32)
    source = jnp.minimum(starts[:, None] + slot_ids[None, :], all_rows - 1).reshape(-1)
    slotted = jnp.take(all_query, source, axis=0).reshape(groups, SHARE, heads, per_kv, width)
    keys = prefix_cache[..., :width]
    values = prefix_cache[..., width:]
    scores = (
        jnp.einsum("gshqe,hgpe->hgsqp", slotted, keys, preferred_element_type=jnp.float32) * SCALE
    )
    pre_pos = block * pre_dev + jnp.arange(pre_dev, dtype=jnp.int32)
    live = pre_pos[None, :] < pre_len[:, None]
    mask = live[None, :, None, None, :]
    scores = jnp.where(mask, scores, NEG)
    top = jnp.max(scores, axis=-1)
    weights = jnp.where(mask, jnp.exp(scores - top[..., None]), 0.0)
    total = jnp.sum(weights, axis=-1)
    numer = jnp.einsum(
        "hgsqp,hgpe->hgsqe",
        weights.astype(jnp.bfloat16),
        values,
        preferred_element_type=jnp.float32,
    )
    match = req_group[:, None] == group_ids[None, :]
    start_req = jnp.sum(jnp.where(match, starts[None, :], 0), axis=1)
    place = req_group * SHARE + jnp.arange(all_rows, dtype=jnp.int32) - start_req
    alive = total > 0.0
    safe = jnp.where(alive, total, 1.0)
    level = jnp.where(alive, top + jnp.log(safe), NEG)
    packed = jnp.concatenate(
        [jnp.where(alive[..., None], numer / safe[..., None], 0.0),
         jnp.broadcast_to(level[..., None], top.shape + (128 - width,))],
        axis=-1,
    ).reshape(heads, groups * SHARE, per_kv, 128)
    packed = jnp.take(packed, place, axis=1)
    return jnp.transpose(packed, (1, 0, 2, 3)).reshape(all_rows * heads * per_kv, 128)


def body(hidden_in, w_query, w_keyval, w_out, own_cache, prefix_cache, own_len, req_group, pre_len):
    rows = hidden_in.shape[0]
    heads = w_keyval.shape[1]
    width = w_keyval.shape[2] // 2
    per_kv = w_query.shape[1] // (heads * width)
    columns = heads * per_kv
    inputs = hidden_in.astype(jnp.float32)
    normed = (inputs * lax.rsqrt(jnp.mean(inputs * inputs, axis=1, keepdims=True) + 1e-05)).astype(
        jnp.bfloat16
    )
    query = jnp.dot(normed, w_query, preferred_element_type=jnp.float32).astype(jnp.bfloat16)
    newkv = jnp.einsum("rd,dhe->rhe", normed, w_keyval, preferred_element_type=jnp.float32).astype(
        jnp.bfloat16
    )
    n_tok = lax.axis_size("tok")
    n_kv = lax.axis_size("kv")
    q_slab = query.astype(jnp.float32).reshape(-1, 128)
    q16 = jnp.concatenate(
        [query.reshape(rows * columns, width), jnp.zeros((rows * columns, width), query.dtype)], axis=1
    )
    all_rows = n_tok * rows
    groups = prefix_cache.shape[1]
    group_ids = jnp.arange(groups, dtype=jnp.int32)
    starts = jnp.sum((req_group[None, :] < group_ids[:, None]).astype(jnp.int32), axis=1)
    base = jnp.minimum(starts, all_rows - SHARE)
    rg = jnp.clip(req_group, 0, groups - 1)
    own_start = jnp.sum((req_group[None, :] < req_group[:, None]).astype(jnp.int32), axis=1)
    own_base = jnp.minimum(own_start, all_rows - SHARE)
    jrow = jnp.clip(jnp.arange(all_rows, dtype=jnp.int32) - own_base, 0, SHARE - 1)
    local_query = query.reshape(rows, heads, per_kv, width)
    s_new = (
        jnp.einsum(
            "rhge,rhe->rhg", local_query, newkv[..., :width], preferred_element_type=jnp.float32
        )
        * SCALE
    )
    s_new = s_new.reshape(rows, columns)
    new_value = jnp.broadcast_to(
        newkv[:, :, None, width:].astype(jnp.float32), (rows, heads, per_kv, width)
    ).reshape(rows, columns, width)
    new_block = jnp.concatenate(
        [new_value, jnp.broadcast_to(s_new[..., None], (rows, columns, 128 - width))],
        axis=-1,
    ).reshape(rows * columns, 128)
    return finish_kernel_call(q_slab, rows * columns, own_len, own_cache, prefix_cache[0], base, rg, jrow, pre_len, normed, w_keyval.reshape(w_keyval.shape[0], -1), w_out, n_tok, n_kv)


def solution(mesh):
    in_specs = (
        P("tok", None),
        P(None, "kv"),
        P(None, "kv", None),
        P("kv", None),
        P("kv", "tok", None, None),
        P("kv", None, "tok", None),
        P("tok"),
        P(),
        P(),
    )
    out_specs = P("tok", "kv")
    return jax.shard_map(body, mesh=mesh, in_specs=in_specs, out_specs=out_specs, check_vma=False)
```

```python
import jax
import jax.numpy as jnp
from jax import lax
from jax.sharding import PartitionSpec as P
from jax.experimental import pallas as pl
from jax.experimental.pallas import tpu as pltpu

SHARE = 16


SCALE = 0.015625
NEG = -1e30


def exchange(slabs, axis, other, n, broadcast, cid):
    slab_shape = slabs.shape[1:] if not broadcast else slabs.shape
    mesh_id = pl.DeviceIdType.MESH

    def kernel(x_ref, out_ref, send_sems, recv_sems, local_sem):
        me = lax.axis_index(axis)
        keep = lax.axis_index(other)

        def dev(peer):
            return (peer, keep) if axis == "tok" else (keep, peer)

        def src(peer):
            return x_ref if broadcast else x_ref.at[peer]

        barrier = pltpu.get_barrier_semaphore()

        def greet(i, c):
            peer = lax.rem(me + i, n)
            pl.semaphore_signal(barrier, inc=1, device_id=dev(peer), device_id_type=mesh_id)
            return c

        lax.fori_loop(1, n, greet, 0)
        pl.semaphore_wait(barrier, n - 1)
        local = pltpu.make_async_copy(src(me), out_ref.at[me], local_sem)
        local.start()

        def send(i, c):
            peer = lax.rem(me + i, n)
            pltpu.make_async_remote_copy(
                src(peer), out_ref.at[me], send_sems.at[i], recv_sems.at[i],
                device_id=dev(peer), device_id_type=mesh_id,
            ).start()
            return c

        lax.fori_loop(1, n, send, 0)

        def finish(i, c):
            peer = lax.rem(me + i, n)
            origin = lax.rem(me + n - i, n)
            pltpu.make_async_remote_copy(
                src(peer), out_ref.at[me], send_sems.at[i], recv_sems.at[i],
                device_id=dev(peer), device_id_type=mesh_id,
            ).wait_send()
            pltpu.make_async_remote_copy(
                src(peer), out_ref.at[origin], send_sems.at[i], recv_sems.at[i],
                device_id=dev(origin), device_id_type=mesh_id,
            ).wait_recv()
            return c

        lax.fori_loop(1, n, finish, 0)
        local.wait()

    return pl.pallas_call(
        kernel,
        out_shape=jax.ShapeDtypeStruct((n,) + tuple(slab_shape), slabs.dtype),
        in_specs=[pl.BlockSpec(memory_space=pltpu.VMEM)],
        out_specs=pl.BlockSpec(memory_space=pltpu.VMEM),
        scratch_shapes=[
            pltpu.SemaphoreType.DMA((n,)),
            pltpu.SemaphoreType.DMA((n,)),
            pltpu.SemaphoreType.DMA(()),
        ],
        compiler_params=pltpu.CompilerParams(collective_id=cid, has_side_effects=True),
    )(slabs)


def broadcast_with_own(q_slab, q16, lens16, own_cache, n, scale):
    mesh_id = pl.DeviceIdType.MESH
    reqs, cap, lanes = own_cache.shape[1:]
    half = lanes // 2
    per = q16.shape[0] // reqs

    def kernel(x_ref, q_ref, len_ref, own_hbm, out_ref, own_out, own_vmem,
               send_sems, recv_sems, local_sem, own_sem):
        me = lax.axis_index("tok")
        keep = lax.axis_index("kv")
        own_copy = pltpu.make_async_copy(own_hbm.at[0], own_vmem, own_sem)
        own_copy.start()
        barrier = pltpu.get_barrier_semaphore()

        def greet(i, c):
            pl.semaphore_signal(barrier, inc=1, device_id=(lax.rem(me + i, n), keep), device_id_type=mesh_id)
            return c

        lax.fori_loop(1, n, greet, 0)
        pl.semaphore_wait(barrier, n - 1)
        local = pltpu.make_async_copy(x_ref, out_ref.at[me], local_sem)
        local.start()

        def send(i, c):
            peer = lax.rem(me + i, n)
            pltpu.make_async_remote_copy(
                x_ref, out_ref.at[me], send_sems.at[i], recv_sems.at[i],
                device_id=(peer, keep), device_id_type=mesh_id,
            ).start()
            return c

        lax.fori_loop(1, n, send, 0)
        own_copy.wait()
        q = q_ref[...]
        row = lax.broadcasted_iota(jnp.int32, (q.shape[0], cap), 0)
        pos = lax.broadcasted_iota(jnp.int32, (q.shape[0], cap), 1)
        scores = jnp.zeros((q.shape[0], cap), jnp.float32)
        for r in range(reqs):
            part = lax.dot_general(q, own_vmem[r], (((1,), (1,)), ((), ())),
                                   preferred_element_type=jnp.float32)
            scores = jnp.where(row // per == r, part, scores)
        scores = scores * scale
        row_len = jnp.zeros((q.shape[0], cap), jnp.int32)
        for r in range(reqs):
            row_len = jnp.where(row // per == r, len_ref[r], row_len)
        live = pos < row_len
        scores = jnp.where(live, scores, NEG)
        top = jnp.max(scores, axis=1, keepdims=True)
        weights = jnp.where(live, jnp.exp(scores - top), 0.0)
        total = jnp.sum(weights, axis=1, keepdims=True)
        wb = weights.astype(jnp.bfloat16)
        acc = jnp.zeros((q.shape[0], lanes), jnp.float32)
        for r in range(reqs):
            acc = acc + jnp.dot(jnp.where(row // per == r, wb, jnp.zeros_like(wb)), own_vmem[r],
                                preferred_element_type=jnp.float32)
        numer = pltpu.roll(acc, half, 1)
        lane = lax.broadcasted_iota(jnp.int32, acc.shape, 1)
        alive = total > 0.0
        safe = jnp.where(alive, total, 1.0)
        level = jnp.where(alive, top + jnp.log(safe), NEG)
        own_out[...] = jnp.where(lane < half, jnp.where(alive, numer / safe, 0.0), level)

        def finish(i, c):
            peer = lax.rem(me + i, n)
            origin = lax.rem(me + n - i, n)
            pltpu.make_async_remote_copy(
                x_ref, out_ref.at[me], send_sems.at[i], recv_sems.at[i],
                device_id=(peer, keep), device_id_type=mesh_id,
            ).wait_send()
            pltpu.make_async_remote_copy(
                x_ref, out_ref.at[origin], send_sems.at[i], recv_sems.at[i],
                device_id=(origin, keep), device_id_type=mesh_id,
            ).wait_recv()
            return c

        lax.fori_loop(1, n, finish, 0)
        local.wait()

    return pl.pallas_call(
        kernel,
        out_shape=(
            jax.ShapeDtypeStruct((n,) + tuple(q_slab.shape), q_slab.dtype),
            jax.ShapeDtypeStruct((q16.shape[0], lanes), jnp.float32),
        ),
        in_specs=[pl.BlockSpec(memory_space=pltpu.VMEM)] * 2
        + [pl.BlockSpec(memory_space=pltpu.SMEM), pl.BlockSpec(memory_space=pl.ANY)],
        out_specs=(pl.BlockSpec(memory_space=pltpu.VMEM), pl.BlockSpec(memory_space=pltpu.VMEM)),
        scratch_shapes=[
            pltpu.VMEM((reqs, cap, lanes), own_cache.dtype),
            pltpu.SemaphoreType.DMA((n,)),
            pltpu.SemaphoreType.DMA((n,)),
            pltpu.SemaphoreType.DMA(()),
            pltpu.SemaphoreType.DMA(()),
        ],
        compiler_params=pltpu.CompilerParams(collective_id=0, has_side_effects=True),
    )(q_slab, q16, lens16, own_cache)


def finish_kernel_call(q_slab, q16_rows, own_len, own_cache, prefix, base, req_group, jrow, pre_len, new, w_out, n_tok, n_kv):
    slab_rows = 16
    rows = slab_rows // 4
    groups, pre_dev, kv_lanes = prefix.shape
    window = 16 * 8
    heads = 4
    width = 64
    d_model = w_out.shape[1]
    cols = d_model // n_kv
    mesh_id = pl.DeviceIdType.MESH

    reqs, cap, lanes = own_cache.shape[1:]
    per = q16_rows // reqs

    def kernel(x_ref, olen_ref, own_hbm, pre_ref, idx_ref, rg_ref, len_ref, new_ref, w_ref,
               out_ref, recv_scr, acc_scr, part_scr, kv_recv, res_scr, packed_ref,
               qrecv, qrows_scr, own_vmem, own_ref, new_scr,
               tsend, trecv, ksend, krecv, loc_sems, qsend, qrsem, extra_sems):
        me = lax.axis_index("tok")
        mk = lax.axis_index("kv")
        barrier = pltpu.get_barrier_semaphore()

        def greet_tok(i, c):
            pl.semaphore_signal(barrier, inc=1, device_id=(lax.rem(me + i, n_tok), mk), device_id_type=mesh_id)
            return c

        def greet_kv(i, c):
            pl.semaphore_signal(barrier, inc=1, device_id=(me, lax.rem(mk + i, n_kv)), device_id_type=mesh_id)
            return c

        own_copy = pltpu.make_async_copy(own_hbm.at[0], own_vmem, extra_sems.at[0])
        own_copy.start()
        lax.fori_loop(1, n_tok, greet_tok, 0)
        lax.fori_loop(1, n_kv, greet_kv, 0)
        pl.semaphore_wait(barrier, n_tok - 1 + n_kv - 1)
        qlocal = pltpu.make_async_copy(x_ref, qrecv.at[me], extra_sems.at[1])
        qlocal.start()

        def q_copy(i, target, slot):
            return pltpu.make_async_remote_copy(
                x_ref, qrecv.at[slot], qsend.at[i], qrsem.at[i],
                device_id=(target, mk), device_id_type=mesh_id,
            )

        def send_q(i, c):
            q_copy(i, lax.rem(me + i, n_tok), me).start()
            return c

        lax.fori_loop(1, n_tok, send_q, 0)
        own_copy.wait()
        xs = x_ref[...]
        xlane = lax.broadcasted_iota(jnp.int32, (1, 128), 1)
        pieces = []
        for r in range(reqs):
            for h in range(per):
                line = xs[r * 2 + h // 2 : r * 2 + h // 2 + 1, :]
                if h % 2:
                    line = pltpu.roll(line, width, 1)
                pieces.append(jnp.where(xlane < width, line, 0.0))
        qf = jnp.concatenate(pieces, axis=0)
        q = qf.astype(jnp.bfloat16)
        nkv = new_ref[...].astype(jnp.float32)
        knew = jnp.concatenate([nkv[r : r + 1] for r in range(reqs) for _ in range(per)], axis=0)
        nlane = lax.broadcasted_iota(jnp.int32, knew.shape, 1)
        s_new = jnp.sum(jnp.where(nlane < width, qf * knew, 0.0), axis=1, keepdims=True) * SCALE
        new_scr[...] = jnp.where(nlane < width, pltpu.roll(knew, width, 1), s_new)
        orow = lax.broadcasted_iota(jnp.int32, (q.shape[0], cap), 0)
        opos = lax.broadcasted_iota(jnp.int32, (q.shape[0], cap), 1)
        scores = jnp.zeros((q.shape[0], cap), jnp.float32)
        for r in range(reqs):
            part = lax.dot_general(q, own_vmem[r], (((1,), (1,)), ((), ())),
                                   preferred_element_type=jnp.float32)
            scores = jnp.where(orow // per == r, part, scores)
        scores = scores * SCALE
        row_len = jnp.zeros((q.shape[0], cap), jnp.int32)
        for r in range(reqs):
            row_len = jnp.where(orow // per == r, olen_ref[r], row_len)
        olive = opos < row_len
        scores = jnp.where(olive, scores, NEG)
        otop = jnp.max(scores, axis=1, keepdims=True)
        oweights = jnp.where(olive, jnp.exp(scores - otop), 0.0)
        ototal = jnp.sum(oweights, axis=1, keepdims=True)
        owb = oweights.astype(jnp.bfloat16)
        oacc = jnp.zeros((q.shape[0], lanes), jnp.float32)
        for r in range(reqs):
            oacc = oacc + jnp.dot(jnp.where(orow // per == r, owb, jnp.zeros_like(owb)), own_vmem[r],
                                  preferred_element_type=jnp.float32)
        onumer = pltpu.roll(oacc, width, 1)
        olane2 = lax.broadcasted_iota(jnp.int32, oacc.shape, 1)
        oalive = ototal > 0.0
        osafe = jnp.where(oalive, ototal, 1.0)
        olevel = jnp.where(oalive, otop + jnp.log(osafe), NEG)
        own_ref[...] = jnp.where(olane2 < width, jnp.where(oalive, onumer / osafe, 0.0), olevel)

        def finish_q(i, c):
            q_copy(i, lax.rem(me + i, n_tok), me).wait_send()
            q_copy(i, lax.rem(me + n_tok - i, n_tok), lax.rem(me + n_tok - i, n_tok)).wait_recv()
            return c

        lax.fori_loop(1, n_tok, finish_q, 0)
        qlocal.wait()
        qrows_scr[...] = jnp.zeros(qrows_scr.shape, jnp.float32)
        got = qrecv[...]
        qlane = lax.broadcasted_iota(jnp.int32, (n_tok, 128), 1)
        for r in range(reqs):
            for h in range(per):
                line = got[:, r * 2 + h // 2, :]
                if h % 2:
                    line = pltpu.roll(line, width, 1)
                qrows_scr[:, r, h, :] = jnp.where(qlane < width, line, 0.0)
        q_ref = qrows_scr.reshape(n_tok * reqs, 8, 128)

        glane = lax.broadcasted_iota(jnp.int32, (window, pre_dev), 1) + me * pre_dev
        olane = lax.broadcasted_iota(jnp.int32, (window, kv_lanes), 1)
        for g in range(groups):
            first = idx_ref[g]
            qb = jnp.concatenate([q_ref[first + k] for k in range(window // 8)], axis=0)
            qb = qb.astype(jnp.bfloat16)
            kv = pre_ref[g]
            s = lax.dot_general(qb, kv, (((1,), (1,)), ((), ())), preferred_element_type=jnp.float32)
            s = s * SCALE
            live = glane < len_ref[g]
            s = jnp.where(live, s, NEG)
            top = jnp.max(s, axis=1, keepdims=True)
            e = jnp.where(live, jnp.exp(s - top), 0.0)
            total = jnp.sum(e, axis=1, keepdims=True)
            nm = jnp.dot(e.astype(jnp.bfloat16), kv, preferred_element_type=jnp.float32)
            nm = pltpu.roll(nm, width, 1)
            alive = total > 0.0
            safe = jnp.where(alive, total, 1.0)
            level = jnp.where(alive, top + jnp.log(safe), NEG)
            res_scr[pl.ds(g * (window // 8), window // 8)] = jnp.where(
                olane < width, jnp.where(alive, nm / safe, 0.0), level).reshape(window // 8, 8, kv_lanes)

        prow = lax.broadcasted_iota(jnp.int32, (8, kv_lanes), 0)

        def place(m, c):
            blocks = []
            for t in range(2):
                r = 2 * m + t
                blocks.append(res_scr[rg_ref[r] * (window // 8) + idx_ref[groups + r]])
            both = jnp.where(prow < 4, blocks[0], pltpu.roll(blocks[1], 4, 0))
            packed_ref[m // 2, pl.ds(pl.multiple_of((m % 2) * 8, 8), 8), :] = both
            return c

        lax.fori_loop(0, n_tok * 2, place, 0)

        local_copy = pltpu.make_async_copy(packed_ref.at[me], recv_scr.at[me], loc_sems.at[0])
        local_copy.start()

        def tok_copy(i, target, slot):
            return pltpu.make_async_remote_copy(
                packed_ref.at[target], recv_scr.at[slot], tsend.at[i], trecv.at[i],
                device_id=(target, mk), device_id_type=mesh_id,
            )

        def send_tok(i, c):
            tok_copy(i, lax.rem(me + i, n_tok), me).start()
            return c

        lax.fori_loop(1, n_tok, send_tok, 0)

        def finish_tok(i, c):
            tok_copy(i, lax.rem(me + i, n_tok), me).wait_send()
            origin = lax.rem(me + n_tok - i, n_tok)
            pltpu.make_async_remote_copy(
                packed_ref.at[origin], recv_scr.at[origin], tsend.at[i], trecv.at[i],
                device_id=(origin, mk), device_id_type=mesh_id,
            ).wait_recv()
            return c

        lax.fori_loop(1, n_tok, finish_tok, 0)
        local_copy.wait()

        x = recv_scr[...]
        loc = own_ref[...]
        nloc = new_scr[...]
        llane = lax.broadcasted_iota(jnp.int32, loc.shape, 1)
        big = jnp.maximum(jnp.maximum(jnp.max(x, axis=0), loc), nloc)
        keep_hi = llane >= width
        weight = jnp.where(keep_hi[None], jnp.exp(x - big[None]), 0.0)
        lweight = jnp.where(keep_hi, jnp.exp(loc - big), 0.0)
        nweight = jnp.where(keep_hi, jnp.exp(nloc - big), 0.0)
        weight = pltpu.roll(weight.reshape(-1, 128), width, 1).reshape(x.shape)
        lweight = pltpu.roll(lweight, width, 1)
        nweight = pltpu.roll(nweight, width, 1)
        denom = jnp.sum(weight, axis=0) + lweight + nweight
        numer = jnp.sum(weight * x, axis=0) + lweight * loc + nweight * nloc
        attn = jnp.where(llane < width, numer / jnp.where(llane < width, denom, 1.0), 0.0).astype(jnp.bfloat16)
        pi = lax.broadcasted_iota(jnp.int32, (slab_rows, slab_rows), 0)
        pj = lax.broadcasted_iota(jnp.int32, (slab_rows, slab_rows), 1)
        perm = jnp.where(pj == (pi % rows) * heads + pi // rows, 1.0, 0.0).astype(jnp.bfloat16)
        attn = jnp.dot(perm, attn, preferred_element_type=jnp.float32)
        shifted = pltpu.roll(attn, width, 1)
        row = lax.broadcasted_iota(jnp.int32, attn.shape, 0)
        head_of = row // rows
        acc = jnp.zeros((slab_rows, d_model), jnp.float32)
        for pair in range(heads // 2):
            lhs = jnp.where(head_of == 2 * pair, attn, jnp.where(head_of == 2 * pair + 1, shifted, 0.0))
            acc = acc + jnp.dot(
                lhs.astype(jnp.bfloat16), w_ref[pl.ds(pair * 2 * width, 2 * width), :],
                preferred_element_type=jnp.float32,
            )
        acc_scr[...] = acc
        partial = acc_scr[pl.ds(0, rows), :]
        for h in range(1, heads):
            partial = partial + acc_scr[pl.ds(h * rows, rows), :]
        part_scr[...] = partial

        def kv_src(target):
            return part_scr.at[:, pl.ds(pl.multiple_of(target * cols, cols), cols)]

        kv_local = pltpu.make_async_copy(kv_src(mk), kv_recv.at[mk], loc_sems.at[1])
        kv_local.start()

        def kv_copy(j, target, slot):
            return pltpu.make_async_remote_copy(
                kv_src(target), kv_recv.at[slot], ksend.at[j], krecv.at[j],
                device_id=(me, target), device_id_type=mesh_id,
            )

        def send_kv(j, c):
            kv_copy(j, lax.rem(mk + j, n_kv), mk).start()
            return c

        lax.fori_loop(1, n_kv, send_kv, 0)

        def finish_kv(j, c):
            kv_copy(j, lax.rem(mk + j, n_kv), mk).wait_send()
            origin = lax.rem(mk + n_kv - j, n_kv)
            pltpu.make_async_remote_copy(
                kv_src(origin), kv_recv.at[origin], ksend.at[j], krecv.at[j],
                device_id=(me, origin), device_id_type=mesh_id,
            ).wait_recv()
            return c

        lax.fori_loop(1, n_kv, finish_kv, 0)
        kv_local.wait()
        out_ref[...] = jnp.sum(kv_recv[...], axis=0).astype(out_ref.dtype)

    return pl.pallas_call(
        kernel,
        out_shape=jax.ShapeDtypeStruct((rows, cols), jnp.bfloat16),
        in_specs=[pl.BlockSpec(memory_space=pltpu.VMEM)]
        + [pl.BlockSpec(memory_space=pltpu.SMEM), pl.BlockSpec(memory_space=pl.ANY),
           pl.BlockSpec(memory_space=pltpu.VMEM)]
        + [pl.BlockSpec(memory_space=pltpu.SMEM)] * 3
        + [pl.BlockSpec(memory_space=pltpu.VMEM)] * 2,
        out_specs=pl.BlockSpec(memory_space=pltpu.VMEM),
        scratch_shapes=[
            pltpu.VMEM((n_tok, slab_rows, 128), jnp.float32),
            pltpu.VMEM((slab_rows, d_model), jnp.float32),
            pltpu.VMEM((rows, d_model), jnp.float32),
            pltpu.VMEM((n_kv, rows, cols), jnp.float32),
            pltpu.VMEM((groups * (window // 8), 8, 128), jnp.float32),
            pltpu.VMEM((n_tok, slab_rows, 128), jnp.float32),
            pltpu.VMEM((n_tok,) + tuple(q_slab.shape), jnp.float32),
            pltpu.VMEM((n_tok, reqs, 8, 128), jnp.float32),
            pltpu.VMEM((reqs, cap, lanes), own_cache.dtype),
            pltpu.VMEM((slab_rows, 128), jnp.float32),
            pltpu.VMEM((slab_rows, 128), jnp.float32),
            pltpu.SemaphoreType.DMA((n_tok,)),
            pltpu.SemaphoreType.DMA((n_tok,)),
            pltpu.SemaphoreType.DMA((n_kv,)),
            pltpu.SemaphoreType.DMA((n_kv,)),
            pltpu.SemaphoreType.DMA((2,)),
            pltpu.SemaphoreType.DMA((n_tok,)),
            pltpu.SemaphoreType.DMA((n_tok,)),
            pltpu.SemaphoreType.DMA((2,)),
        ],
        compiler_params=pltpu.CompilerParams(collective_id=1, has_side_effects=True),
    )(q_slab, own_len, own_cache, prefix, jnp.concatenate([base, jrow]), req_group, pre_len, new, w_out)


def block_stats(query, keyval, live):
    width = query.shape[-1]
    keys = keyval[..., :width]
    values = keyval[..., width:]
    scores = jnp.einsum("rhge,hrpe->rhgp", query, keys, preferred_element_type=jnp.float32) * SCALE
    mask = live[:, None, None, :]
    scores = jnp.where(mask, scores, NEG)
    top = jnp.max(scores, axis=-1)
    weights = jnp.where(mask, jnp.exp(scores - top[..., None]), 0.0)
    total = jnp.sum(weights, axis=-1)
    numer = jnp.einsum(
        "rhgp,hrpe->rhge", weights.astype(jnp.bfloat16), values, preferred_element_type=jnp.float32
    )
    return (top, total, numer)


def prompt_stats(all_query, prefix_cache, req_group, pre_len, block):
    all_rows, heads, per_kv, width = all_query.shape
    groups = prefix_cache.shape[1]
    pre_dev = prefix_cache.shape[2]
    group_ids = jnp.arange(groups, dtype=jnp.int32)
    starts = jnp.sum((req_group[None, :] < group_ids[:, None]).astype(jnp.int32), axis=1)
    slot_ids = jnp.arange(SHARE, dtype=jnp.int32)
    source = jnp.minimum(starts[:, None] + slot_ids[None, :], all_rows - 1).reshape(-1)
    slotted = jnp.take(all_query, source, axis=0).reshape(groups, SHARE, heads, per_kv, width)
    keys = prefix_cache[..., :width]
    values = prefix_cache[..., width:]
    scores = (
        jnp.einsum("gshqe,hgpe->hgsqp", slotted, keys, preferred_element_type=jnp.float32) * SCALE
    )
    pre_pos = block * pre_dev + jnp.arange(pre_dev, dtype=jnp.int32)
    live = pre_pos[None, :] < pre_len[:, None]
    mask = live[None, :, None, None, :]
    scores = jnp.where(mask, scores, NEG)
    top = jnp.max(scores, axis=-1)
    weights = jnp.where(mask, jnp.exp(scores - top[..., None]), 0.0)
    total = jnp.sum(weights, axis=-1)
    numer = jnp.einsum(
        "hgsqp,hgpe->hgsqe",
        weights.astype(jnp.bfloat16),
        values,
        preferred_element_type=jnp.float32,
    )
    match = req_group[:, None] == group_ids[None, :]
    start_req = jnp.sum(jnp.where(match, starts[None, :], 0), axis=1)
    place = req_group * SHARE + jnp.arange(all_rows, dtype=jnp.int32) - start_req
    alive = total > 0.0
    safe = jnp.where(alive, total, 1.0)
    level = jnp.where(alive, top + jnp.log(safe), NEG)
    packed = jnp.concatenate(
        [jnp.where(alive[..., None], numer / safe[..., None], 0.0),
         jnp.broadcast_to(level[..., None], top.shape + (128 - width,))],
        axis=-1,
    ).reshape(heads, groups * SHARE, per_kv, 128)
    packed = jnp.take(packed, place, axis=1)
    return jnp.transpose(packed, (1, 0, 2, 3)).reshape(all_rows * heads * per_kv, 128)


def body(hidden_in, w_query, w_keyval, w_out, own_cache, prefix_cache, own_len, req_group, pre_len):
    rows = hidden_in.shape[0]
    heads = w_keyval.shape[1]
    width = w_keyval.shape[2] // 2
    per_kv = w_query.shape[1] // (heads * width)
    columns = heads * per_kv
    inputs = hidden_in.astype(jnp.float32)
    normed = (inputs * lax.rsqrt(jnp.mean(inputs * inputs, axis=1, keepdims=True) + 1e-05)).astype(
        jnp.bfloat16
    )
    query = jnp.dot(normed, w_query, preferred_element_type=jnp.float32).astype(jnp.bfloat16)
    newkv = jnp.einsum("rd,dhe->rhe", normed, w_keyval, preferred_element_type=jnp.float32).astype(
        jnp.bfloat16
    )
    n_tok = lax.axis_size("tok")
    n_kv = lax.axis_size("kv")
    q_slab = query.astype(jnp.float32).reshape(-1, 128)
    q16 = jnp.concatenate(
        [query.reshape(rows * columns, width), jnp.zeros((rows * columns, width), query.dtype)], axis=1
    )
    all_rows = n_tok * rows
    groups = prefix_cache.shape[1]
    group_ids = jnp.arange(groups, dtype=jnp.int32)
    starts = jnp.sum((req_group[None, :] < group_ids[:, None]).astype(jnp.int32), axis=1)
    base = jnp.minimum(starts, all_rows - SHARE)
    rg = req_group
    own_start = jnp.sum((req_group[None, :] < req_group[:, None]).astype(jnp.int32), axis=1)
    own_base = jnp.minimum(own_start, all_rows - SHARE)
    jrow = jnp.clip(jnp.arange(all_rows, dtype=jnp.int32) - own_base, 0, SHARE - 1)
    local_query = query.reshape(rows, heads, per_kv, width)
    s_new = (
        jnp.einsum(
            "rhge,rhe->rhg", local_query, newkv[..., :width], preferred_element_type=jnp.float32
        )
        * SCALE
    )
    s_new = s_new.reshape(rows, columns)
    new_value = jnp.broadcast_to(
        newkv[:, :, None, width:].astype(jnp.float32), (rows, heads, per_kv, width)
    ).reshape(rows, columns, width)
    new_block = jnp.concatenate(
        [new_value, jnp.broadcast_to(s_new[..., None], (rows, columns, 128 - width))],
        axis=-1,
    ).reshape(rows * columns, 128)
    return finish_kernel_call(q_slab, rows * columns, own_len, own_cache, prefix_cache[0], base, rg, jrow, pre_len, newkv.reshape(rows, -1), w_out, n_tok, n_kv)


def solution(mesh):
    in_specs = (
        P("tok", None),
        P(None, "kv"),
        P(None, "kv", None),
        P("kv", None),
        P("kv", "tok", None, None),
        P("kv", None, "tok", None),
        P("tok"),
        P(),
        P(),
    )
    out_specs = P("tok", "kv")
    return jax.shard_map(body, mesh=mesh, in_specs=in_specs, out_specs=out_specs, check_vma=False)
```
